512 devices in a mesh: seq: 128 (over y, x_lo, z), ch: 4 (over x_hi, core).
Axes of the slice: x: 4 (x_hi: 2, x_lo: 2; x = x_hi * 2 + x_lo), y: 8, z: 8, core: 2. Of those that a mesh axis runs over, the one named last changes fastest.
Arguments:
- signal_x: bfloat16 [64, 65536], P('ch', 'seq'), may hold values from -6 to 6
- gate_q: bfloat16 [64, 65536], P('ch', 'seq'), may hold values from -6 to 6
- gate_k: bfloat16 [64, 65536], P('ch', 'seq'), may hold values from -6 to 6
- skip_gain: float32 [64], P('ch'), may hold values from 0.5 to 1.5
- residue: float32 [16], replicated, may hold values from -1.5 to 1.5
- memory: float32 [16], replicated, may hold values from 30 to 262144
- cotangent: bfloat16 [64, 65536], P('ch', 'seq'), may hold values from -6 to 6
Outputs:
- output: bfloat16 [64, 65536], P('ch', 'seq')
- grad_x: bfloat16 [64, 65536], P('ch', 'seq')
- grad_q: bfloat16 [64, 65536], P('ch', 'seq')
- grad_k: bfloat16 [64, 65536], P('ch', 'seq')
- grad_skip: float32 [64], P('ch')
- grad_residue: float32 [16], replicated
- grad_memory: float32 [16], replicated
The draws below stay inside these ranges and needn't reach their ends.
All inputs are finite; a program needn't handle non-finite values.
Results may differ from the reference program's by a relative error of at most 0.002.
Values sent between devices are 32-bit elements; how exact they have to be, the bound alone decides.
A program may use at most 64 MiB of HBM per device.

```python
import math
import jax
import jax.numpy as jnp
from jax import lax

ORDER = 16
SEQLEN = 65536
CHANNELS = 64


def steps_of(own_key, dims, split, smallest, largest):
    loudness, own = 1.0, jax.random.fold_in(own_key, 6)
    for dim, parts in split:
        steps = jnp.exp(jax.random.uniform(jax.random.fold_in(own, dim), (parts,), jnp.float32, smallest / len(split), largest / len(split)))
        loudness = loudness * jnp.repeat(steps, dims[dim] // parts).reshape([-1 if axis == dim else 1 for axis in range(len(dims))])
    return loudness


def centred(key, shape, spread, most, shards=(), kind=jnp.bfloat16):
    values = jax.random.normal(key, shape, jnp.float32) * spread
    if len(shards) > 0:
        values = steps_of(key, shape, shards, -0.22, 0.18) * values
    return jnp.clip(values, min=-most, max=most).astype(kind)


def setup_inputs(seed: int = 0) -> dict:
    arg_keys = jax.random.split(jax.random.key(seed), 8)
    return {
        "signal_x": centred(arg_keys[0], (CHANNELS, SEQLEN), 1.0, 6.0, ((0, 4), (1, 128))),
        "gate_q": centred(arg_keys[1], (CHANNELS, SEQLEN), 1.0, 6.0, ((0, 4), (1, 128))),
        "gate_k": centred(arg_keys[2], (CHANNELS, SEQLEN), 1.0, 6.0, ((0, 4), (1, 128))),
        "skip_gain": jnp.clip(0.5 + 1.0 * jax.random.uniform(arg_keys[3], (CHANNELS,), jnp.float32) ** steps_of(arg_keys[3], (CHANNELS,), ((0, 4),), -0.2, 0.2), 0.5, 1.5),
        "residue": centred(arg_keys[4], (ORDER,), 0.25, 1.5, (), jnp.float32),
        "memory": jnp.clip(jnp.exp(jax.random.uniform(arg_keys[5], (ORDER,), jnp.float32, math.log(30.0), math.log(262144.0))), 30.0, 262144.0),
        "cotangent": centred(arg_keys[6], (CHANNELS, SEQLEN), 1.0, 6.0, ((0, 4), (1, 128))),
    }


def reference(signal_x, gate_q, gate_k, skip_gain, residue, memory, cotangent):
    seq_len = signal_x.shape[1]
    positions = jnp.arange(seq_len).astype(jnp.float32)
    weights = jnp.sqrt(2.0 / memory)[:, None] * jnp.exp(-positions[None, :] / memory[:, None])
    filter_taps = lax.optimization_barrier(jnp.sum(residue[:, None] * weights, axis=0))
    spec_taps = jnp.fft.fft(filter_taps, n=2 * seq_len)
    x_float = signal_x.astype(jnp.float32)
    q_float = gate_q.astype(jnp.float32)
    k_float = gate_k.astype(jnp.float32)
    d_float = cotangent.astype(jnp.float32)
    values = x_float * k_float
    grad_mixed = d_float * q_float

    def per_channel(carried, inputs):
        channel_val, channel_grad = inputs
        spec_val = jnp.fft.fft(channel_val, n=2 * seq_len)
        spec_grad = jnp.fft.fft(channel_grad, n=2 * seq_len)
        conv_out = jnp.fft.ifft(spec_val * spec_taps)[:seq_len].real
        corr_out = jnp.fft.ifft(jnp.conj(spec_taps) * spec_grad)[:seq_len].real
        taps_term = jnp.fft.ifft(jnp.conj(spec_val) * spec_grad)[:seq_len].real
        return (carried + taps_term, (conv_out, corr_out))
    grad_taps, (conv_out, corr_out) = lax.scan(per_channel, jnp.zeros((seq_len,), jnp.float32), (values, grad_mixed))
    mixed_out = conv_out + skip_gain[:, None] * values
    output = (q_float * mixed_out).astype(jnp.bfloat16)
    grad_values = skip_gain[:, None] * grad_mixed + corr_out
    grad_x = (grad_values * k_float).astype(jnp.bfloat16)
    grad_q = (d_float * mixed_out).astype(jnp.bfloat16)
    grad_k = (grad_values * x_float).astype(jnp.bfloat16)
    norm_scale = 1.0 / math.sqrt(CHANNELS * SEQLEN)
    grad_skip = lax.optimization_barrier(jnp.sum(grad_mixed * values, axis=1)) / math.sqrt(SEQLEN)
    weighted = weights * grad_taps[None, :]
    grad_residue = lax.optimization_barrier(jnp.sum(weighted, axis=1)) * norm_scale
    grad_memory = residue * lax.optimization_barrier(jnp.sum(weighted * (positions[None, :] / memory[:, None] - 0.5), axis=1)) * norm_scale
    return (output, grad_x, grad_q, grad_k, grad_skip, grad_residue, grad_memory)
```

```python
import math

import jax
import jax.numpy as jnp
from jax import lax
from jax.sharding import PartitionSpec as P

HIGH_PREC = lax.Precision.HIGHEST


def mm(pattern, left_op, right_op):
    return jnp.einsum(pattern, left_op, right_op, precision=HIGH_PREC)


def exchange(shard, axis, bit):
    size = lax.axis_size(axis)
    return lax.ppermute(shard, axis, [(i, i ^ (1 << bit)) for i in range(size)])


def decay(blocks, block_len, inv_m):
    return jnp.exp(-(blocks * block_len).astype(jnp.float32) * inv_m)


def state_scan(fwd, fwd_m, bwd, inv_m, block_len):
    seq_index = lax.axis_index("seq")
    sections = lax.axis_size("seq").bit_length() - 1
    pre = jnp.zeros_like(fwd)
    pre_m = jnp.zeros_like(fwd)
    post = jnp.zeros_like(bwd)
    for bit in range(sections):
        size = 1 << bit
        recv = exchange(jnp.stack([fwd, fwd_m, bwd]), "seq", bit)
        o_fwd, o_fwd_m, o_bwd = recv[0], recv[1], recv[2]
        rank = seq_index % size
        upper = (seq_index >> bit) & 1
        lag = decay(rank, block_len, inv_m)
        lead = decay(size - 1 - rank, block_len, inv_m)
        whole = jnp.exp(-float(size * block_len) * inv_m)
        shift = float(size * block_len)
        lag_len = (rank * block_len).astype(jnp.float32)
        pre = jnp.where(upper == 1, pre + lag * o_fwd, pre)
        pre_m = jnp.where(upper == 1, pre_m + lag * (o_fwd_m + lag_len * o_fwd), pre_m)
        post = jnp.where(upper == 1, post, post + lead * o_bwd)
        lo_f, lo_fm = jnp.where(upper == 1, o_fwd, fwd), jnp.where(upper == 1, o_fwd_m, fwd_m)
        hi_f, hi_fm = jnp.where(upper == 1, fwd, o_fwd), jnp.where(upper == 1, fwd_m, o_fwd_m)
        lo_b, hi_b = jnp.where(upper == 1, o_bwd, bwd), jnp.where(upper == 1, bwd, o_bwd)
        fwd = whole * lo_f + hi_f
        fwd_m = whole * (lo_fm + shift * lo_f) + hi_fm
        bwd = lo_b + whole * hi_b
    return pre, pre_m, post


def butterfly_sum(value, axis):
    sections = lax.axis_size(axis).bit_length() - 1
    for bit in range(sections):
        value = value + exchange(value, axis, bit)
    return value


def per_device(signal_x, gate_q, gate_k, skip_gain, residue, memory, cotangent):
    channels, block_len = signal_x.shape
    seq_total = lax.axis_size("seq") * block_len
    all_channels = channels * lax.axis_size("ch")
    inv_m = 1.0 / memory
    gain = jnp.sqrt(2.0 / memory)
    amp = residue * gain
    offs = jnp.arange(block_len, dtype=jnp.float32)[:, None]
    e_down = jnp.exp(-offs * inv_m)
    e_up = jnp.exp(offs * inv_m)
    e_tail = jnp.exp(-(block_len - 1 - offs) * inv_m)
    e_next = jnp.exp(-(offs + 1) * inv_m)
    e_in = jnp.exp(-(block_len - offs) * inv_m)
    lower = offs >= offs.T
    toeplitz = jnp.where(lower, mm("tn,sn->ts", e_down * amp, e_up), 0.0)

    x_float = signal_x.astype(jnp.float32)
    q_float = gate_q.astype(jnp.float32)
    k_float = gate_k.astype(jnp.float32)
    d_float = cotangent.astype(jnp.float32)
    values = x_float * k_float
    grad_mixed = d_float * q_float

    conv_local = mm("cs,ts->ct", values, toeplitz)
    corr_local = mm("ct,ts->cs", grad_mixed, toeplitz)
    fwd = mm("cs,sn->cn", values, e_tail)
    fwd_m = mm("cs,sn->cn", values, e_tail * (block_len - 1 - offs))
    bwd = mm("ct,tn->cn", grad_mixed, e_down)
    fold = mm("ct,tn->cn", grad_mixed, e_next)
    fold_m = mm("ct,tn->cn", grad_mixed, e_next * (offs + 1) * inv_m)
    pair = jnp.where(lower, mm("ct,cs->ts", grad_mixed, values), 0.0)
    near = mm("ts,sn->tn", pair, e_up)
    near_m = mm("ts,sn->tn", pair, e_up * offs * inv_m)
    local_res = jnp.sum(e_down * near, axis=0)
    local_mem = jnp.sum(e_down * ((offs * inv_m - 0.5) * near - near_m), axis=0)

    pre, pre_m, post = state_scan(fwd, fwd_m, bwd, inv_m, block_len)

    conv_out = conv_local + mm("cn,tn->ct", pre, e_next * amp)
    corr_out = corr_local + mm("cn,sn->cs", post, e_in * amp)
    cross_res = jnp.sum(pre * fold, axis=0)
    cross_mem = jnp.sum(pre * (fold_m - 0.5 * fold) + pre_m * inv_m * fold, axis=0)

    mixed_out = conv_out + skip_gain[:, None] * values
    output = (q_float * mixed_out).astype(jnp.bfloat16)
    grad_values = skip_gain[:, None] * grad_mixed + corr_out
    grad_x = (grad_values * k_float).astype(jnp.bfloat16)
    grad_q = (d_float * mixed_out).astype(jnp.bfloat16)
    grad_k = (grad_values * x_float).astype(jnp.bfloat16)

    part_skip = jnp.sum(grad_mixed * values, axis=1)
    part_res = gain * (local_res + cross_res)
    part_mem = residue * gain * (local_mem + cross_mem)
    seq_sums = butterfly_sum(jnp.concatenate([part_res, part_mem, part_skip]), "seq")
    order = memory.shape[0]
    both = butterfly_sum(seq_sums[: 2 * order], "ch")
    norm_scale = 1.0 / math.sqrt(all_channels * seq_total)
    grad_skip = seq_sums[2 * order :] / math.sqrt(seq_total)
    grad_residue = both[:order] * norm_scale
    grad_memory = both[order:] * norm_scale
    return (output, grad_x, grad_q, grad_k, grad_skip, grad_residue, grad_memory)


def solution(mesh):
    return jax.shard_map(
        per_device,
        mesh=mesh,
        in_specs=(
            P("ch", "seq"),
            P("ch", "seq"),
            P("ch", "seq"),
            P("ch"),
            P(),
            P(),
            P("ch", "seq"),
        ),
        out_specs=(
            P("ch", "seq"),
            P("ch", "seq"),
            P("ch", "seq"),
            P("ch", "seq"),
            P("ch"),
            P(),
            P(),
        ),
        check_vma=False,
    )
```

```python
import functools
import math

import jax
import jax.numpy as jnp
from jax import lax
from jax.experimental import pallas as pl
from jax.experimental.pallas import tpu as pltpu
from jax.sharding import PartitionSpec as P

HIGH_PREC = lax.Precision.HIGHEST


def mm(pattern, left_op, right_op):
    return jnp.einsum(pattern, left_op, right_op, precision=HIGH_PREC)


STATE_SLABS = 7


def partner_of(index, bit):
    size = 1 << bit
    upper = (index // size) % 2
    return index + size - 2 * size * upper


def combine_kernel(seq_bits, ch_bits, state_ref, coef_ref, agg_ref, edge_ref,
                   send_buf, recv_buf, ch_send, ch_recv, send_sem, recv_sem, ch_send_sem, ch_recv_sem):
    seq_index = lax.axis_index("seq")
    ch_index = lax.axis_index("ch")
    barrier = pltpu.get_barrier_semaphore()
    for bit in range(seq_bits):
        pl.semaphore_signal(barrier, inc=1, device_id=(partner_of(seq_index, bit), ch_index),
                            device_id_type=pl.DeviceIdType.MESH)
    for bit in range(ch_bits):
        pl.semaphore_signal(barrier, inc=1, device_id=(seq_index, partner_of(ch_index, bit)),
                            device_id_type=pl.DeviceIdType.MESH)
    pl.semaphore_wait(barrier, seq_bits + ch_bits)

    mine = [state_ref[i] for i in range(STATE_SLABS)]
    rows = lax.broadcasted_iota(jnp.int32, mine[0].shape, 0)
    pre = jnp.zeros_like(mine[0])
    post = jnp.zeros_like(mine[0])
    for bit in range(seq_bits):
        for i in range(STATE_SLABS):
            send_buf[bit, i] = mine[i]
        copy = pltpu.make_async_remote_copy(
            src_ref=send_buf.at[bit],
            dst_ref=recv_buf.at[bit],
            send_sem=send_sem.at[bit],
            recv_sem=recv_sem.at[bit],
            device_id=(partner_of(seq_index, bit), ch_index),
            device_id_type=pl.DeviceIdType.MESH,
        )
        copy.start()
        copy.wait()
        other = [recv_buf[bit, i] for i in range(STATE_SLABS)]
        coef = coef_ref[bit]
        pick = coef[0:1] > 0.5
        whole, whole_len, whole_q = coef[1:2], coef[2:3], coef[3:4]
        lag, lead, inv_m = coef[4:5], coef[5:6], coef[6:7]
        lo = [jnp.where(pick, o, m) for o, m in zip(other, mine)]
        hi = [jnp.where(pick, m, o) for o, m in zip(other, mine)]
        pre = pre + lag * other[0]
        post = post + lead * other[2]
        cross_res = jnp.sum(lo[0] * hi[3], axis=0, keepdims=True)
        cross_mem = jnp.sum(lo[0] * hi[4] + lo[1] * hi[3] * inv_m, axis=0, keepdims=True)
        mine = [
            whole * lo[0] + hi[0],
            whole * lo[1] + whole_len * lo[0] + hi[1],
            lo[2] + whole * hi[2],
            lo[3] + whole * hi[3],
            lo[4] + whole * hi[4] + whole_q * hi[3],
            lo[5] + hi[5] + jnp.where(rows == 0, cross_res, jnp.where(rows == 1, cross_mem, 0.0)),
            lo[6] + hi[6],
        ]
    sums = mine[5]
    for bit in range(ch_bits):
        ch_send[bit] = sums
        copy = pltpu.make_async_remote_copy(
            src_ref=ch_send.at[bit],
            dst_ref=ch_recv.at[bit],
            send_sem=ch_send_sem.at[bit],
            recv_sem=ch_recv_sem.at[bit],
            device_id=(seq_index, partner_of(ch_index, bit)),
            device_id_type=pl.DeviceIdType.MESH,
        )
        copy.start()
        copy.wait()
        sums = sums + ch_recv[bit]
    agg_ref[0] = sums
    agg_ref[1] = mine[6]
    edge_ref[0] = pre
    edge_ref[1] = post


def combine_states(state, inv_m, block_len):
    seq_index = lax.axis_index("seq")
    seq_bits = lax.axis_size("seq").bit_length() - 1
    ch_bits = lax.axis_size("ch").bit_length() - 1
    coefs = []
    for bit in range(seq_bits):
        size = 1 << bit
        upper = ((seq_index // size) % 2).astype(jnp.float32)
        rank = (seq_index % size).astype(jnp.float32)
        whole = jnp.exp(-float(size * block_len) * inv_m)
        lag = upper * jnp.exp(-(rank * block_len) * inv_m)
        lead = (1.0 - upper) * jnp.exp(-((size - 1 - rank) * block_len) * inv_m)
        rows = [
            jnp.broadcast_to(upper, inv_m.shape),
            whole,
            whole * float(size * block_len),
            whole * float(size * block_len) * inv_m,
            lag,
            lead,
            inv_m,
            jnp.zeros_like(inv_m),
        ]
        coefs.append(jnp.stack(rows))
    coef = jnp.stack(coefs)
    slab = state.shape[1:]
    vmem = pl.BlockSpec(memory_space=pltpu.VMEM)
    return pl.pallas_call(
        functools.partial(combine_kernel, seq_bits, ch_bits),
        out_shape=(
            jax.ShapeDtypeStruct((2,) + slab, jnp.float32),
            jax.ShapeDtypeStruct((2,) + slab, jnp.float32),
        ),
        in_specs=[vmem, vmem],
        out_specs=(vmem, vmem),
        scratch_shapes=[
            pltpu.VMEM((seq_bits, STATE_SLABS) + slab, jnp.float32),
            pltpu.VMEM((seq_bits, STATE_SLABS) + slab, jnp.float32),
            pltpu.VMEM((ch_bits,) + slab, jnp.float32),
            pltpu.VMEM((ch_bits,) + slab, jnp.float32),
            pltpu.SemaphoreType.DMA((seq_bits,)),
            pltpu.SemaphoreType.DMA((seq_bits,)),
            pltpu.SemaphoreType.DMA((ch_bits,)),
            pltpu.SemaphoreType.DMA((ch_bits,)),
        ],
        compiler_params=pltpu.CompilerParams(collective_id=0, has_side_effects=True),
    )(state, coef)


def per_device(signal_x, gate_q, gate_k, skip_gain, residue, memory, cotangent):
    channels, block_len = signal_x.shape
    seq_total = lax.axis_size("seq") * block_len
    all_channels = channels * lax.axis_size("ch")
    inv_m = 1.0 / memory
    gain = jnp.sqrt(2.0 / memory)
    amp = residue * gain
    offs = jnp.arange(block_len, dtype=jnp.float32)[:, None]
    e_down = jnp.exp(-offs * inv_m)
    e_up = jnp.exp(offs * inv_m)
    e_tail = jnp.exp(-(block_len - 1 - offs) * inv_m)
    e_next = jnp.exp(-(offs + 1) * inv_m)
    e_in = jnp.exp(-(block_len - offs) * inv_m)
    lower = offs >= offs.T
    toeplitz = jnp.where(lower, mm("tn,sn->ts", e_down * amp, e_up), 0.0)

    x_float = signal_x.astype(jnp.float32)
    q_float = gate_q.astype(jnp.float32)
    k_float = gate_k.astype(jnp.float32)
    d_float = cotangent.astype(jnp.float32)
    values = x_float * k_float
    grad_mixed = d_float * q_float

    conv_local = mm("cs,ts->ct", values, toeplitz)
    corr_local = mm("ct,ts->cs", grad_mixed, toeplitz)
    fwd = mm("cs,sn->cn", values, e_tail)
    fwd_m = mm("cs,sn->cn", values, e_tail * (block_len - 1 - offs))
    bwd = mm("ct,tn->cn", grad_mixed, e_down)
    fold = mm("ct,tn->cn", grad_mixed, e_next)
    fold_m = mm("ct,tn->cn", grad_mixed, e_next * (offs + 1) * inv_m)
    pair = jnp.where(lower, mm("ct,cs->ts", grad_mixed, values), 0.0)
    near = mm("ts,sn->tn", pair, e_up)
    near_m = mm("ts,sn->tn", pair, e_up * offs * inv_m)
    local_res = jnp.sum(e_down * near, axis=0)
    local_mem = jnp.sum(e_down * ((offs * inv_m - 0.5) * near - near_m), axis=0)

    rows = lax.broadcasted_iota(jnp.int32, fwd.shape, 0)
    sums = jnp.where(rows == 0, local_res[None, :], jnp.where(rows == 1, local_mem[None, :], 0.0))
    part_skip = jnp.sum(grad_mixed * values, axis=1)
    state = jnp.stack([fwd, fwd_m, bwd, fold, fold_m - 0.5 * fold, sums, jnp.broadcast_to(part_skip[:, None], fwd.shape)])
    agg, edge = combine_states(state, inv_m, block_len)
    pre, post = edge[0], edge[1]

    conv_out = conv_local + mm("cn,tn->ct", pre, e_next * amp)
    corr_out = corr_local + mm("cn,sn->cs", post, e_in * amp)

    mixed_out = conv_out + skip_gain[:, None] * values
    output = (q_float * mixed_out).astype(jnp.bfloat16)
    grad_values = skip_gain[:, None] * grad_mixed + corr_out
    grad_x = (grad_values * k_float).astype(jnp.bfloat16)
    grad_q = (d_float * mixed_out).astype(jnp.bfloat16)
    grad_k = (grad_values * x_float).astype(jnp.bfloat16)

    norm_scale = 1.0 / math.sqrt(all_channels * seq_total)
    grad_skip = agg[1][:, 0] / math.sqrt(seq_total)
    grad_residue = gain * agg[0][0] * norm_scale
    grad_memory = residue * gain * agg[0][1] * norm_scale
    return (output, grad_x, grad_q, grad_k, grad_skip, grad_residue, grad_memory)


def solution(mesh):
    return jax.shard_map(
        per_device,
        mesh=mesh,
        in_specs=(
            P("ch", "seq"),
            P("ch", "seq"),
            P("ch", "seq"),
            P("ch"),
            P(),
            P(),
            P("ch", "seq"),
        ),
        out_specs=(
            P("ch", "seq"),
            P("ch", "seq"),
            P("ch", "seq"),
            P("ch", "seq"),
            P("ch"),
            P(),
            P(),
        ),
        check_vma=False,
    )
```

```python
import functools
import math

import jax
import jax.numpy as jnp
from jax import lax
from jax.experimental import pallas as pl
from jax.experimental.pallas import tpu as pltpu
from jax.sharding import PartitionSpec as P

HIGH_PREC = lax.Precision.HIGHEST


def mm(pattern, left_op, right_op):
    return jnp.einsum(pattern, left_op, right_op, precision=HIGH_PREC)


GROUP = 8
LANES = 128
SLAB_NAMES = ("fwd", "fwd_m", "bwd", "fold", "fold_v", "res", "mem", "skip")


def unpack(block, rows):
    return {name: block[i * rows:(i + 1) * rows] for i, name in enumerate(SLAB_NAMES)}


def chan_sum(value, modes):
    total = value[0:1]
    for row in range(1, value.shape[0]):
        total = total + value[row:row + 1]
    shift = LANES // 2
    while shift >= modes:
        total = total + pltpu.roll(total, shift, 1)
        shift //= 2
    return jnp.broadcast_to(total, value.shape)


def fold_items(items, coef_ref, rows, modes):
    acc = unpack(items[0], rows)
    coef = coef_ref[0]
    pre = coef[5:6] * acc["fwd"]
    post = coef[6:7] * acc["bwd"]
    for index in range(1, len(items)):
        item = unpack(items[index], rows)
        coef = coef_ref[index]
        step, step_len, lag, lag_q, inv_m = coef[0:1], coef[1:2], coef[2:3], coef[3:4], coef[4:5]
        pre = pre + coef[5:6] * item["fwd"]
        post = post + coef[6:7] * item["bwd"]
        cross_res = chan_sum(acc["fwd"] * item["fold"], modes)
        cross_mem = chan_sum(acc["fwd"] * item["fold_v"] + acc["fwd_m"] * item["fold"] * inv_m, modes)
        acc = {
            "fwd": step * acc["fwd"] + item["fwd"],
            "fwd_m": step * acc["fwd_m"] + step_len * acc["fwd"] + item["fwd_m"],
            "bwd": acc["bwd"] + lag * item["bwd"],
            "fold": acc["fold"] + lag * item["fold"],
            "fold_v": acc["fold_v"] + lag * item["fold_v"] + lag_q * item["fold"],
            "res": acc["res"] + item["res"] + cross_res,
            "mem": acc["mem"] + item["mem"] + cross_mem,
            "skip": acc["skip"] + item["skip"],
        }
    return acc, pre, post


def gather_ring(buf, send_sems, recv_sems, count, pos, device_of):
    descs = []
    for dist in range(1, count):
        desc = pltpu.make_async_remote_copy(
            src_ref=buf.at[0],
            dst_ref=buf.at[count - dist],
            send_sem=send_sems.at[dist],
            recv_sem=recv_sems.at[count - dist],
            device_id=device_of((pos + dist) % count),
            device_id_type=pl.DeviceIdType.MESH,
        )
        desc.start()
        descs.append(desc)
    for desc in descs:
        desc.wait_recv()
    for desc in descs:
        desc.wait_send()
    return [buf[(slot - pos + count) % count] for slot in range(count)]


def combine_kernel(counts, rows, modes, state_ref, coef_a, coef_b, fin_ref, out_ref,
                   buf_a, buf_b, buf_c, send_a, recv_a, send_b, recv_b, send_c, recv_c):
    count_a, count_b, count_c = counts
    seq_index = lax.axis_index("seq")
    ch_index = lax.axis_index("ch")
    pos_a = seq_index % count_a
    pos_b = seq_index // count_a

    def dev_a(other):
        return (pos_b * count_a + other, ch_index)

    def dev_b(other):
        return (other * count_a + pos_a, ch_index)

    def dev_c(other):
        return (seq_index, other)

    barrier = pltpu.get_barrier_semaphore()
    for count, pos, device_of in ((count_a, pos_a, dev_a), (count_b, pos_b, dev_b), (count_c, ch_index, dev_c)):
        for dist in range(1, count):
            pl.semaphore_signal(barrier, inc=1, device_id=device_of((pos + dist) % count),
                                device_id_type=pl.DeviceIdType.MESH)
    pl.semaphore_wait(barrier, count_a + count_b + count_c - 3)

    buf_a[0] = state_ref[...]
    items = gather_ring(buf_a, send_a, recv_a, count_a, pos_a, dev_a)
    group, pre_a, post_a = fold_items(items, coef_a, rows, modes)
    buf_b[0] = jnp.concatenate([group[name] for name in SLAB_NAMES], axis=0)
    items = gather_ring(buf_b, send_b, recv_b, count_b, pos_b, dev_b)
    total, pre_b, post_b = fold_items(items, coef_b, rows, modes)
    fin = fin_ref[...]
    pre = fin[0:1] * pre_b + pre_a
    post = fin[1:2] * post_b + post_a
    buf_c[0] = jnp.concatenate([total["res"], total["mem"]], axis=0)
    items = gather_ring(buf_c, send_c, recv_c, count_c, ch_index, dev_c)
    sums = items[0]
    for item in items[1:]:
        sums = sums + item
    out_ref[...] = jnp.concatenate([pre, post, sums, total["skip"], jnp.zeros_like(total["skip"])], axis=0)


def lanes_of(vec):
    return jnp.tile(vec, LANES // vec.shape[0])


def fold_coefs(count, size, pos, inv_m, block_len):
    def decay(blocks):
        return jnp.exp(-(blocks * block_len) * inv_m)

    step = decay(float(size))
    coefs = []
    for index in range(count):
        lag = decay(float(index * size))
        before = (index < pos).astype(jnp.float32) * decay(jnp.maximum(pos - 1 - index, 0).astype(jnp.float32) * size)
        after = (index > pos).astype(jnp.float32) * decay(jnp.maximum(index - pos - 1, 0).astype(jnp.float32) * size)
        rows = [step, step * float(size * block_len), lag, lag * float(index * size * block_len) * inv_m,
                inv_m, before, after, jnp.zeros_like(inv_m)]
        coefs.append(jnp.stack([lanes_of(r) for r in rows]))
    return jnp.stack(coefs)


def combine_states(slabs, inv_m, block_len):
    channels, modes = slabs[0].shape
    rows = channels * modes // LANES
    seq_index = lax.axis_index("seq")
    count_a = min(GROUP, lax.axis_size("seq"))
    count_b = lax.axis_size("seq") // count_a
    count_c = lax.axis_size("ch")
    pos_a = seq_index % count_a
    pos_b = seq_index // count_a
    state = jnp.concatenate([s.reshape(rows, LANES) for s in slabs], axis=0)
    coef_a = fold_coefs(count_a, 1, pos_a, inv_m, block_len)
    coef_b = fold_coefs(count_b, count_a, pos_b, inv_m, block_len)
    near = jnp.exp(-(pos_a * block_len).astype(jnp.float32) * inv_m)
    far = jnp.exp(-((count_a - 1 - pos_a) * block_len).astype(jnp.float32) * inv_m)
    fin = jnp.stack([lanes_of(near), lanes_of(far)] + [lanes_of(jnp.zeros_like(inv_m))] * 6)
    msg = (len(SLAB_NAMES) * rows, LANES)
    vmem = pl.BlockSpec(memory_space=pltpu.VMEM)
    out = pl.pallas_call(
        functools.partial(combine_kernel, (count_a, count_b, count_c), rows, modes),
        out_shape=jax.ShapeDtypeStruct((6 * rows, LANES), jnp.float32),
        in_specs=[vmem] * 4,
        out_specs=vmem,
        scratch_shapes=[
            pltpu.VMEM((count_a,) + msg, jnp.float32),
            pltpu.VMEM((count_b,) + msg, jnp.float32),
            pltpu.VMEM((count_c, 2 * rows, LANES), jnp.float32),
            pltpu.SemaphoreType.DMA((count_a,)),
            pltpu.SemaphoreType.DMA((count_a,)),
            pltpu.SemaphoreType.DMA((count_b,)),
            pltpu.SemaphoreType.DMA((count_b,)),
            pltpu.SemaphoreType.DMA((count_c,)),
            pltpu.SemaphoreType.DMA((count_c,)),
        ],
        compiler_params=pltpu.CompilerParams(collective_id=0, has_side_effects=True),
    )(state, coef_a, coef_b, fin)
    pieces = [out[i * rows:(i + 1) * rows].reshape(channels, modes) for i in range(5)]
    return pieces


def per_device(signal_x, gate_q, gate_k, skip_gain, residue, memory, cotangent):
    channels, block_len = signal_x.shape
    seq_total = lax.axis_size("seq") * block_len
    all_channels = channels * lax.axis_size("ch")
    inv_m = 1.0 / memory
    gain = jnp.sqrt(2.0 / memory)
    amp = residue * gain
    offs = jnp.arange(block_len, dtype=jnp.float32)[:, None]
    e_down = jnp.exp(-offs * inv_m)
    e_up = jnp.exp(offs * inv_m)
    e_tail = jnp.exp(-(block_len - 1 - offs) * inv_m)
    e_next = jnp.exp(-(offs + 1) * inv_m)
    e_in = jnp.exp(-(block_len - offs) * inv_m)
    lower = offs >= offs.T
    toeplitz = jnp.where(lower, mm("tn,sn->ts", e_down * amp, e_up), 0.0)

    x_float = signal_x.astype(jnp.float32)
    q_float = gate_q.astype(jnp.float32)
    k_float = gate_k.astype(jnp.float32)
    d_float = cotangent.astype(jnp.float32)
    values = x_float * k_float
    grad_mixed = d_float * q_float

    conv_local = mm("cs,ts->ct", values, toeplitz)
    corr_local = mm("ct,ts->cs", grad_mixed, toeplitz)
    fwd = mm("cs,sn->cn", values, e_tail)
    fwd_m = mm("cs,sn->cn", values, e_tail * (block_len - 1 - offs))
    bwd = mm("ct,tn->cn", grad_mixed, e_down)
    fold = mm("ct,tn->cn", grad_mixed, e_next)
    fold_m = mm("ct,tn->cn", grad_mixed, e_next * (offs + 1) * inv_m)
    pair = jnp.where(lower, mm("ct,cs->ts", grad_mixed, values), 0.0)
    near = mm("ts,sn->tn", pair, e_up)
    near_m = mm("ts,sn->tn", pair, e_up * offs * inv_m)
    local_res = jnp.sum(e_down * near, axis=0)
    local_mem = jnp.sum(e_down * ((offs * inv_m - 0.5) * near - near_m), axis=0)

    part_skip = jnp.sum(grad_mixed * values, axis=1)
    slabs = [fwd, fwd_m, bwd, fold, fold_m - 0.5 * fold]
    slabs += [jnp.broadcast_to(v, fwd.shape) for v in (local_res[None, :], local_mem[None, :], part_skip[:, None])]
    pre, post, res_sum, mem_sum, skip_sum = combine_states(slabs, inv_m, block_len)

    conv_out = conv_local + mm("cn,tn->ct", pre, e_next * amp)
    corr_out = corr_local + mm("cn,sn->cs", post, e_in * amp)

    mixed_out = conv_out + skip_gain[:, None] * values
    output = (q_float * mixed_out).astype(jnp.bfloat16)
    grad_values = skip_gain[:, None] * grad_mixed + corr_out
    grad_x = (grad_values * k_float).astype(jnp.bfloat16)
    grad_q = (d_float * mixed_out).astype(jnp.bfloat16)
    grad_k = (grad_values * x_float).astype(jnp.bfloat16)

    norm_scale = 1.0 / math.sqrt(all_channels * seq_total)
    grad_skip = skip_sum[:, 0] / math.sqrt(seq_total)
    grad_residue = gain * res_sum[0] * norm_scale
    grad_memory = residue * gain * mem_sum[0] * norm_scale
    return (output, grad_x, grad_q, grad_k, grad_skip, grad_residue, grad_memory)


def solution(mesh):
    return jax.shard_map(
        per_device,
        mesh=mesh,
        in_specs=(
            P("ch", "seq"),
            P("ch", "seq"),
            P("ch", "seq"),
            P("ch"),
            P(),
            P(),
            P("ch", "seq"),
        ),
        out_specs=(
            P("ch", "seq"),
            P("ch", "seq"),
            P("ch", "seq"),
            P("ch", "seq"),
            P("ch"),
            P(),
            P(),
        ),
        check_vma=False,
    )
```

```python
import functools
import math

import jax
import jax.numpy as jnp
from jax import lax
from jax.experimental import pallas as pl
from jax.experimental.pallas import tpu as pltpu
from jax.sharding import PartitionSpec as P

HIGH_PREC = lax.Precision.HIGHEST


def mm(pattern, left_op, right_op):
    return jnp.einsum(pattern, left_op, right_op, precision=HIGH_PREC)


GROUP = 8
LANES = 128
SLAB_NAMES = ("fwd", "fwd_m", "bwd", "fold", "fold_v", "res", "mem", "skip")


def unpack(block, rows):
    return {name: block[i * rows:(i + 1) * rows] for i, name in enumerate(SLAB_NAMES)}


def chan_sum(value, modes):
    total = value[0:1]
    for row in range(1, value.shape[0]):
        total = total + value[row:row + 1]
    shift = LANES // 2
    while shift >= modes:
        total = total + pltpu.roll(total, shift, 1)
        shift //= 2
    return jnp.broadcast_to(total, value.shape)


def fold_items(items, coef_ref, rows, modes):
    acc = unpack(items[0], rows)
    coef = coef_ref[0]
    pre = coef[5:6] * acc["fwd"]
    post = coef[6:7] * acc["bwd"]
    for index in range(1, len(items)):
        item = unpack(items[index], rows)
        coef = coef_ref[index]
        step, step_len, lag, lag_q, inv_m = coef[0:1], coef[1:2], coef[2:3], coef[3:4], coef[4:5]
        pre = pre + coef[5:6] * item["fwd"]
        post = post + coef[6:7] * item["bwd"]
        cross_res = chan_sum(acc["fwd"] * item["fold"], modes)
        cross_mem = chan_sum(acc["fwd"] * item["fold_v"] + acc["fwd_m"] * item["fold"] * inv_m, modes)
        acc = {
            "fwd": step * acc["fwd"] + item["fwd"],
            "fwd_m": step * acc["fwd_m"] + step_len * acc["fwd"] + item["fwd_m"],
            "bwd": acc["bwd"] + lag * item["bwd"],
            "fold": acc["fold"] + lag * item["fold"],
            "fold_v": acc["fold_v"] + lag * item["fold_v"] + lag_q * item["fold"],
            "res": acc["res"] + item["res"] + cross_res,
            "mem": acc["mem"] + item["mem"] + cross_mem,
            "skip": acc["skip"] + item["skip"],
        }
    return acc, pre, post


def gather_ring(buf, send_sems, recv_sems, count, pos, device_of):
    descs = []
    for dist in range(1, count):
        desc = pltpu.make_async_remote_copy(
            src_ref=buf.at[0],
            dst_ref=buf.at[count - dist],
            send_sem=send_sems.at[dist],
            recv_sem=recv_sems.at[count - dist],
            device_id=device_of((pos + dist) % count),
            device_id_type=pl.DeviceIdType.MESH,
        )
        desc.start()
        descs.append(desc)
    for desc in descs:
        desc.wait_recv()
    for desc in descs:
        desc.wait_send()
    return [buf[(slot - pos + count) % count] for slot in range(count)]


def combine_kernel(counts, rows, modes, state_ref, coef_a, coef_b, fin_ref, out_ref,
                   buf_a, buf_b, buf_c, send_a, recv_a, send_b, recv_b, send_c, recv_c):
    count_a, count_b, count_c = counts
    seq_index = lax.axis_index("seq")
    ch_index = lax.axis_index("ch")
    pos_a = seq_index % count_a
    pos_b = seq_index // count_a

    def dev_a(other):
        return (pos_b * count_a + other, ch_index)

    def dev_b(other):
        return (other * count_a + pos_a, ch_index)

    def dev_c(other):
        return (seq_index, other)

    barrier = pltpu.get_barrier_semaphore()
    for count, pos, device_of in ((count_a, pos_a, dev_a), (count_b, pos_b, dev_b), (count_c, ch_index, dev_c)):
        for dist in range(1, count):
            pl.semaphore_signal(barrier, inc=1, device_id=device_of((pos + dist) % count),
                                device_id_type=pl.DeviceIdType.MESH)
    pl.semaphore_wait(barrier, count_a + count_b + count_c - 3)

    buf_a[0] = state_ref[...]
    items = gather_ring(buf_a, send_a, recv_a, count_a, pos_a, dev_a)
    group, pre_a, post_a = fold_items(items, coef_a, rows, modes)
    buf_b[0] = jnp.concatenate([group[name] for name in SLAB_NAMES], axis=0)
    items = gather_ring(buf_b, send_b, recv_b, count_b, pos_b, dev_b)
    total, pre_b, post_b = fold_items(items, coef_b, rows, modes)
    fin = fin_ref[...]
    pre = fin[0:1] * pre_b + pre_a
    post = fin[1:2] * post_b + post_a
    buf_c[0] = jnp.concatenate([total["res"], total["mem"]], axis=0)
    items = gather_ring(buf_c, send_c, recv_c, count_c, ch_index, dev_c)
    sums = items[0]
    for item in items[1:]:
        sums = sums + item
    out_ref[...] = jnp.concatenate([pre, post, sums, total["skip"], jnp.zeros_like(total["skip"])], axis=0)


def lanes_of(vec):
    return jnp.tile(vec, LANES // vec.shape[0])


def fold_coefs(count, size, pos, inv_m, block_len):
    inv = lanes_of(inv_m)[None, :]
    index = jnp.arange(count, dtype=jnp.int32)[:, None]
    span = float(size * block_len)
    step = jnp.broadcast_to(jnp.exp(-span * inv), (count, LANES))
    starts = index.astype(jnp.float32) * span
    lag = jnp.exp(-starts * inv)
    before = jnp.where(index < pos, jnp.exp(-((pos - 1 - index).astype(jnp.float32) * span) * inv), 0.0)
    after = jnp.where(index > pos, jnp.exp(-((index - pos - 1).astype(jnp.float32) * span) * inv), 0.0)
    rows = [step, step * span, lag, lag * starts * inv, jnp.broadcast_to(inv, (count, LANES)), before, after,
            jnp.zeros((count, LANES), jnp.float32)]
    return jnp.stack(rows, axis=1)


def combine_states(slabs, inv_m, block_len):
    channels, modes = slabs[0].shape
    rows = channels * modes // LANES
    seq_index = lax.axis_index("seq")
    count_a = min(GROUP, lax.axis_size("seq"))
    count_b = lax.axis_size("seq") // count_a
    count_c = lax.axis_size("ch")
    pos_a = seq_index % count_a
    pos_b = seq_index // count_a
    state = jnp.concatenate([s.reshape(rows, LANES) for s in slabs], axis=0)
    coef_a = fold_coefs(count_a, 1, pos_a, inv_m, block_len)
    coef_b = fold_coefs(count_b, count_a, pos_b, inv_m, block_len)
    near = jnp.exp(-(pos_a * block_len).astype(jnp.float32) * inv_m)
    far = jnp.exp(-((count_a - 1 - pos_a) * block_len).astype(jnp.float32) * inv_m)
    fin = jnp.stack([lanes_of(near), lanes_of(far)] + [lanes_of(jnp.zeros_like(inv_m))] * 6)
    msg = (len(SLAB_NAMES) * rows, LANES)
    vmem = pl.BlockSpec(memory_space=pltpu.VMEM)
    out = pl.pallas_call(
        functools.partial(combine_kernel, (count_a, count_b, count_c), rows, modes),
        out_shape=jax.ShapeDtypeStruct((6 * rows, LANES), jnp.float32),
        in_specs=[vmem] * 4,
        out_specs=vmem,
        scratch_shapes=[
            pltpu.VMEM((count_a,) + msg, jnp.float32),
            pltpu.VMEM((count_b,) + msg, jnp.float32),
            pltpu.VMEM((count_c, 2 * rows, LANES), jnp.float32),
            pltpu.SemaphoreType.DMA((count_a,)),
            pltpu.SemaphoreType.DMA((count_a,)),
            pltpu.SemaphoreType.DMA((count_b,)),
            pltpu.SemaphoreType.DMA((count_b,)),
            pltpu.SemaphoreType.DMA((count_c,)),
            pltpu.SemaphoreType.DMA((count_c,)),
        ],
        compiler_params=pltpu.CompilerParams(collective_id=0, has_side_effects=True),
    )(state, coef_a, coef_b, fin)
    pieces = [out[i * rows:(i + 1) * rows].reshape(channels, modes) for i in range(5)]
    return pieces


def per_device(signal_x, gate_q, gate_k, skip_gain, residue, memory, cotangent):
    channels, block_len = signal_x.shape
    seq_total = lax.axis_size("seq") * block_len
    all_channels = channels * lax.axis_size("ch")
    inv_m = 1.0 / memory
    gain = jnp.sqrt(2.0 / memory)
    amp = residue * gain
    offs = jnp.arange(block_len, dtype=jnp.float32)[:, None]
    e_down = jnp.exp(-offs * inv_m)
    e_up = jnp.exp(offs * inv_m)
    e_tail = jnp.exp(-(block_len - 1 - offs) * inv_m)
    e_next = jnp.exp(-(offs + 1) * inv_m)
    e_in = jnp.exp(-(block_len - offs) * inv_m)
    lower = offs >= offs.T
    toeplitz = jnp.where(lower, mm("tn,sn->ts", e_down * amp, e_up), 0.0)

    x_float = signal_x.astype(jnp.float32)
    q_float = gate_q.astype(jnp.float32)
    k_float = gate_k.astype(jnp.float32)
    d_float = cotangent.astype(jnp.float32)
    values = x_float * k_float
    grad_mixed = d_float * q_float

    conv_local = mm("cs,ts->ct", values, toeplitz)
    corr_local = mm("ct,ts->cs", grad_mixed, toeplitz)
    fwd = mm("cs,sn->cn", values, e_tail)
    fwd_m = mm("cs,sn->cn", values, e_tail * (block_len - 1 - offs))
    bwd = mm("ct,tn->cn", grad_mixed, e_down)
    fold = mm("ct,tn->cn", grad_mixed, e_next)
    fold_m = mm("ct,tn->cn", grad_mixed, e_next * (offs + 1) * inv_m)
    pair = jnp.where(lower, mm("ct,cs->ts", grad_mixed, values), 0.0)
    near = mm("ts,sn->tn", pair, e_up)
    near_m = mm("ts,sn->tn", pair, e_up * offs * inv_m)
    local_res = jnp.sum(e_down * near, axis=0)
    local_mem = jnp.sum(e_down * ((offs * inv_m - 0.5) * near - near_m), axis=0)

    part_skip = jnp.sum(grad_mixed * values, axis=1)
    slabs = [fwd, fwd_m, bwd, fold, fold_m - 0.5 * fold]
    slabs += [jnp.broadcast_to(v, fwd.shape) for v in (local_res[None, :], local_mem[None, :], part_skip[:, None])]
    pre, post, res_sum, mem_sum, skip_sum = combine_states(slabs, inv_m, block_len)

    conv_out = conv_local + mm("cn,tn->ct", pre, e_next * amp)
    corr_out = corr_local + mm("cn,sn->cs", post, e_in * amp)

    mixed_out = conv_out + skip_gain[:, None] * values
    output = (q_float * mixed_out).astype(jnp.bfloat16)
    grad_values = skip_gain[:, None] * grad_mixed + corr_out
    grad_x = (grad_values * k_float).astype(jnp.bfloat16)
    grad_q = (d_float * mixed_out).astype(jnp.bfloat16)
    grad_k = (grad_values * x_float).astype(jnp.bfloat16)

    norm_scale = 1.0 / math.sqrt(all_channels * seq_total)
    grad_skip = skip_sum[:, 0] / math.sqrt(seq_total)
    grad_residue = gain * res_sum[0] * norm_scale
    grad_memory = residue * gain * mem_sum[0] * norm_scale
    return (output, grad_x, grad_q, grad_k, grad_skip, grad_residue, grad_memory)


def solution(mesh):
    return jax.shard_map(
        per_device,
        mesh=mesh,
        in_specs=(
            P("ch", "seq"),
            P("ch", "seq"),
            P("ch", "seq"),
            P("ch"),
            P(),
            P(),
            P("ch", "seq"),
        ),
        out_specs=(
            P("ch", "seq"),
            P("ch", "seq"),
            P("ch", "seq"),
            P("ch", "seq"),
            P("ch"),
            P(),
            P(),
        ),
        check_vma=False,
    )
```

```python
import functools
import math

import jax
import jax.numpy as jnp
from jax import lax
from jax.experimental import pallas as pl
from jax.experimental.pallas import tpu as pltpu
from jax.sharding import PartitionSpec as P

HIGH_PREC = lax.Precision.HIGHEST


def mm(pattern, left_op, right_op):
    return jnp.einsum(pattern, left_op, right_op, precision=HIGH_PREC)


GROUP = 8
LANES = 128
SLAB_NAMES = ("fwd", "fwd_m", "bwd", "fold", "fold_v", "res", "mem", "skip")


def unpack(block, rows):
    return {name: block[i * rows:(i + 1) * rows] for i, name in enumerate(SLAB_NAMES)}


def chan_sum(value, modes):
    total = value[0:1]
    for row in range(1, value.shape[0]):
        total = total + value[row:row + 1]
    shift = LANES // 2
    while shift >= modes:
        total = total + pltpu.roll(total, shift, 1)
        shift //= 2
    return jnp.broadcast_to(total, value.shape)


def fold_items(items, coefs, rows, modes):
    step, step_len, lags, lags_q, inv_m, befores, afters = coefs
    acc = unpack(items[0], rows)
    pre = befores[0:1] * acc["fwd"]
    post = afters[0:1] * acc["bwd"]
    for index in range(1, len(items)):
        item = unpack(items[index], rows)
        lag, lag_q = lags[index:index + 1], lags_q[index:index + 1]
        pre = pre + befores[index:index + 1] * item["fwd"]
        post = post + afters[index:index + 1] * item["bwd"]
        cross_res = chan_sum(acc["fwd"] * item["fold"], modes)
        cross_mem = chan_sum(acc["fwd"] * item["fold_v"] + acc["fwd_m"] * item["fold"] * inv_m, modes)
        acc = {
            "fwd": step * acc["fwd"] + item["fwd"],
            "fwd_m": step * acc["fwd_m"] + step_len * acc["fwd"] + item["fwd_m"],
            "bwd": acc["bwd"] + lag * item["bwd"],
            "fold": acc["fold"] + lag * item["fold"],
            "fold_v": acc["fold_v"] + lag * item["fold_v"] + lag_q * item["fold"],
            "res": acc["res"] + item["res"] + cross_res,
            "mem": acc["mem"] + item["mem"] + cross_mem,
            "skip": acc["skip"] + item["skip"],
        }
    return acc, pre, post


def gather_ring(buf, send_sems, recv_sems, count, pos, device_of):
    descs = []
    for dist in range(1, count):
        desc = pltpu.make_async_remote_copy(
            src_ref=buf.at[0],
            dst_ref=buf.at[count - dist],
            send_sem=send_sems.at[dist],
            recv_sem=recv_sems.at[count - dist],
            device_id=device_of((pos + dist) % count),
            device_id_type=pl.DeviceIdType.MESH,
        )
        desc.start()
        descs.append(desc)
    for desc in descs:
        desc.wait_recv()
    for desc in descs:
        desc.wait_send()
    return [buf[(slot - pos + count) % count] for slot in range(count)]


def fold_coefs(count, size, pos, inv, block_len):
    index = lax.broadcasted_iota(jnp.int32, (count, LANES), 0)
    span = float(size * block_len)
    step = jnp.exp(-span * inv)
    starts = index.astype(jnp.float32) * span
    lag = jnp.exp(-starts * inv)
    before = jnp.where(index < pos, jnp.exp(-((pos - 1 - index).astype(jnp.float32) * span) * inv), 0.0)
    after = jnp.where(index > pos, jnp.exp(-((index - pos - 1).astype(jnp.float32) * span) * inv), 0.0)
    return step, step * span, lag, lag * starts * inv, inv, before, after


def combine_kernel(counts, rows, modes, block_len, *refs):
    count_a, count_b, count_c = counts
    slab_refs = refs[:len(SLAB_NAMES)]
    inv_ref, out_ref, buf_a, buf_b, buf_c, send_a, recv_a, send_b, recv_b, send_c, recv_c = refs[len(SLAB_NAMES):]
    seq_index = lax.axis_index("seq")
    ch_index = lax.axis_index("ch")
    pos_a = seq_index % count_a
    pos_b = seq_index // count_a

    def dev_a(other):
        return (pos_b * count_a + other, ch_index)

    def dev_b(other):
        return (other * count_a + pos_a, ch_index)

    def dev_c(other):
        return (seq_index, other)

    barrier = pltpu.get_barrier_semaphore()
    for count, pos, device_of in ((count_a, pos_a, dev_a), (count_b, pos_b, dev_b), (count_c, ch_index, dev_c)):
        for dist in range(1, count):
            pl.semaphore_signal(barrier, inc=1, device_id=device_of((pos + dist) % count),
                                device_id_type=pl.DeviceIdType.MESH)

    for i, ref in enumerate(slab_refs):
        buf_a[0, i * rows:(i + 1) * rows, :] = ref[...]
    inv = inv_ref[...][0:1]
    coefs_a = fold_coefs(count_a, 1, pos_a, inv, block_len)
    coefs_b = fold_coefs(count_b, count_a, pos_b, inv, block_len)
    near = jnp.exp(-(pos_a * block_len).astype(jnp.float32) * inv)
    far = jnp.exp(-((count_a - 1 - pos_a) * block_len).astype(jnp.float32) * inv)
    pl.semaphore_wait(barrier, count_a + count_b + count_c - 3)

    items = gather_ring(buf_a, send_a, recv_a, count_a, pos_a, dev_a)
    group, pre_a, post_a = fold_items(items, coefs_a, rows, modes)
    buf_b[0] = jnp.concatenate([group[name] for name in SLAB_NAMES], axis=0)
    items = gather_ring(buf_b, send_b, recv_b, count_b, pos_b, dev_b)
    total, pre_b, post_b = fold_items(items, coefs_b, rows, modes)
    pre = near * pre_b + pre_a
    post = far * post_b + post_a
    buf_c[0] = jnp.concatenate([total["res"], total["mem"]], axis=0)
    items = gather_ring(buf_c, send_c, recv_c, count_c, ch_index, dev_c)
    sums = items[0]
    for item in items[1:]:
        sums = sums + item
    out_ref[...] = jnp.concatenate([pre, post, sums, total["skip"], jnp.zeros_like(total["skip"])], axis=0)


def lanes_of(vec):
    return jnp.tile(vec, LANES // vec.shape[0])


def combine_states(slabs, inv_m, block_len):
    channels, modes = slabs[0].shape
    rows = channels * modes // LANES
    count_a = min(GROUP, lax.axis_size("seq"))
    count_b = lax.axis_size("seq") // count_a
    count_c = lax.axis_size("ch")
    packed = [s.reshape(rows, LANES) for s in slabs]
    inv = jnp.broadcast_to(lanes_of(inv_m)[None, :], (8, LANES))
    msg = (len(SLAB_NAMES) * rows, LANES)
    vmem = pl.BlockSpec(memory_space=pltpu.VMEM)
    out = pl.pallas_call(
        functools.partial(combine_kernel, (count_a, count_b, count_c), rows, modes, block_len),
        out_shape=jax.ShapeDtypeStruct((6 * rows, LANES), jnp.float32),
        in_specs=[vmem] * (len(SLAB_NAMES) + 1),
        out_specs=vmem,
        scratch_shapes=[
            pltpu.VMEM((count_a,) + msg, jnp.float32),
            pltpu.VMEM((count_b,) + msg, jnp.float32),
            pltpu.VMEM((count_c, 2 * rows, LANES), jnp.float32),
            pltpu.SemaphoreType.DMA((count_a,)),
            pltpu.SemaphoreType.DMA((count_a,)),
            pltpu.SemaphoreType.DMA((count_b,)),
            pltpu.SemaphoreType.DMA((count_b,)),
            pltpu.SemaphoreType.DMA((count_c,)),
            pltpu.SemaphoreType.DMA((count_c,)),
        ],
        compiler_params=pltpu.CompilerParams(collective_id=0, has_side_effects=True),
    )(*packed, inv)
    pieces = [out[i * rows:(i + 1) * rows].reshape(channels, modes) for i in range(5)]
    return pieces


def per_device(signal_x, gate_q, gate_k, skip_gain, residue, memory, cotangent):
    channels, block_len = signal_x.shape
    seq_total = lax.axis_size("seq") * block_len
    all_channels = channels * lax.axis_size("ch")
    inv_m = 1.0 / memory
    gain = jnp.sqrt(2.0 / memory)
    amp = residue * gain
    offs = jnp.arange(block_len, dtype=jnp.float32)[:, None]
    e_down = jnp.exp(-offs * inv_m)
    e_up = jnp.exp(offs * inv_m)
    e_tail = jnp.exp(-(block_len - 1 - offs) * inv_m)
    e_next = jnp.exp(-(offs + 1) * inv_m)
    e_in = jnp.exp(-(block_len - offs) * inv_m)
    lower = offs >= offs.T
    toeplitz = jnp.where(lower, mm("tn,sn->ts", e_down * amp, e_up), 0.0)

    x_float = signal_x.astype(jnp.float32)
    q_float = gate_q.astype(jnp.float32)
    k_float = gate_k.astype(jnp.float32)
    d_float = cotangent.astype(jnp.float32)
    values = x_float * k_float
    grad_mixed = d_float * q_float

    conv_local = mm("cs,ts->ct", values, toeplitz)
    corr_local = mm("ct,ts->cs", grad_mixed, toeplitz)
    fwd = mm("cs,sn->cn", values, e_tail)
    fwd_m = mm("cs,sn->cn", values, e_tail * (block_len - 1 - offs))
    bwd = mm("ct,tn->cn", grad_mixed, e_down)
    fold = mm("ct,tn->cn", grad_mixed, e_next)
    fold_m = mm("ct,tn->cn", grad_mixed, e_next * (offs + 1) * inv_m)
    pair = jnp.where(lower, mm("ct,cs->ts", grad_mixed, values), 0.0)
    near = mm("ts,sn->tn", pair, e_up)
    near_m = mm("ts,sn->tn", pair, e_up * offs * inv_m)
    local_res = jnp.sum(e_down * near, axis=0)
    local_mem = jnp.sum(e_down * ((offs * inv_m - 0.5) * near - near_m), axis=0)

    part_skip = jnp.sum(grad_mixed * values, axis=1)
    slabs = [fwd, fwd_m, bwd, fold, fold_m - 0.5 * fold]
    slabs += [jnp.broadcast_to(v, fwd.shape) for v in (local_res[None, :], local_mem[None, :], part_skip[:, None])]
    pre, post, res_sum, mem_sum, skip_sum = combine_states(slabs, inv_m, block_len)

    conv_out = conv_local + mm("cn,tn->ct", pre, e_next * amp)
    corr_out = corr_local + mm("cn,sn->cs", post, e_in * amp)

    mixed_out = conv_out + skip_gain[:, None] * values
    output = (q_float * mixed_out).astype(jnp.bfloat16)
    grad_values = skip_gain[:, None] * grad_mixed + corr_out
    grad_x = (grad_values * k_float).astype(jnp.bfloat16)
    grad_q = (d_float * mixed_out).astype(jnp.bfloat16)
    grad_k = (grad_values * x_float).astype(jnp.bfloat16)

    norm_scale = 1.0 / math.sqrt(all_channels * seq_total)
    grad_skip = skip_sum[:, 0] / math.sqrt(seq_total)
    grad_residue = gain * res_sum[0] * norm_scale
    grad_memory = residue * gain * mem_sum[0] * norm_scale
    return (output, grad_x, grad_q, grad_k, grad_skip, grad_residue, grad_memory)


def solution(mesh):
    return jax.shard_map(
        per_device,
        mesh=mesh,
        in_specs=(
            P("ch", "seq"),
            P("ch", "seq"),
            P("ch", "seq"),
            P("ch"),
            P(),
            P(),
            P("ch", "seq"),
        ),
        out_specs=(
            P("ch", "seq"),
            P("ch", "seq"),
            P("ch", "seq"),
            P("ch", "seq"),
            P("ch"),
            P(),
            P(),
        ),
        check_vma=False,
    )
```

```python
import functools
import math

import jax
import jax.numpy as jnp
from jax import lax
from jax.experimental import pallas as pl
from jax.experimental.pallas import tpu as pltpu
from jax.sharding import PartitionSpec as P

HIGH_PREC = lax.Precision.HIGHEST


def mm(pattern, left_op, right_op):
    return jnp.einsum(pattern, left_op, right_op, precision=HIGH_PREC)


GROUP = 8
LANES = 128
SLABS = 8


def row_sum(value):
    return jnp.sum(value, axis=0, keepdims=True)


def slab_coefs(count, size, pos, inv, block_len, modes):
    lane = lax.broadcasted_iota(jnp.int32, (count, LANES), 1) // modes
    index = lax.broadcasted_iota(jnp.int32, (count, LANES), 0)
    span = float(size * block_len)
    step = jnp.exp(-span * inv)
    starts = index.astype(jnp.float32) * span
    lag = jnp.exp(-starts * inv)
    before = jnp.where(index < pos, jnp.exp(-((pos - 1 - index).astype(jnp.float32) * span) * inv), 0.0)
    after = jnp.where(index > pos, jnp.exp(-((index - pos - 1).astype(jnp.float32) * span) * inv), 0.0)
    keep = jnp.where(lane <= 1, step, 1.0)[0:1]
    carry = jnp.where(lane == 1, step * span, 0.0)[0:1]
    take = jnp.where((lane >= 2) & (lane <= 4), lag, 1.0)
    shift = jnp.where(lane == 4, lag * starts * inv, 0.0)
    edge = jnp.where(lane == 0, before, jnp.where(lane == 2, after, 0.0))
    return keep, carry, take, shift, edge


def fold_items(items, coefs, inv, modes):
    keep, carry, take, shift, edge_c = coefs
    lane = lax.broadcasted_iota(jnp.int32, (1, LANES), 1) // modes
    acc = items[0]
    edge = edge_c[0:1] * acc
    for index in range(1, len(items)):
        item = items[index]
        s1 = row_sum(pltpu.roll(acc, 3 * modes, 1) * item)
        s2 = row_sum(pltpu.roll(acc, 4 * modes, 1) * item)
        s3 = row_sum(pltpu.roll(acc, 2 * modes, 1) * item)
        cross = jnp.where(lane == 5, pltpu.roll(s1, 2 * modes, 1), 0.0) + jnp.where(
            lane == 6, pltpu.roll(s2, 2 * modes, 1) + pltpu.roll(s3 * inv, 3 * modes, 1), 0.0)
        acc = (keep * acc + take[index:index + 1] * item + carry * pltpu.roll(acc, modes, 1)
               + shift[index:index + 1] * pltpu.roll(item, modes, 1) + cross)
        edge = edge + edge_c[index:index + 1] * item
    return acc, edge


def gather_ring(buf, send_sems, recv_sems, count, pos, device_of):
    descs = []
    for dist in range(1, count):
        desc = pltpu.make_async_remote_copy(
            src_ref=buf.at[0],
            dst_ref=buf.at[count - dist],
            send_sem=send_sems.at[dist],
            recv_sem=recv_sems.at[count - dist],
            device_id=device_of((pos + dist) % count),
            device_id_type=pl.DeviceIdType.MESH,
        )
        desc.start()
        descs.append(desc)
    for desc in descs:
        desc.wait_recv()
    for desc in descs:
        desc.wait_send()
    return [buf[(slot - pos + count) % count] for slot in range(count)]


def combine_kernel(counts, modes, block_len, state_ref, inv_ref, out_ref,
                   buf_a, buf_b, buf_c, send_a, recv_a, send_b, recv_b, send_c, recv_c):
    count_a, count_b, count_c = counts
    seq_index = lax.axis_index("seq")
    ch_index = lax.axis_index("ch")
    pos_a = seq_index % count_a
    pos_b = seq_index // count_a

    def dev_a(other):
        return (pos_b * count_a + other, ch_index)

    def dev_b(other):
        return (other * count_a + pos_a, ch_index)

    def dev_c(other):
        return (seq_index, other)

    barrier = pltpu.get_barrier_semaphore()
    for count, pos, device_of in ((count_a, pos_a, dev_a), (count_b, pos_b, dev_b), (count_c, ch_index, dev_c)):
        for dist in range(1, count):
            pl.semaphore_signal(barrier, inc=1, device_id=device_of((pos + dist) % count),
                                device_id_type=pl.DeviceIdType.MESH)

    buf_a[0] = state_ref[...]
    inv = inv_ref[...][0:1]
    coefs_a = slab_coefs(count_a, 1, pos_a, inv, block_len, modes)
    coefs_b = slab_coefs(count_b, count_a, pos_b, inv, block_len, modes)
    lane = lax.broadcasted_iota(jnp.int32, (1, LANES), 1) // modes
    near = jnp.exp(-(pos_a * block_len).astype(jnp.float32) * inv)
    far = jnp.exp(-((count_a - 1 - pos_a) * block_len).astype(jnp.float32) * inv)
    join = jnp.where(lane == 0, near, jnp.where(lane == 2, far, 0.0))
    pl.semaphore_wait(barrier, count_a + count_b + count_c - 3)

    items = gather_ring(buf_a, send_a, recv_a, count_a, pos_a, dev_a)
    group, edge_a = fold_items(items, coefs_a, inv, modes)
    buf_b[0] = group
    items = gather_ring(buf_b, send_b, recv_b, count_b, pos_b, dev_b)
    total, edge_b = fold_items(items, coefs_b, inv, modes)
    buf_c[0] = total
    items = gather_ring(buf_c, send_c, recv_c, count_c, ch_index, dev_c)
    sums = items[0]
    for item in items[1:]:
        sums = sums + item
    out_ref[0] = join * edge_b + edge_a
    out_ref[1] = total
    out_ref[2] = sums


def combine_states(state, inv_m, block_len):
    channels = state.shape[0]
    modes = inv_m.shape[0]
    count_a = min(GROUP, lax.axis_size("seq"))
    count_b = lax.axis_size("seq") // count_a
    count_c = lax.axis_size("ch")
    inv = jnp.broadcast_to(jnp.tile(inv_m, LANES // modes)[None, :], (8, LANES))
    msg = (channels, LANES)
    vmem = pl.BlockSpec(memory_space=pltpu.VMEM)
    return pl.pallas_call(
        functools.partial(combine_kernel, (count_a, count_b, count_c), modes, block_len),
        out_shape=jax.ShapeDtypeStruct((3,) + msg, jnp.float32),
        in_specs=[vmem, vmem],
        out_specs=vmem,
        scratch_shapes=[
            pltpu.VMEM((count_a,) + msg, jnp.float32),
            pltpu.VMEM((count_b,) + msg, jnp.float32),
            pltpu.VMEM((count_c,) + msg, jnp.float32),
            pltpu.SemaphoreType.DMA((count_a,)),
            pltpu.SemaphoreType.DMA((count_a,)),
            pltpu.SemaphoreType.DMA((count_b,)),
            pltpu.SemaphoreType.DMA((count_b,)),
            pltpu.SemaphoreType.DMA((count_c,)),
            pltpu.SemaphoreType.DMA((count_c,)),
        ],
        compiler_params=pltpu.CompilerParams(collective_id=0, has_side_effects=True),
    )(state, inv)


def finish_kernel(x_ref, q_ref, k_ref, d_ref, gain_ref, toep_ref, into_ref, edge_ref,
                  out_ref, gx_ref, gq_ref, gk_ref):
    x_float = x_ref[...].astype(jnp.float32)
    q_float = q_ref[...].astype(jnp.float32)
    k_float = k_ref[...].astype(jnp.float32)
    d_float = d_ref[...].astype(jnp.float32)
    values = x_float * k_float
    grad_mixed = d_float * q_float
    toep = toep_ref[...]
    edge = edge_ref[...]
    conv = lax.dot_general(values, toep, (((1,), (1,)), ((), ())), precision=HIGH_PREC,
                           preferred_element_type=jnp.float32)
    conv = conv + jnp.dot(edge, into_ref[0], precision=HIGH_PREC, preferred_element_type=jnp.float32)
    corr = jnp.dot(grad_mixed, toep, precision=HIGH_PREC, preferred_element_type=jnp.float32)
    corr = corr + jnp.dot(edge, into_ref[1], precision=HIGH_PREC, preferred_element_type=jnp.float32)
    gain = gain_ref[...]
    mixed_out = conv + gain * values
    grad_values = gain * grad_mixed + corr
    out_ref[...] = (q_float * mixed_out).astype(jnp.bfloat16)
    gx_ref[...] = (grad_values * k_float).astype(jnp.bfloat16)
    gq_ref[...] = (d_float * mixed_out).astype(jnp.bfloat16)
    gk_ref[...] = (grad_values * x_float).astype(jnp.bfloat16)


def finish(signal_x, gate_q, gate_k, cotangent, skip_gain, toeplitz, into, edge):
    vmem = pl.BlockSpec(memory_space=pltpu.VMEM)
    half = jax.ShapeDtypeStruct(signal_x.shape, jnp.bfloat16)
    return pl.pallas_call(
        finish_kernel,
        out_shape=(half, half, half, half),
        in_specs=[vmem] * 8,
        out_specs=(vmem, vmem, vmem, vmem),
    )(signal_x, gate_q, gate_k, cotangent, skip_gain[:, None], toeplitz, into, edge)


def per_device(signal_x, gate_q, gate_k, skip_gain, residue, memory, cotangent):
    channels, block_len = signal_x.shape
    modes = memory.shape[0]
    seq_total = lax.axis_size("seq") * block_len
    all_channels = channels * lax.axis_size("ch")
    inv_m = 1.0 / memory
    gain = jnp.sqrt(2.0 / memory)
    amp = residue * gain
    offs = jnp.arange(block_len, dtype=jnp.float32)[:, None]
    e_down = jnp.exp(-offs * inv_m)
    e_up = jnp.exp(offs * inv_m)
    e_tail = jnp.exp(-(block_len - 1 - offs) * inv_m)
    e_next = jnp.exp(-(offs + 1) * inv_m)
    e_in = jnp.exp(-(block_len - offs) * inv_m)
    lower = offs >= offs.T
    toeplitz = jnp.where(lower, mm("tn,sn->ts", e_down * amp, e_up), 0.0)
    pad = jnp.zeros((block_len, LANES - 5 * modes), jnp.float32)
    right_v = jnp.concatenate([e_tail, e_tail * (block_len - 1 - offs), jnp.zeros((block_len, 3 * modes)), pad], axis=1)
    right_g = jnp.concatenate([jnp.zeros((block_len, 2 * modes)), e_down, e_next,
                               e_next * ((offs + 1) * inv_m - 0.5), pad], axis=1)
    zero_rows = jnp.zeros((2 * modes, block_len), jnp.float32)
    fill = jnp.zeros((LANES - 3 * modes, block_len), jnp.float32)
    into = jnp.stack([
        jnp.concatenate([(e_next * amp).T, zero_rows, fill], axis=0),
        jnp.concatenate([zero_rows, (e_in * amp).T, fill], axis=0),
    ])

    values = signal_x.astype(jnp.float32) * gate_k.astype(jnp.float32)
    grad_mixed = cotangent.astype(jnp.float32) * gate_q.astype(jnp.float32)
    pair = jnp.where(lower, mm("ct,cs->ts", grad_mixed, values), 0.0)
    near = mm("ts,sn->tn", pair, e_up)
    near_m = mm("ts,sn->tn", pair, e_up * offs * inv_m)
    local_res = jnp.sum(e_down * near, axis=0)
    local_mem = jnp.sum(e_down * ((offs * inv_m - 0.5) * near - near_m), axis=0)
    part_skip = jnp.sum(grad_mixed * values, axis=1)
    lane = jnp.arange(LANES, dtype=jnp.int32)[None, :]
    extra = jnp.concatenate([jnp.zeros((5 * modes,)), local_res, local_mem, jnp.zeros((LANES - 7 * modes,))])
    state = mm("cs,sl->cl", values, right_v) + mm("ct,tl->cl", grad_mixed, right_g)
    state = state + jnp.where(lane >= 7 * modes, part_skip[:, None], extra[None, :])
    out = combine_states(state, inv_m, block_len)
    edge, total, sums = out[0], out[1], out[2]

    output, grad_x, grad_q, grad_k = finish(signal_x, gate_q, gate_k, cotangent, skip_gain, toeplitz, into, edge)

    norm_scale = 1.0 / math.sqrt(all_channels * seq_total)
    grad_skip = total[:, 7 * modes] / math.sqrt(seq_total)
    grad_residue = gain * sums[0, 5 * modes:6 * modes] * norm_scale
    grad_memory = residue * gain * sums[0, 6 * modes:7 * modes] * norm_scale
    return (output, grad_x, grad_q, grad_k, grad_skip, grad_residue, grad_memory)


def solution(mesh):
    return jax.shard_map(
        per_device,
        mesh=mesh,
        in_specs=(
            P("ch", "seq"),
            P("ch", "seq"),
            P("ch", "seq"),
            P("ch"),
            P(),
            P(),
            P("ch", "seq"),
        ),
        out_specs=(
            P("ch", "seq"),
            P("ch", "seq"),
            P("ch", "seq"),
            P("ch", "seq"),
            P("ch"),
            P(),
            P(),
        ),
        check_vma=False,
    )
```

```python
import functools
import math

import jax
import jax.numpy as jnp
from jax import lax
from jax.experimental import pallas as pl
from jax.experimental.pallas import tpu as pltpu
from jax.sharding import PartitionSpec as P

HIGH_PREC = lax.Precision.HIGHEST


def mm(pattern, left_op, right_op):
    return jnp.einsum(pattern, left_op, right_op, precision=HIGH_PREC)


GROUP = 8
LANES = 128
SLABS = 8


def row_sum(value):
    return jnp.sum(value, axis=0, keepdims=True)


def slab_coefs(count, size, pos, inv, block_len, modes):
    lane = lax.broadcasted_iota(jnp.int32, (count, LANES), 1) // modes
    index = lax.broadcasted_iota(jnp.int32, (count, LANES), 0)
    span = float(size * block_len)
    step = jnp.exp(-span * inv)
    starts = index.astype(jnp.float32) * span
    lag = jnp.exp(-starts * inv)
    before = jnp.where(index < pos, jnp.exp(-((pos - 1 - index).astype(jnp.float32) * span) * inv), 0.0)
    after = jnp.where(index > pos, jnp.exp(-((index - pos - 1).astype(jnp.float32) * span) * inv), 0.0)
    keep = jnp.where(lane <= 1, step, 1.0)[0:1]
    carry = jnp.where(lane == 1, step * span, 0.0)[0:1]
    take = jnp.where((lane >= 2) & (lane <= 4), lag, 1.0)
    shift = jnp.where(lane == 4, lag * starts * inv, 0.0)
    edge = jnp.where(lane == 0, before, jnp.where(lane == 2, after, 0.0))
    return keep, carry, take, shift, edge


def fold_items(items, coefs, inv, modes):
    keep, carry, take, shift, edge_c = coefs
    lane = lax.broadcasted_iota(jnp.int32, (1, LANES), 1) // modes
    acc = items[0]
    edge = edge_c[0:1] * acc
    for index in range(1, len(items)):
        item = items[index]
        s1 = row_sum(pltpu.roll(acc, 3 * modes, 1) * item)
        s2 = row_sum(pltpu.roll(acc, 4 * modes, 1) * item)
        s3 = row_sum(pltpu.roll(acc, 2 * modes, 1) * item)
        cross = jnp.where(lane == 5, pltpu.roll(s1, 2 * modes, 1), 0.0) + jnp.where(
            lane == 6, pltpu.roll(s2, 2 * modes, 1) + pltpu.roll(s3 * inv, 3 * modes, 1), 0.0)
        acc = (keep * acc + take[index:index + 1] * item + carry * pltpu.roll(acc, modes, 1)
               + shift[index:index + 1] * pltpu.roll(item, modes, 1) + cross)
        edge = edge + edge_c[index:index + 1] * item
    return acc, edge


def start_ring(buf, send_sems, recv_sems, count, pos, device_of):
    descs = []
    for dist in range(1, count):
        desc = pltpu.make_async_remote_copy(
            src_ref=buf.at[0],
            dst_ref=buf.at[count - dist],
            send_sem=send_sems.at[dist],
            recv_sem=recv_sems.at[count - dist],
            device_id=device_of((pos + dist) % count),
            device_id_type=pl.DeviceIdType.MESH,
        )
        desc.start()
        descs.append(desc)
    return descs


def finish_ring(descs, buf, count, pos):
    for desc in descs:
        desc.wait_recv()
    for desc in descs:
        desc.wait_send()
    return [buf[(slot - pos + count) % count] for slot in range(count)]


def dot_nn(left_op, right_op):
    return jnp.dot(left_op, right_op, precision=HIGH_PREC, preferred_element_type=jnp.float32)


def dot_nt(left_op, right_op):
    return lax.dot_general(left_op, right_op, (((1,), (1,)), ((), ())), precision=HIGH_PREC,
                           preferred_element_type=jnp.float32)


def dot_tn(left_op, right_op):
    return lax.dot_general(left_op, right_op, (((0,), (0,)), ((), ())), precision=HIGH_PREC,
                           preferred_element_type=jnp.float32)


def fused_kernel(counts, modes, x_ref, q_ref, k_ref, d_ref, par_ref,
                 out_ref, gx_ref, gq_ref, gk_ref, small_ref,
                 buf_a, buf_b, buf_c, send_a, recv_a, send_b, recv_b, send_c, recv_c):
    count_a, count_b, count_c = counts
    channels, block_len = x_ref.shape
    seq_index = lax.axis_index("seq")
    ch_index = lax.axis_index("ch")
    pos_a = seq_index % count_a
    pos_b = seq_index // count_a

    def dev_a(other):
        return (pos_b * count_a + other, ch_index)

    def dev_b(other):
        return (other * count_a + pos_a, ch_index)

    def dev_c(other):
        return (seq_index, other)

    barrier = pltpu.get_barrier_semaphore()
    for count, pos, device_of in ((count_a, pos_a, dev_a), (count_b, pos_b, dev_b), (count_c, ch_index, dev_c)):
        for dist in range(1, count):
            pl.semaphore_signal(barrier, inc=1, device_id=device_of((pos + dist) % count),
                                device_id_type=pl.DeviceIdType.MESH)

    par = par_ref[...]
    inv = par[0:1]
    amp = par[1:2]
    gain = par[8:8 + channels, 0:1]
    slab = lax.broadcasted_iota(jnp.int32, (1, LANES), 1) // modes
    offs = lax.broadcasted_iota(jnp.int32, (block_len, LANES), 0).astype(jnp.float32)
    back = float(block_len - 1) - offs
    e_down = jnp.exp(-offs * inv)
    e_tail = jnp.exp(-back * inv)
    e_next = jnp.exp(-(offs + 1.0) * inv)
    e_up = jnp.exp(offs * inv)
    right_v = jnp.where(slab == 0, e_tail, jnp.where(slab == 1, e_tail * back, 0.0))
    right_g = jnp.where(slab == 2, e_down, jnp.where(slab == 3, e_next, jnp.where(
        slab == 4, e_next * ((offs + 1.0) * inv - 0.5), 0.0)))
    right_r = jnp.where(slab == 5, e_up, jnp.where(slab == 6, e_up * offs * inv, 0.0))

    x_float = x_ref[...].astype(jnp.float32)
    q_float = q_ref[...].astype(jnp.float32)
    k_float = k_ref[...].astype(jnp.float32)
    d_float = d_ref[...].astype(jnp.float32)
    values = x_float * k_float
    grad_mixed = d_float * q_float
    row_t = lax.broadcasted_iota(jnp.int32, (block_len, block_len), 0)
    col_s = lax.broadcasted_iota(jnp.int32, (block_len, block_len), 1)
    lower = row_t >= col_s
    pair = jnp.where(lower, dot_tn(grad_mixed, values), 0.0)
    near = dot_nn(pair, right_r)
    terms = jnp.where(slab == 5, e_down * near, jnp.where(
        slab == 6, e_down * ((offs * inv - 0.5) * pltpu.roll(near, modes, 1) - near), 0.0))
    local = row_sum(terms)
    skip = jnp.sum(grad_mixed * values, axis=1, keepdims=True)
    state = dot_nn(values, right_v) + dot_nn(grad_mixed, right_g) + jnp.where(slab == 7, skip, local)
    buf_a[0] = state
    coefs_a = slab_coefs(count_a, 1, pos_a, inv, block_len, modes)
    coefs_b = slab_coefs(count_b, count_a, pos_b, inv, block_len, modes)
    near_w = jnp.exp(-(pos_a * block_len).astype(jnp.float32) * inv)
    far_w = jnp.exp(-((count_a - 1 - pos_a) * block_len).astype(jnp.float32) * inv)
    join = jnp.where(slab == 0, near_w, jnp.where(slab == 2, far_w, 0.0))
    pl.semaphore_wait(barrier, count_a + count_b + count_c - 3)

    descs = start_ring(buf_a, send_a, recv_a, count_a, pos_a, dev_a)
    toep = jnp.where(lower, dot_nt(jnp.where(slab == 0, e_down * amp, 0.0), jnp.where(slab == 0, e_up, 0.0)), 0.0)
    conv = dot_nt(values, toep)
    corr = dot_nn(grad_mixed, toep)
    into_f = jnp.where(slab == 0, e_next * amp, 0.0)
    into_b = jnp.where(slab == 2, jnp.exp(-(float(block_len) - offs) * inv) * amp, 0.0)
    items = finish_ring(descs, buf_a, count_a, pos_a)
    group, edge_a = fold_items(items, coefs_a, inv, modes)
    buf_b[0] = group
    descs = start_ring(buf_b, send_b, recv_b, count_b, pos_b, dev_b)
    items = finish_ring(descs, buf_b, count_b, pos_b)
    total, edge_b = fold_items(items, coefs_b, inv, modes)
    buf_c[0] = total
    descs = start_ring(buf_c, send_c, recv_c, count_c, ch_index, dev_c)
    edge = join * edge_b + edge_a
    conv = conv + dot_nt(edge, into_f)
    corr = corr + dot_nt(edge, into_b)
    mixed_out = conv + gain * values
    grad_values = gain * grad_mixed + corr
    out_ref[...] = (q_float * mixed_out).astype(jnp.bfloat16)
    gx_ref[...] = (grad_values * k_float).astype(jnp.bfloat16)
    gq_ref[...] = (d_float * mixed_out).astype(jnp.bfloat16)
    gk_ref[...] = (grad_values * x_float).astype(jnp.bfloat16)
    items = finish_ring(descs, buf_c, count_c, ch_index)
    sums = items[0]
    for item in items[1:]:
        sums = sums + item
    small_ref[0] = total
    small_ref[1] = sums


def per_device(signal_x, gate_q, gate_k, skip_gain, residue, memory, cotangent):
    channels, block_len = signal_x.shape
    modes = memory.shape[0]
    seq_total = lax.axis_size("seq") * block_len
    all_channels = channels * lax.axis_size("ch")
    count_a = min(GROUP, lax.axis_size("seq"))
    count_b = lax.axis_size("seq") // count_a
    count_c = lax.axis_size("ch")
    inv_m = 1.0 / memory
    gain = jnp.sqrt(2.0 / memory)
    amp = residue * gain
    reps = LANES // modes
    par = jnp.concatenate([
        jnp.tile(inv_m, reps)[None, :],
        jnp.tile(amp, reps)[None, :],
        jnp.zeros((6, LANES), jnp.float32),
        jnp.broadcast_to(skip_gain[:, None], (channels, LANES)),
    ], axis=0)
    msg = (channels, LANES)
    vmem = pl.BlockSpec(memory_space=pltpu.VMEM)
    half = jax.ShapeDtypeStruct(signal_x.shape, jnp.bfloat16)
    output, grad_x, grad_q, grad_k, small = pl.pallas_call(
        functools.partial(fused_kernel, (count_a, count_b, count_c), modes),
        out_shape=(half, half, half, half, jax.ShapeDtypeStruct((2,) + msg, jnp.float32)),
        in_specs=[vmem] * 5,
        out_specs=(vmem,) * 5,
        scratch_shapes=[
            pltpu.VMEM((count_a,) + msg, jnp.float32),
            pltpu.VMEM((count_b,) + msg, jnp.float32),
            pltpu.VMEM((count_c,) + msg, jnp.float32),
            pltpu.SemaphoreType.DMA((count_a,)),
            pltpu.SemaphoreType.DMA((count_a,)),
            pltpu.SemaphoreType.DMA((count_b,)),
            pltpu.SemaphoreType.DMA((count_b,)),
            pltpu.SemaphoreType.DMA((count_c,)),
            pltpu.SemaphoreType.DMA((count_c,)),
        ],
        compiler_params=pltpu.CompilerParams(collective_id=0, has_side_effects=True),
    )(signal_x, gate_q, gate_k, cotangent, par)
    total, sums = small[0], small[1]
    norm_scale = 1.0 / math.sqrt(all_channels * seq_total)
    grad_skip = total[:, 7 * modes] / math.sqrt(seq_total)
    grad_residue = gain * sums[0, 5 * modes:6 * modes] * norm_scale
    grad_memory = residue * gain * sums[0, 6 * modes:7 * modes] * norm_scale
    return (output, grad_x, grad_q, grad_k, grad_skip, grad_residue, grad_memory)


def solution(mesh):
    return jax.shard_map(
        per_device,
        mesh=mesh,
        in_specs=(
            P("ch", "seq"),
            P("ch", "seq"),
            P("ch", "seq"),
            P("ch"),
            P(),
            P(),
            P("ch", "seq"),
        ),
        out_specs=(
            P("ch", "seq"),
            P("ch", "seq"),
            P("ch", "seq"),
            P("ch", "seq"),
            P("ch"),
            P(),
            P(),
        ),
        check_vma=False,
    )
```

```python
import functools
import math

import jax
import jax.numpy as jnp
from jax import lax
from jax.experimental import pallas as pl
from jax.experimental.pallas import tpu as pltpu
from jax.sharding import PartitionSpec as P

HIGH_PREC = lax.Precision.HIGHEST


def mm(pattern, left_op, right_op):
    return jnp.einsum(pattern, left_op, right_op, precision=HIGH_PREC)


GROUP = 8
LANES = 128
SLABS = 8


def row_sum(value):
    return jnp.sum(value, axis=0, keepdims=True)


def slab_coefs(count, size, pos, inv, block_len, modes):
    lane = lax.broadcasted_iota(jnp.int32, (count, LANES), 1) // modes
    index = lax.broadcasted_iota(jnp.int32, (count, LANES), 0)
    span = float(size * block_len)
    step = jnp.exp(-span * inv)
    starts = index.astype(jnp.float32) * span
    lag = jnp.exp(-starts * inv)
    before = jnp.where(index < pos, jnp.exp(-((pos - 1 - index).astype(jnp.float32) * span) * inv), 0.0)
    after = jnp.where(index > pos, jnp.exp(-((index - pos - 1).astype(jnp.float32) * span) * inv), 0.0)
    keep = jnp.where(lane <= 1, step, 1.0)[0:1]
    carry = jnp.where(lane == 1, step * span, 0.0)[0:1]
    take = jnp.where((lane >= 2) & (lane <= 4), lag, 1.0)
    shift = jnp.where(lane == 4, lag * starts * inv, 0.0)
    edge = jnp.where(lane == 0, before, jnp.where(lane == 2, after, 0.0))
    return keep, carry, take, shift, edge


def level_coefs(count, size, inv, block_len, modes):
    slab = lax.broadcasted_iota(jnp.int32, (1, LANES), 1) // modes
    levels = []
    width = size
    while width < count * size:
        span = float(width * block_len)
        step = jnp.exp(-span * inv)
        levels.append((
            jnp.where(slab <= 1, step, 1.0),
            jnp.where(slab == 1, step * span, 0.0),
            jnp.where((slab >= 2) & (slab <= 4), step, 1.0),
            jnp.where(slab == 4, step * span * inv, 0.0),
        ))
        width *= 2
    return levels


def combine_pair(left, right, coefs, inv, modes):
    keep, carry, take, shift = coefs
    slab = lax.broadcasted_iota(jnp.int32, (1, LANES), 1) // modes
    s1 = row_sum(pltpu.roll(left, 3 * modes, 1) * right)
    s2 = row_sum(pltpu.roll(left, 4 * modes, 1) * right)
    s3 = row_sum(pltpu.roll(left, 2 * modes, 1) * right)
    cross = jnp.where(slab == 5, pltpu.roll(s1, 2 * modes, 1), 0.0) + jnp.where(
        slab == 6, pltpu.roll(s2, 2 * modes, 1) + pltpu.roll(s3 * inv, 3 * modes, 1), 0.0)
    return (keep * left + take * right + carry * pltpu.roll(left, modes, 1)
            + shift * pltpu.roll(right, modes, 1) + cross)


def fold_items(items, levels, edge_c, inv, modes):
    edge = edge_c[0:1] * items[0]
    for index in range(1, len(items)):
        edge = edge + edge_c[index:index + 1] * items[index]
    layer = list(items)
    for coefs in levels:
        layer = [combine_pair(layer[i], layer[i + 1], coefs, inv, modes) for i in range(0, len(layer), 2)]
    return layer[0], edge


def start_ring(buf, send_sems, recv_sems, count, pos, device_of):
    descs = []
    for dist in range(1, count):
        desc = pltpu.make_async_remote_copy(
            src_ref=buf.at[0],
            dst_ref=buf.at[count - dist],
            send_sem=send_sems.at[dist],
            recv_sem=recv_sems.at[count - dist],
            device_id=device_of((pos + dist) % count),
            device_id_type=pl.DeviceIdType.MESH,
        )
        desc.start()
        descs.append(desc)
    return descs


def finish_ring(descs, buf, count, pos):
    for desc in descs:
        desc.wait_recv()
    for desc in descs:
        desc.wait_send()
    return [buf[(slot - pos + count) % count] for slot in range(count)]


def dot_nn(left_op, right_op):
    return jnp.dot(left_op, right_op, precision=HIGH_PREC, preferred_element_type=jnp.float32)


def dot_nt(left_op, right_op):
    return lax.dot_general(left_op, right_op, (((1,), (1,)), ((), ())), precision=HIGH_PREC,
                           preferred_element_type=jnp.float32)


def dot_tn(left_op, right_op):
    return lax.dot_general(left_op, right_op, (((0,), (0,)), ((), ())), precision=HIGH_PREC,
                           preferred_element_type=jnp.float32)


def fused_kernel(counts, modes, x_ref, q_ref, k_ref, d_ref, par_ref,
                 out_ref, gx_ref, gq_ref, gk_ref, small_ref,
                 buf_a, buf_b, buf_c, send_a, recv_a, send_b, recv_b, send_c, recv_c):
    count_a, count_b, count_c = counts
    channels, block_len = x_ref.shape
    seq_index = lax.axis_index("seq")
    ch_index = lax.axis_index("ch")
    pos_a = seq_index % count_a
    pos_b = seq_index // count_a

    def dev_a(other):
        return (pos_b * count_a + other, ch_index)

    def dev_b(other):
        return (other * count_a + pos_a, ch_index)

    def dev_c(other):
        return (seq_index, other)

    barrier = pltpu.get_barrier_semaphore()
    for count, pos, device_of in ((count_a, pos_a, dev_a), (count_b, pos_b, dev_b), (count_c, ch_index, dev_c)):
        for dist in range(1, count):
            pl.semaphore_signal(barrier, inc=1, device_id=device_of((pos + dist) % count),
                                device_id_type=pl.DeviceIdType.MESH)

    par = par_ref[...]
    inv = par[0:1]
    amp = par[1:2]
    gain = par[8:8 + channels, 0:1]
    slab = lax.broadcasted_iota(jnp.int32, (1, LANES), 1) // modes
    offs = lax.broadcasted_iota(jnp.int32, (block_len, LANES), 0).astype(jnp.float32)
    back = float(block_len - 1) - offs
    e_down = jnp.exp(-offs * inv)
    e_tail = jnp.exp(-back * inv)
    e_next = jnp.exp(-(offs + 1.0) * inv)
    e_up = jnp.exp(offs * inv)
    right_v = jnp.where(slab == 0, e_tail, jnp.where(slab == 1, e_tail * back, 0.0))
    right_g = jnp.where(slab == 2, e_down, jnp.where(slab == 3, e_next, jnp.where(
        slab == 4, e_next * ((offs + 1.0) * inv - 0.5), 0.0)))
    right_r = jnp.where(slab == 5, e_up, jnp.where(slab == 6, e_up * offs * inv, 0.0))

    x_float = x_ref[...].astype(jnp.float32)
    q_float = q_ref[...].astype(jnp.float32)
    k_float = k_ref[...].astype(jnp.float32)
    d_float = d_ref[...].astype(jnp.float32)
    values = x_float * k_float
    grad_mixed = d_float * q_float
    row_t = lax.broadcasted_iota(jnp.int32, (block_len, block_len), 0)
    col_s = lax.broadcasted_iota(jnp.int32, (block_len, block_len), 1)
    lower = row_t >= col_s
    pair = jnp.where(lower, dot_tn(grad_mixed, values), 0.0)
    near = dot_nn(pair, right_r)
    terms = jnp.where(slab == 5, e_down * near, jnp.where(
        slab == 6, e_down * ((offs * inv - 0.5) * pltpu.roll(near, modes, 1) - near), 0.0))
    local = row_sum(terms)
    skip = jnp.sum(grad_mixed * values, axis=1, keepdims=True)
    state = dot_nn(values, right_v) + dot_nn(grad_mixed, right_g) + jnp.where(slab == 7, skip, local)
    buf_a[0] = state
    edge_a_c = slab_coefs(count_a, 1, pos_a, inv, block_len, modes)[4]
    edge_b_c = slab_coefs(count_b, count_a, pos_b, inv, block_len, modes)[4]
    levels_a = level_coefs(count_a, 1, inv, block_len, modes)
    levels_b = level_coefs(count_b, count_a, inv, block_len, modes)
    near_w = jnp.exp(-(pos_a * block_len).astype(jnp.float32) * inv)
    far_w = jnp.exp(-((count_a - 1 - pos_a) * block_len).astype(jnp.float32) * inv)
    join = jnp.where(slab == 0, near_w, jnp.where(slab == 2, far_w, 0.0))
    pl.semaphore_wait(barrier, count_a + count_b + count_c - 3)

    descs = start_ring(buf_a, send_a, recv_a, count_a, pos_a, dev_a)
    toep = jnp.where(lower, dot_nt(jnp.where(slab == 0, e_down * amp, 0.0), jnp.where(slab == 0, e_up, 0.0)), 0.0)
    conv = dot_nt(values, toep)
    corr = dot_nn(grad_mixed, toep)
    into_f = jnp.where(slab == 0, e_next * amp, 0.0)
    into_b = jnp.where(slab == 2, jnp.exp(-(float(block_len) - offs) * inv) * amp, 0.0)
    items = finish_ring(descs, buf_a, count_a, pos_a)
    group, edge_a = fold_items(items, levels_a, edge_a_c, inv, modes)
    buf_b[0] = group
    descs = start_ring(buf_b, send_b, recv_b, count_b, pos_b, dev_b)
    items = finish_ring(descs, buf_b, count_b, pos_b)
    total, edge_b = fold_items(items, levels_b, edge_b_c, inv, modes)
    buf_c[0] = total
    descs = start_ring(buf_c, send_c, recv_c, count_c, ch_index, dev_c)
    edge = join * edge_b + edge_a
    conv = conv + dot_nt(edge, into_f)
    corr = corr + dot_nt(edge, into_b)
    mixed_out = conv + gain * values
    grad_values = gain * grad_mixed + corr
    out_ref[...] = (q_float * mixed_out).astype(jnp.bfloat16)
    gx_ref[...] = (grad_values * k_float).astype(jnp.bfloat16)
    gq_ref[...] = (d_float * mixed_out).astype(jnp.bfloat16)
    gk_ref[...] = (grad_values * x_float).astype(jnp.bfloat16)
    items = finish_ring(descs, buf_c, count_c, ch_index)
    sums = items[0]
    for item in items[1:]:
        sums = sums + item
    small_ref[0] = total
    small_ref[1] = sums


def per_device(signal_x, gate_q, gate_k, skip_gain, residue, memory, cotangent):
    channels, block_len = signal_x.shape
    modes = memory.shape[0]
    seq_total = lax.axis_size("seq") * block_len
    all_channels = channels * lax.axis_size("ch")
    count_a = min(GROUP, lax.axis_size("seq"))
    count_b = lax.axis_size("seq") // count_a
    count_c = lax.axis_size("ch")
    inv_m = 1.0 / memory
    gain = jnp.sqrt(2.0 / memory)
    amp = residue * gain
    reps = LANES // modes
    par = jnp.concatenate([
        jnp.tile(inv_m, reps)[None, :],
        jnp.tile(amp, reps)[None, :],
        jnp.zeros((6, LANES), jnp.float32),
        jnp.broadcast_to(skip_gain[:, None], (channels, LANES)),
    ], axis=0)
    msg = (channels, LANES)
    vmem = pl.BlockSpec(memory_space=pltpu.VMEM)
    half = jax.ShapeDtypeStruct(signal_x.shape, jnp.bfloat16)
    output, grad_x, grad_q, grad_k, small = pl.pallas_call(
        functools.partial(fused_kernel, (count_a, count_b, count_c), modes),
        out_shape=(half, half, half, half, jax.ShapeDtypeStruct((2,) + msg, jnp.float32)),
        in_specs=[vmem] * 5,
        out_specs=(vmem,) * 5,
        scratch_shapes=[
            pltpu.VMEM((count_a,) + msg, jnp.float32),
            pltpu.VMEM((count_b,) + msg, jnp.float32),
            pltpu.VMEM((count_c,) + msg, jnp.float32),
            pltpu.SemaphoreType.DMA((count_a,)),
            pltpu.SemaphoreType.DMA((count_a,)),
            pltpu.SemaphoreType.DMA((count_b,)),
            pltpu.SemaphoreType.DMA((count_b,)),
            pltpu.SemaphoreType.DMA((count_c,)),
            pltpu.SemaphoreType.DMA((count_c,)),
        ],
        compiler_params=pltpu.CompilerParams(collective_id=0, has_side_effects=True),
    )(signal_x, gate_q, gate_k, cotangent, par)
    total, sums = small[0], small[1]
    norm_scale = 1.0 / math.sqrt(all_channels * seq_total)
    grad_skip = total[:, 7 * modes] / math.sqrt(seq_total)
    grad_residue = gain * sums[0, 5 * modes:6 * modes] * norm_scale
    grad_memory = residue * gain * sums[0, 6 * modes:7 * modes] * norm_scale
    return (output, grad_x, grad_q, grad_k, grad_skip, grad_residue, grad_memory)


def solution(mesh):
    return jax.shard_map(
        per_device,
        mesh=mesh,
        in_specs=(
            P("ch", "seq"),
            P("ch", "seq"),
            P("ch", "seq"),
            P("ch"),
            P(),
            P(),
            P("ch", "seq"),
        ),
        out_specs=(
            P("ch", "seq"),
            P("ch", "seq"),
            P("ch", "seq"),
            P("ch", "seq"),
            P("ch"),
            P(),
            P(),
        ),
        check_vma=False,
    )
```

```python
import functools
import math

import jax
import jax.numpy as jnp
from jax import lax
from jax.experimental import pallas as pl
from jax.experimental.pallas import tpu as pltpu
from jax.sharding import PartitionSpec as P

HIGH_PREC = lax.Precision.HIGHEST


def mm(pattern, left_op, right_op):
    return jnp.einsum(pattern, left_op, right_op, precision=HIGH_PREC)


GROUP = 8
LANES = 128
SLABS = 8


def row_sum(value):
    return jnp.sum(value, axis=0, keepdims=True)


def slab_coefs(count, size, pos, inv, block_len, modes):
    lane = lax.broadcasted_iota(jnp.int32, (count, LANES), 1) // modes
    index = lax.broadcasted_iota(jnp.int32, (count, LANES), 0)
    span = float(size * block_len)
    step = jnp.exp(-span * inv)
    starts = index.astype(jnp.float32) * span
    lag = jnp.exp(-starts * inv)
    before = jnp.where(index < pos, jnp.exp(-((pos - 1 - index).astype(jnp.float32) * span) * inv), 0.0)
    after = jnp.where(index > pos, jnp.exp(-((index - pos - 1).astype(jnp.float32) * span) * inv), 0.0)
    keep = jnp.where(lane <= 1, step, 1.0)[0:1]
    carry = jnp.where(lane == 1, step * span, 0.0)[0:1]
    take = jnp.where((lane >= 2) & (lane <= 4), lag, 1.0)
    shift = jnp.where(lane == 4, lag * starts * inv, 0.0)
    edge = jnp.where(lane == 0, before, jnp.where(lane == 2, after, 0.0))
    return keep, carry, take, shift, edge


def level_coefs(count, size, inv, block_len, modes):
    slab = lax.broadcasted_iota(jnp.int32, (1, LANES), 1) // modes
    levels = []
    width = size
    while width < count * size:
        span = float(width * block_len)
        step = jnp.exp(-span * inv)
        levels.append((
            jnp.where(slab <= 1, step, 1.0),
            jnp.where(slab == 1, step * span, 0.0),
            jnp.where((slab >= 2) & (slab <= 4), step, 1.0),
            jnp.where(slab == 4, step * span * inv, 0.0),
        ))
        width *= 2
    return levels


def combine_pair(left, right, coefs, inv, modes):
    keep, carry, take, shift = coefs
    slab = lax.broadcasted_iota(jnp.int32, (1, LANES), 1) // modes
    s1 = row_sum(pltpu.roll(left, 3 * modes, 1) * right)
    s2 = row_sum(pltpu.roll(left, 4 * modes, 1) * right)
    s3 = row_sum(pltpu.roll(left, 2 * modes, 1) * right)
    cross = jnp.where(slab == 5, pltpu.roll(s1, 2 * modes, 1), 0.0) + jnp.where(
        slab == 6, pltpu.roll(s2, 2 * modes, 1) + pltpu.roll(s3 * inv, 3 * modes, 1), 0.0)
    return (keep * left + take * right + carry * pltpu.roll(left, modes, 1)
            + shift * pltpu.roll(right, modes, 1) + cross)


def fold_items(items, levels, edge_c, inv, modes):
    edge = edge_c[0:1] * items[0]
    for index in range(1, len(items)):
        edge = edge + edge_c[index:index + 1] * items[index]
    layer = list(items)
    for coefs in levels:
        layer = [combine_pair(layer[i], layer[i + 1], coefs, inv, modes) for i in range(0, len(layer), 2)]
    return layer[0], edge


def start_ring(buf, send_sems, recv_sems, count, pos, device_of):
    descs = []
    for dist in range(1, count):
        desc = pltpu.make_async_remote_copy(
            src_ref=buf.at[0],
            dst_ref=buf.at[count - dist],
            send_sem=send_sems.at[dist],
            recv_sem=recv_sems.at[count - dist],
            device_id=device_of((pos + dist) % count),
            device_id_type=pl.DeviceIdType.MESH,
        )
        desc.start()
        descs.append(desc)
    return descs


def finish_ring(descs, buf, count, pos):
    for desc in descs:
        desc.wait_recv()
    for desc in descs:
        desc.wait_send()
    return [buf[(slot - pos + count) % count] for slot in range(count)]


def dot_nn(left_op, right_op):
    return jnp.dot(left_op, right_op, precision=HIGH_PREC, preferred_element_type=jnp.float32)


def dot_nt(left_op, right_op):
    return lax.dot_general(left_op, right_op, (((1,), (1,)), ((), ())), precision=HIGH_PREC,
                           preferred_element_type=jnp.float32)


def dot_tn(left_op, right_op):
    return lax.dot_general(left_op, right_op, (((0,), (0,)), ((), ())), precision=HIGH_PREC,
                           preferred_element_type=jnp.float32)


def fused_kernel(counts, modes, x_ref, q_ref, k_ref, d_ref, mem_ref, res_ref, gain_ref,
                 out_ref, gx_ref, gq_ref, gk_ref, small_ref,
                 buf_a, buf_b, buf_c, send_a, recv_a, send_b, recv_b, send_c, recv_c):
    count_a, count_b, count_c = counts
    channels, block_len = x_ref.shape
    seq_index = lax.axis_index("seq")
    ch_index = lax.axis_index("ch")
    pos_a = seq_index % count_a
    pos_b = seq_index // count_a

    def dev_a(other):
        return (pos_b * count_a + other, ch_index)

    def dev_b(other):
        return (other * count_a + pos_a, ch_index)

    def dev_c(other):
        return (seq_index, other)

    barrier = pltpu.get_barrier_semaphore()
    for count, pos, device_of in ((count_a, pos_a, dev_a), (count_b, pos_b, dev_b), (count_c, ch_index, dev_c)):
        for dist in range(1, count):
            pl.semaphore_signal(barrier, inc=1, device_id=device_of((pos + dist) % count),
                                device_id_type=pl.DeviceIdType.MESH)

    slab = lax.broadcasted_iota(jnp.int32, (1, LANES), 1) // modes
    mode_of = lax.broadcasted_iota(jnp.int32, (1, LANES), 1) % modes
    mem_v = jnp.zeros((1, LANES), jnp.float32)
    res_v = jnp.zeros((1, LANES), jnp.float32)
    for mode in range(modes):
        mem_v = jnp.where(mode_of == mode, mem_ref[mode], mem_v)
        res_v = jnp.where(mode_of == mode, res_ref[mode], res_v)
    inv = 1.0 / mem_v
    amp = res_v * jnp.sqrt(2.0 * inv)
    chan_of = lax.broadcasted_iota(jnp.int32, (channels, 1), 0)
    gain = jnp.zeros((channels, 1), jnp.float32)
    for chan in range(channels):
        gain = jnp.where(chan_of == chan, gain_ref[chan], gain)
    offs = lax.broadcasted_iota(jnp.int32, (block_len, LANES), 0).astype(jnp.float32)
    back = float(block_len - 1) - offs
    e_down = jnp.exp(-offs * inv)
    e_tail = jnp.exp(-back * inv)
    e_next = jnp.exp(-(offs + 1.0) * inv)
    e_up = jnp.exp(offs * inv)
    right_v = jnp.where(slab == 0, e_tail, jnp.where(slab == 1, e_tail * back, 0.0))
    right_g = jnp.where(slab == 2, e_down, jnp.where(slab == 3, e_next, jnp.where(
        slab == 4, e_next * ((offs + 1.0) * inv - 0.5), 0.0)))
    right_r = jnp.where(slab == 5, e_up, jnp.where(slab == 6, e_up * offs * inv, 0.0))

    x_float = x_ref[...].astype(jnp.float32)
    q_float = q_ref[...].astype(jnp.float32)
    k_float = k_ref[...].astype(jnp.float32)
    d_float = d_ref[...].astype(jnp.float32)
    values = x_float * k_float
    grad_mixed = d_float * q_float
    row_t = lax.broadcasted_iota(jnp.int32, (block_len, block_len), 0)
    col_s = lax.broadcasted_iota(jnp.int32, (block_len, block_len), 1)
    lower = row_t >= col_s
    pair = jnp.where(lower, dot_tn(grad_mixed, values), 0.0)
    near = dot_nn(pair, right_r)
    terms = jnp.where(slab == 5, e_down * near, jnp.where(
        slab == 6, e_down * ((offs * inv - 0.5) * pltpu.roll(near, modes, 1) - near), 0.0))
    local = row_sum(terms)
    skip = jnp.sum(grad_mixed * values, axis=1, keepdims=True)
    state = dot_nn(values, right_v) + dot_nn(grad_mixed, right_g) + jnp.where(slab == 7, skip, local)
    buf_a[0] = state
    edge_a_c = slab_coefs(count_a, 1, pos_a, inv, block_len, modes)[4]
    edge_b_c = slab_coefs(count_b, count_a, pos_b, inv, block_len, modes)[4]
    levels_a = level_coefs(count_a, 1, inv, block_len, modes)
    levels_b = level_coefs(count_b, count_a, inv, block_len, modes)
    near_w = jnp.exp(-(pos_a * block_len).astype(jnp.float32) * inv)
    far_w = jnp.exp(-((count_a - 1 - pos_a) * block_len).astype(jnp.float32) * inv)
    join = jnp.where(slab == 0, near_w, jnp.where(slab == 2, far_w, 0.0))
    pl.semaphore_wait(barrier, count_a + count_b + count_c - 3)

    descs = start_ring(buf_a, send_a, recv_a, count_a, pos_a, dev_a)
    toep = jnp.where(lower, dot_nt(jnp.where(slab == 0, e_down * amp, 0.0), jnp.where(slab == 0, e_up, 0.0)), 0.0)
    conv = dot_nt(values, toep)
    corr = dot_nn(grad_mixed, toep)
    into_f = jnp.where(slab == 0, e_next * amp, 0.0)
    into_b = jnp.where(slab == 2, jnp.exp(-(float(block_len) - offs) * inv) * amp, 0.0)
    items = finish_ring(descs, buf_a, count_a, pos_a)
    group, edge_a = fold_items(items, levels_a, edge_a_c, inv, modes)
    buf_b[0] = group
    descs = start_ring(buf_b, send_b, recv_b, count_b, pos_b, dev_b)
    items = finish_ring(descs, buf_b, count_b, pos_b)
    total, edge_b = fold_items(items, levels_b, edge_b_c, inv, modes)
    buf_c[0] = total
    descs = start_ring(buf_c, send_c, recv_c, count_c, ch_index, dev_c)
    edge = join * edge_b + edge_a
    conv = conv + dot_nt(edge, into_f)
    corr = corr + dot_nt(edge, into_b)
    mixed_out = conv + gain * values
    grad_values = gain * grad_mixed + corr
    out_ref[...] = (q_float * mixed_out).astype(jnp.bfloat16)
    gx_ref[...] = (grad_values * k_float).astype(jnp.bfloat16)
    gq_ref[...] = (d_float * mixed_out).astype(jnp.bfloat16)
    gk_ref[...] = (grad_values * x_float).astype(jnp.bfloat16)
    items = finish_ring(descs, buf_c, count_c, ch_index)
    sums = items[0]
    for item in items[1:]:
        sums = sums + item
    small_ref[0] = total
    small_ref[1] = sums


def per_device(signal_x, gate_q, gate_k, skip_gain, residue, memory, cotangent):
    channels, block_len = signal_x.shape
    modes = memory.shape[0]
    seq_total = lax.axis_size("seq") * block_len
    all_channels = channels * lax.axis_size("ch")
    count_a = min(GROUP, lax.axis_size("seq"))
    count_b = lax.axis_size("seq") // count_a
    count_c = lax.axis_size("ch")
    inv_m = 1.0 / memory
    gain = jnp.sqrt(2.0 / memory)
    amp = residue * gain
    msg = (channels, LANES)
    vmem = pl.BlockSpec(memory_space=pltpu.VMEM)
    half = jax.ShapeDtypeStruct(signal_x.shape, jnp.bfloat16)
    output, grad_x, grad_q, grad_k, small = pl.pallas_call(
        functools.partial(fused_kernel, (count_a, count_b, count_c), modes),
        out_shape=(half, half, half, half, jax.ShapeDtypeStruct((2,) + msg, jnp.float32)),
        in_specs=[vmem] * 4 + [pl.BlockSpec(memory_space=pltpu.SMEM)] * 3,
        out_specs=(vmem,) * 5,
        scratch_shapes=[
            pltpu.VMEM((count_a,) + msg, jnp.float32),
            pltpu.VMEM((count_b,) + msg, jnp.float32),
            pltpu.VMEM((count_c,) + msg, jnp.float32),
            pltpu.SemaphoreType.DMA((count_a,)),
            pltpu.SemaphoreType.DMA((count_a,)),
            pltpu.SemaphoreType.DMA((count_b,)),
            pltpu.SemaphoreType.DMA((count_b,)),
            pltpu.SemaphoreType.DMA((count_c,)),
            pltpu.SemaphoreType.DMA((count_c,)),
        ],
        compiler_params=pltpu.CompilerParams(collective_id=0, has_side_effects=True),
    )(signal_x, gate_q, gate_k, cotangent, memory, residue, skip_gain)
    total, sums = small[0], small[1]
    norm_scale = 1.0 / math.sqrt(all_channels * seq_total)
    grad_skip = total[:, 7 * modes] / math.sqrt(seq_total)
    grad_residue = gain * sums[0, 5 * modes:6 * modes] * norm_scale
    grad_memory = residue * gain * sums[0, 6 * modes:7 * modes] * norm_scale
    return (output, grad_x, grad_q, grad_k, grad_skip, grad_residue, grad_memory)


def solution(mesh):
    return jax.shard_map(
        per_device,
        mesh=mesh,
        in_specs=(
            P("ch", "seq"),
            P("ch", "seq"),
            P("ch", "seq"),
            P("ch"),
            P(),
            P(),
            P("ch", "seq"),
        ),
        out_specs=(
            P("ch", "seq"),
            P("ch", "seq"),
            P("ch", "seq"),
            P("ch", "seq"),
            P("ch"),
            P(),
            P(),
        ),
        check_vma=False,
    )
```

```python
import functools
import math

import jax
import jax.numpy as jnp
from jax import lax
from jax.experimental import pallas as pl
from jax.experimental.pallas import tpu as pltpu
from jax.sharding import PartitionSpec as P

HIGH_PREC = lax.Precision.HIGHEST


def mm(pattern, left_op, right_op):
    return jnp.einsum(pattern, left_op, right_op, precision=HIGH_PREC)


GROUP = 8
LANES = 128
SLABS = 8


def row_sum(value):
    return jnp.sum(value, axis=0, keepdims=True)


def slab_coefs(count, size, pos, inv, block_len, modes):
    lane = lax.broadcasted_iota(jnp.int32, (count, LANES), 1) // modes
    index = lax.broadcasted_iota(jnp.int32, (count, LANES), 0)
    span = float(size * block_len)
    step = jnp.exp(-span * inv)
    starts = index.astype(jnp.float32) * span
    lag = jnp.exp(-starts * inv)
    before = jnp.where(index < pos, jnp.exp(-((pos - 1 - index).astype(jnp.float32) * span) * inv), 0.0)
    after = jnp.where(index > pos, jnp.exp(-((index - pos - 1).astype(jnp.float32) * span) * inv), 0.0)
    keep = jnp.where(lane <= 1, step, 1.0)[0:1]
    carry = jnp.where(lane == 1, step * span, 0.0)[0:1]
    take = jnp.where((lane >= 2) & (lane <= 4), lag, 1.0)
    shift = jnp.where(lane == 4, lag * starts * inv, 0.0)
    edge = jnp.where(lane == 0, before, jnp.where(lane == 2, after, 0.0))
    return keep, carry, take, shift, edge


def level_coefs(count, size, inv, block_len, modes):
    slab = lax.broadcasted_iota(jnp.int32, (1, LANES), 1) // modes
    levels = []
    width = size
    while width < count * size:
        span = float(width * block_len)
        step = jnp.exp(-span * inv)
        levels.append((
            jnp.where(slab <= 1, step, 1.0),
            jnp.where(slab == 1, step * span, 0.0),
            jnp.where((slab >= 2) & (slab <= 4), step, 1.0),
            jnp.where(slab == 4, step * span * inv, 0.0),
        ))
        width *= 2
    return levels


def combine_pair(left, right, coefs, inv, modes):
    keep, carry, take, shift = coefs
    slab = lax.broadcasted_iota(jnp.int32, (1, LANES), 1) // modes
    s1 = row_sum(pltpu.roll(left, 3 * modes, 1) * right)
    s2 = row_sum(pltpu.roll(left, 4 * modes, 1) * right)
    s3 = row_sum(pltpu.roll(left, 2 * modes, 1) * right)
    cross = jnp.where(slab == 5, pltpu.roll(s1, 2 * modes, 1), 0.0) + jnp.where(
        slab == 6, pltpu.roll(s2, 2 * modes, 1) + pltpu.roll(s3 * inv, 3 * modes, 1), 0.0)
    return (keep * left + take * right + carry * pltpu.roll(left, modes, 1)
            + shift * pltpu.roll(right, modes, 1) + cross)


def fold_items(items, levels, edge_c, inv, modes):
    edge = edge_c[0:1] * items[0]
    for index in range(1, len(items)):
        edge = edge + edge_c[index:index + 1] * items[index]
    layer = list(items)
    for coefs in levels:
        layer = [combine_pair(layer[i], layer[i + 1], coefs, inv, modes) for i in range(0, len(layer), 2)]
    return layer[0], edge


def start_ring(buf, send_sems, recv_sems, count, pos, device_of):
    descs = []
    for dist in range(1, count):
        desc = pltpu.make_async_remote_copy(
            src_ref=buf.at[0],
            dst_ref=buf.at[count - dist],
            send_sem=send_sems.at[dist],
            recv_sem=recv_sems.at[count - dist],
            device_id=device_of((pos + dist) % count),
            device_id_type=pl.DeviceIdType.MESH,
        )
        desc.start()
        descs.append(desc)
    return descs


def finish_ring(descs, buf, count, pos):
    for desc in descs:
        desc.wait_recv()
    for desc in descs:
        desc.wait_send()
    return [buf[(slot - pos + count) % count] for slot in range(count)]


def dot_nn(left_op, right_op):
    return jnp.dot(left_op, right_op, precision=HIGH_PREC, preferred_element_type=jnp.float32)


def dot_nt(left_op, right_op):
    return lax.dot_general(left_op, right_op, (((1,), (1,)), ((), ())), precision=HIGH_PREC,
                           preferred_element_type=jnp.float32)


def dot_tn(left_op, right_op):
    return lax.dot_general(left_op, right_op, (((0,), (0,)), ((), ())), precision=HIGH_PREC,
                           preferred_element_type=jnp.float32)


def fused_kernel(counts, modes, x_ref, q_ref, k_ref, d_ref, mem_ref, res_ref, gain_ref,
                 mix_ref, small_ref,
                 buf_a, buf_b, buf_c, send_a, recv_a, send_b, recv_b, send_c, recv_c):
    count_a, count_b, count_c = counts
    channels, block_len = x_ref.shape
    seq_index = lax.axis_index("seq")
    ch_index = lax.axis_index("ch")
    pos_a = seq_index % count_a
    pos_b = seq_index // count_a

    def dev_a(other):
        return (pos_b * count_a + other, ch_index)

    def dev_b(other):
        return (other * count_a + pos_a, ch_index)

    def dev_c(other):
        return (seq_index, other)

    barrier = pltpu.get_barrier_semaphore()
    for count, pos, device_of in ((count_a, pos_a, dev_a), (count_b, pos_b, dev_b), (count_c, ch_index, dev_c)):
        for dist in range(1, count):
            pl.semaphore_signal(barrier, inc=1, device_id=device_of((pos + dist) % count),
                                device_id_type=pl.DeviceIdType.MESH)

    slab = lax.broadcasted_iota(jnp.int32, (1, LANES), 1) // modes
    mode_of = lax.broadcasted_iota(jnp.int32, (1, LANES), 1) % modes
    mem_v = jnp.zeros((1, LANES), jnp.float32)
    res_v = jnp.zeros((1, LANES), jnp.float32)
    for mode in range(modes):
        mem_v = jnp.where(mode_of == mode, mem_ref[mode], mem_v)
        res_v = jnp.where(mode_of == mode, res_ref[mode], res_v)
    inv = 1.0 / mem_v
    amp = res_v * jnp.sqrt(2.0 * inv)
    chan_of = lax.broadcasted_iota(jnp.int32, (channels, 1), 0)
    gain = jnp.zeros((channels, 1), jnp.float32)
    for chan in range(channels):
        gain = jnp.where(chan_of == chan, gain_ref[chan], gain)
    offs = lax.broadcasted_iota(jnp.int32, (block_len, LANES), 0).astype(jnp.float32)
    back = float(block_len - 1) - offs
    e_down = jnp.exp(-offs * inv)
    e_tail = jnp.exp(-back * inv)
    e_next = jnp.exp(-(offs + 1.0) * inv)
    e_up = jnp.exp(offs * inv)
    right_v = jnp.where(slab == 0, e_tail, jnp.where(slab == 1, e_tail * back, 0.0))
    right_g = jnp.where(slab == 2, e_down, jnp.where(slab == 3, e_next, jnp.where(
        slab == 4, e_next * ((offs + 1.0) * inv - 0.5), 0.0)))
    right_r = jnp.where(slab == 5, e_up, jnp.where(slab == 6, e_up * offs * inv, 0.0))

    x_float = x_ref[...].astype(jnp.float32)
    q_float = q_ref[...].astype(jnp.float32)
    k_float = k_ref[...].astype(jnp.float32)
    d_float = d_ref[...].astype(jnp.float32)
    values = x_float * k_float
    grad_mixed = d_float * q_float
    row_t = lax.broadcasted_iota(jnp.int32, (block_len, block_len), 0)
    col_s = lax.broadcasted_iota(jnp.int32, (block_len, block_len), 1)
    lower = row_t >= col_s
    pair = jnp.where(lower, dot_tn(grad_mixed, values), 0.0)
    near = dot_nn(pair, right_r)
    terms = jnp.where(slab == 5, e_down * near, jnp.where(
        slab == 6, e_down * ((offs * inv - 0.5) * pltpu.roll(near, modes, 1) - near), 0.0))
    local = row_sum(terms)
    skip = jnp.sum(grad_mixed * values, axis=1, keepdims=True)
    state = dot_nn(values, right_v) + dot_nn(grad_mixed, right_g) + jnp.where(slab == 7, skip, local)
    buf_a[0] = state
    edge_a_c = slab_coefs(count_a, 1, pos_a, inv, block_len, modes)[4]
    edge_b_c = slab_coefs(count_b, count_a, pos_b, inv, block_len, modes)[4]
    levels_a = level_coefs(count_a, 1, inv, block_len, modes)
    levels_b = level_coefs(count_b, count_a, inv, block_len, modes)
    near_w = jnp.exp(-(pos_a * block_len).astype(jnp.float32) * inv)
    far_w = jnp.exp(-((count_a - 1 - pos_a) * block_len).astype(jnp.float32) * inv)
    join = jnp.where(slab == 0, near_w, jnp.where(slab == 2, far_w, 0.0))
    pl.semaphore_wait(barrier, count_a + count_b + count_c - 3)

    descs = start_ring(buf_a, send_a, recv_a, count_a, pos_a, dev_a)
    toep = jnp.where(lower, dot_nt(jnp.where(slab == 0, e_down * amp, 0.0), jnp.where(slab == 0, e_up, 0.0)), 0.0)
    conv = dot_nt(values, toep)
    corr = dot_nn(grad_mixed, toep)
    into_f = jnp.where(slab == 0, e_next * amp, 0.0)
    into_b = jnp.where(slab == 2, jnp.exp(-(float(block_len) - offs) * inv) * amp, 0.0)
    items = finish_ring(descs, buf_a, count_a, pos_a)
    group, edge_a = fold_items(items, levels_a, edge_a_c, inv, modes)
    buf_b[0] = group
    descs = start_ring(buf_b, send_b, recv_b, count_b, pos_b, dev_b)
    items = finish_ring(descs, buf_b, count_b, pos_b)
    total, edge_b = fold_items(items, levels_b, edge_b_c, inv, modes)
    buf_c[0] = total
    descs = start_ring(buf_c, send_c, recv_c, count_c, ch_index, dev_c)
    edge = join * edge_b + edge_a
    conv = conv + dot_nt(edge, into_f)
    corr = corr + dot_nt(edge, into_b)
    mixed_out = conv + gain * values
    grad_values = gain * grad_mixed + corr
    mix_ref[0] = mixed_out
    mix_ref[1] = grad_values
    items = finish_ring(descs, buf_c, count_c, ch_index)
    sums = items[0]
    for item in items[1:]:
        sums = sums + item
    small_ref[0] = total
    small_ref[1] = sums


def output_kernel(x_ref, q_ref, k_ref, d_ref, mix_ref, out_ref, gx_ref, gq_ref, gk_ref):
    mixed_out = mix_ref[0]
    grad_values = mix_ref[1]
    out_ref[...] = (q_ref[...].astype(jnp.float32) * mixed_out).astype(jnp.bfloat16)
    gx_ref[...] = (grad_values * k_ref[...].astype(jnp.float32)).astype(jnp.bfloat16)
    gq_ref[...] = (d_ref[...].astype(jnp.float32) * mixed_out).astype(jnp.bfloat16)
    gk_ref[...] = (grad_values * x_ref[...].astype(jnp.float32)).astype(jnp.bfloat16)


def per_device(signal_x, gate_q, gate_k, skip_gain, residue, memory, cotangent):
    channels, block_len = signal_x.shape
    modes = memory.shape[0]
    seq_total = lax.axis_size("seq") * block_len
    all_channels = channels * lax.axis_size("ch")
    count_a = min(GROUP, lax.axis_size("seq"))
    count_b = lax.axis_size("seq") // count_a
    count_c = lax.axis_size("ch")
    inv_m = 1.0 / memory
    gain = jnp.sqrt(2.0 / memory)
    amp = residue * gain
    msg = (channels, LANES)
    vmem = pl.BlockSpec(memory_space=pltpu.VMEM)
    half = jax.ShapeDtypeStruct(signal_x.shape, jnp.bfloat16)
    mix, small = pl.pallas_call(
        functools.partial(fused_kernel, (count_a, count_b, count_c), modes),
        out_shape=(jax.ShapeDtypeStruct((2,) + signal_x.shape, jnp.float32),
                   jax.ShapeDtypeStruct((2,) + msg, jnp.float32)),
        in_specs=[vmem] * 4 + [pl.BlockSpec(memory_space=pltpu.SMEM)] * 3,
        out_specs=(vmem,) * 2,
        scratch_shapes=[
            pltpu.VMEM((count_a,) + msg, jnp.float32),
            pltpu.VMEM((count_b,) + msg, jnp.float32),
            pltpu.VMEM((count_c,) + msg, jnp.float32),
            pltpu.SemaphoreType.DMA((count_a,)),
            pltpu.SemaphoreType.DMA((count_a,)),
            pltpu.SemaphoreType.DMA((count_b,)),
            pltpu.SemaphoreType.DMA((count_b,)),
            pltpu.SemaphoreType.DMA((count_c,)),
            pltpu.SemaphoreType.DMA((count_c,)),
        ],
        compiler_params=pltpu.CompilerParams(collective_id=0, has_side_effects=True),
    )(signal_x, gate_q, gate_k, cotangent, memory, residue, skip_gain)
    output, grad_x, grad_q, grad_k = pl.pallas_call(
        output_kernel,
        out_shape=(half, half, half, half),
        in_specs=[vmem] * 5,
        out_specs=(vmem,) * 4,
    )(signal_x, gate_q, gate_k, cotangent, mix)
    total, sums = small[0], small[1]
    norm_scale = 1.0 / math.sqrt(all_channels * seq_total)
    grad_skip = total[:, 7 * modes] / math.sqrt(seq_total)
    grad_residue = gain * sums[0, 5 * modes:6 * modes] * norm_scale
    grad_memory = residue * gain * sums[0, 6 * modes:7 * modes] * norm_scale
    return (output, grad_x, grad_q, grad_k, grad_skip, grad_residue, grad_memory)


def solution(mesh):
    return jax.shard_map(
        per_device,
        mesh=mesh,
        in_specs=(
            P("ch", "seq"),
            P("ch", "seq"),
            P("ch", "seq"),
            P("ch"),
            P(),
            P(),
            P("ch", "seq"),
        ),
        out_specs=(
            P("ch", "seq"),
            P("ch", "seq"),
            P("ch", "seq"),
            P("ch", "seq"),
            P("ch"),
            P(),
            P(),
        ),
        check_vma=False,
    )
```

```python
import functools
import math

import jax
import jax.numpy as jnp
from jax import lax
from jax.experimental import pallas as pl
from jax.experimental.pallas import tpu as pltpu
from jax.sharding import PartitionSpec as P

HIGH_PREC = lax.Precision.HIGHEST


def mm(pattern, left_op, right_op):
    return jnp.einsum(pattern, left_op, right_op, precision=HIGH_PREC)


GROUP = 8
LANES = 128
SLABS = 8


def row_sum(value):
    return jnp.sum(value, axis=0, keepdims=True)


def slab_coefs(count, size, pos, inv, block_len, modes):
    lane = lax.broadcasted_iota(jnp.int32, (count, LANES), 1) // modes
    index = lax.broadcasted_iota(jnp.int32, (count, LANES), 0)
    span = float(size * block_len)
    step = jnp.exp(-span * inv)
    starts = index.astype(jnp.float32) * span
    lag = jnp.exp(-starts * inv)
    before = jnp.where(index < pos, jnp.exp(-((pos - 1 - index).astype(jnp.float32) * span) * inv), 0.0)
    after = jnp.where(index > pos, jnp.exp(-((index - pos - 1).astype(jnp.float32) * span) * inv), 0.0)
    keep = jnp.where(lane <= 1, step, 1.0)[0:1]
    carry = jnp.where(lane == 1, step * span, 0.0)[0:1]
    take = jnp.where((lane >= 2) & (lane <= 4), lag, 1.0)
    shift = jnp.where(lane == 4, lag * starts * inv, 0.0)
    edge = jnp.where(lane == 0, before, jnp.where(lane == 2, after, 0.0))
    return keep, carry, take, shift, edge


def level_coefs(count, size, inv, block_len, modes):
    slab = lax.broadcasted_iota(jnp.int32, (1, LANES), 1) // modes
    levels = []
    width = size
    while width < count * size:
        span = float(width * block_len)
        step = jnp.exp(-span * inv)
        levels.append((
            jnp.where(slab <= 1, step, 1.0),
            jnp.where(slab == 1, step * span, 0.0),
            jnp.where((slab >= 2) & (slab <= 4), step, 1.0),
            jnp.where(slab == 4, step * span * inv, 0.0),
        ))
        width *= 2
    return levels


def combine_pair(left, right, coefs, inv, modes):
    keep, carry, take, shift = coefs
    slab = lax.broadcasted_iota(jnp.int32, (1, LANES), 1) // modes
    s1 = row_sum(pltpu.roll(left, 3 * modes, 1) * right)
    s2 = row_sum(pltpu.roll(left, 4 * modes, 1) * right)
    s3 = row_sum(pltpu.roll(left, 2 * modes, 1) * right)
    cross = jnp.where(slab == 5, pltpu.roll(s1, 2 * modes, 1), 0.0) + jnp.where(
        slab == 6, pltpu.roll(s2, 2 * modes, 1) + pltpu.roll(s3 * inv, 3 * modes, 1), 0.0)
    return (keep * left + take * right + carry * pltpu.roll(left, modes, 1)
            + shift * pltpu.roll(right, modes, 1) + cross)


def fold_items(items, levels, edge_c, inv, modes):
    edge = edge_c[0:1] * items[0]
    for index in range(1, len(items)):
        edge = edge + edge_c[index:index + 1] * items[index]
    layer = list(items)
    for coefs in levels:
        layer = [combine_pair(layer[i], layer[i + 1], coefs, inv, modes) for i in range(0, len(layer), 2)]
    return layer[0], edge


def start_ring(buf, send_sems, recv_sems, count, pos, device_of):
    descs = []
    for dist in range(1, count):
        desc = pltpu.make_async_remote_copy(
            src_ref=buf.at[0],
            dst_ref=buf.at[count - dist],
            send_sem=send_sems.at[dist],
            recv_sem=recv_sems.at[count - dist],
            device_id=device_of((pos + dist) % count),
            device_id_type=pl.DeviceIdType.MESH,
        )
        desc.start()
        descs.append(desc)
    return descs


def finish_ring(descs, buf, count, pos):
    for desc in descs:
        desc.wait_recv()
    for desc in descs:
        desc.wait_send()
    return [buf[(slot - pos + count) % count] for slot in range(count)]


def dot_nn(left_op, right_op):
    return jnp.dot(left_op, right_op, precision=HIGH_PREC, preferred_element_type=jnp.float32)


def dot_nt(left_op, right_op):
    return lax.dot_general(left_op, right_op, (((1,), (1,)), ((), ())), precision=HIGH_PREC,
                           preferred_element_type=jnp.float32)


def dot_tn(left_op, right_op):
    return lax.dot_general(left_op, right_op, (((0,), (0,)), ((), ())), precision=HIGH_PREC,
                           preferred_element_type=jnp.float32)


def fused_kernel(counts, modes, x_ref, q_ref, k_ref, d_ref, mem_ref, res_ref, gain_ref,
                 mix_ref, small_ref,
                 buf_a, buf_b, send_a, recv_a, send_b, recv_b):
    count_a, count_b, count_c = counts
    channels, block_len = x_ref.shape
    seq_index = lax.axis_index("seq")
    ch_index = lax.axis_index("ch")
    pos_a = seq_index % count_a
    pos_b = seq_index // count_a

    def dev_a(other):
        return (pos_b * count_a + other, ch_index)

    def dev_b(other):
        return ((other // count_c) * count_a + pos_a, other % count_c)

    barrier = pltpu.get_barrier_semaphore()
    for count, pos, device_of in ((count_a, pos_a, dev_a), (count_b * count_c, pos_b * count_c + ch_index, dev_b)):
        for dist in range(1, count):
            pl.semaphore_signal(barrier, inc=1, device_id=device_of((pos + dist) % count),
                                device_id_type=pl.DeviceIdType.MESH)

    slab = lax.broadcasted_iota(jnp.int32, (1, LANES), 1) // modes
    mode_of = lax.broadcasted_iota(jnp.int32, (1, LANES), 1) % modes
    mem_v = jnp.zeros((1, LANES), jnp.float32)
    res_v = jnp.zeros((1, LANES), jnp.float32)
    for mode in range(modes):
        mem_v = jnp.where(mode_of == mode, mem_ref[mode], mem_v)
        res_v = jnp.where(mode_of == mode, res_ref[mode], res_v)
    inv = 1.0 / mem_v
    amp = res_v * jnp.sqrt(2.0 * inv)
    chan_of = lax.broadcasted_iota(jnp.int32, (channels, 1), 0)
    gain = jnp.zeros((channels, 1), jnp.float32)
    for chan in range(channels):
        gain = jnp.where(chan_of == chan, gain_ref[chan], gain)
    offs = lax.broadcasted_iota(jnp.int32, (block_len, LANES), 0).astype(jnp.float32)
    back = float(block_len - 1) - offs
    e_down = jnp.exp(-offs * inv)
    e_tail = jnp.exp(-back * inv)
    e_next = jnp.exp(-(offs + 1.0) * inv)
    e_up = jnp.exp(offs * inv)
    right_v = jnp.where(slab == 0, e_tail, jnp.where(slab == 1, e_tail * back, 0.0))
    right_g = jnp.where(slab == 2, e_down, jnp.where(slab == 3, e_next, jnp.where(
        slab == 4, e_next * ((offs + 1.0) * inv - 0.5), 0.0)))
    right_r = jnp.where(slab == 5, e_up, jnp.where(slab == 6, e_up * offs * inv, 0.0))

    x_float = x_ref[...].astype(jnp.float32)
    q_float = q_ref[...].astype(jnp.float32)
    k_float = k_ref[...].astype(jnp.float32)
    d_float = d_ref[...].astype(jnp.float32)
    values = x_float * k_float
    grad_mixed = d_float * q_float
    row_t = lax.broadcasted_iota(jnp.int32, (block_len, block_len), 0)
    col_s = lax.broadcasted_iota(jnp.int32, (block_len, block_len), 1)
    lower = row_t >= col_s
    pair = jnp.where(lower, dot_tn(grad_mixed, values), 0.0)
    near = dot_nn(pair, right_r)
    terms = jnp.where(slab == 5, e_down * near, jnp.where(
        slab == 6, e_down * ((offs * inv - 0.5) * pltpu.roll(near, modes, 1) - near), 0.0))
    local = row_sum(terms)
    skip = jnp.sum(grad_mixed * values, axis=1, keepdims=True)
    state = dot_nn(values, right_v) + dot_nn(grad_mixed, right_g) + jnp.where(slab == 7, skip, local)
    buf_a[0] = state
    edge_a_c = slab_coefs(count_a, 1, pos_a, inv, block_len, modes)[4]
    edge_b_c = slab_coefs(count_b, count_a, pos_b, inv, block_len, modes)[4]
    levels_a = level_coefs(count_a, 1, inv, block_len, modes)
    levels_b = level_coefs(count_b, count_a, inv, block_len, modes)
    near_w = jnp.exp(-(pos_a * block_len).astype(jnp.float32) * inv)
    far_w = jnp.exp(-((count_a - 1 - pos_a) * block_len).astype(jnp.float32) * inv)
    join = jnp.where(slab == 0, near_w, jnp.where(slab == 2, far_w, 0.0))
    pl.semaphore_wait(barrier, count_a + count_b * count_c - 2)

    descs = start_ring(buf_a, send_a, recv_a, count_a, pos_a, dev_a)
    toep = jnp.where(lower, dot_nt(jnp.where(slab == 0, e_down * amp, 0.0), jnp.where(slab == 0, e_up, 0.0)), 0.0)
    conv = dot_nt(values, toep)
    corr = dot_nn(grad_mixed, toep)
    into_f = jnp.where(slab == 0, e_next * amp, 0.0)
    into_b = jnp.where(slab == 2, jnp.exp(-(float(block_len) - offs) * inv) * amp, 0.0)
    items = finish_ring(descs, buf_a, count_a, pos_a)
    group, edge_a = fold_items(items, levels_a, edge_a_c, inv, modes)
    buf_b[0] = group
    count_bc = count_b * count_c
    pos_bc = pos_b * count_c + ch_index
    descs = start_ring(buf_b, send_b, recv_b, count_bc, pos_bc, dev_b)
    for desc in descs:
        desc.wait_recv()
    for desc in descs:
        desc.wait_send()
    totals = []
    for chan in range(count_c):
        column = [buf_b[(group * count_c + chan - pos_bc + count_bc) % count_bc] for group in range(count_b)]
        totals.append(fold_items(column, levels_b, edge_b_c, inv, modes)[0])
    own = [buf_b[(group * count_c + ch_index - pos_bc + count_bc) % count_bc] for group in range(count_b)]
    edge_b = edge_b_c[0:1] * own[0]
    for group in range(1, count_b):
        edge_b = edge_b + edge_b_c[group:group + 1] * own[group]
    total = totals[0]
    sums = totals[0]
    for chan in range(1, count_c):
        total = jnp.where(ch_index == chan, totals[chan], total)
        sums = sums + totals[chan]
    edge = join * edge_b + edge_a
    conv = conv + dot_nt(edge, into_f)
    corr = corr + dot_nt(edge, into_b)
    mixed_out = conv + gain * values
    grad_values = gain * grad_mixed + corr
    mix_ref[0] = mixed_out
    mix_ref[1] = grad_values
    small_ref[0] = total
    small_ref[1] = sums


def output_kernel(x_ref, q_ref, k_ref, d_ref, mix_ref, out_ref, gx_ref, gq_ref, gk_ref):
    mixed_out = mix_ref[0]
    grad_values = mix_ref[1]
    out_ref[...] = (q_ref[...].astype(jnp.float32) * mixed_out).astype(jnp.bfloat16)
    gx_ref[...] = (grad_values * k_ref[...].astype(jnp.float32)).astype(jnp.bfloat16)
    gq_ref[...] = (d_ref[...].astype(jnp.float32) * mixed_out).astype(jnp.bfloat16)
    gk_ref[...] = (grad_values * x_ref[...].astype(jnp.float32)).astype(jnp.bfloat16)


def per_device(signal_x, gate_q, gate_k, skip_gain, residue, memory, cotangent):
    channels, block_len = signal_x.shape
    modes = memory.shape[0]
    seq_total = lax.axis_size("seq") * block_len
    all_channels = channels * lax.axis_size("ch")
    count_a = min(GROUP, lax.axis_size("seq"))
    count_b = lax.axis_size("seq") // count_a
    count_c = lax.axis_size("ch")
    inv_m = 1.0 / memory
    gain = jnp.sqrt(2.0 / memory)
    amp = residue * gain
    msg = (channels, LANES)
    vmem = pl.BlockSpec(memory_space=pltpu.VMEM)
    half = jax.ShapeDtypeStruct(signal_x.shape, jnp.bfloat16)
    mix, small = pl.pallas_call(
        functools.partial(fused_kernel, (count_a, count_b, count_c), modes),
        out_shape=(jax.ShapeDtypeStruct((2,) + signal_x.shape, jnp.float32),
                   jax.ShapeDtypeStruct((2,) + msg, jnp.float32)),
        in_specs=[vmem] * 4 + [pl.BlockSpec(memory_space=pltpu.SMEM)] * 3,
        out_specs=(vmem,) * 2,
        scratch_shapes=[
            pltpu.VMEM((count_a,) + msg, jnp.float32),
            pltpu.VMEM((count_b * count_c,) + msg, jnp.float32),
            pltpu.SemaphoreType.DMA((count_a,)),
            pltpu.SemaphoreType.DMA((count_a,)),
            pltpu.SemaphoreType.DMA((count_b * count_c,)),
            pltpu.SemaphoreType.DMA((count_b * count_c,)),
        ],
        compiler_params=pltpu.CompilerParams(collective_id=0, has_side_effects=True),
    )(signal_x, gate_q, gate_k, cotangent, memory, residue, skip_gain)
    output, grad_x, grad_q, grad_k = pl.pallas_call(
        output_kernel,
        out_shape=(half, half, half, half),
        in_specs=[vmem] * 5,
        out_specs=(vmem,) * 4,
    )(signal_x, gate_q, gate_k, cotangent, mix)
    total, sums = small[0], small[1]
    norm_scale = 1.0 / math.sqrt(all_channels * seq_total)
    grad_skip = total[:, 7 * modes] / math.sqrt(seq_total)
    grad_residue = gain * sums[0, 5 * modes:6 * modes] * norm_scale
    grad_memory = residue * gain * sums[0, 6 * modes:7 * modes] * norm_scale
    return (output, grad_x, grad_q, grad_k, grad_skip, grad_residue, grad_memory)


def solution(mesh):
    return jax.shard_map(
        per_device,
        mesh=mesh,
        in_specs=(
            P("ch", "seq"),
            P("ch", "seq"),
            P("ch", "seq"),
            P("ch"),
            P(),
            P(),
            P("ch", "seq"),
        ),
        out_specs=(
            P("ch", "seq"),
            P("ch", "seq"),
            P("ch", "seq"),
            P("ch", "seq"),
            P("ch"),
            P(),
            P(),
        ),
        check_vma=False,
    )
```

```python
import functools
import math

import jax
import jax.numpy as jnp
from jax import lax
from jax.experimental import pallas as pl
from jax.experimental.pallas import tpu as pltpu
from jax.sharding import PartitionSpec as P

HIGH_PREC = lax.Precision.HIGHEST


def mm(pattern, left_op, right_op):
    return jnp.einsum(pattern, left_op, right_op, precision=HIGH_PREC)


GROUP = 8
LANES = 128
SLABS = 8


def row_sum(value):
    return jnp.sum(value, axis=0, keepdims=True)


def slab_coefs(count, size, pos, inv, block_len, modes):
    lane = lax.broadcasted_iota(jnp.int32, (count, LANES), 1) // modes
    index = lax.broadcasted_iota(jnp.int32, (count, LANES), 0)
    span = float(size * block_len)
    step = jnp.exp(-span * inv)
    starts = index.astype(jnp.float32) * span
    lag = jnp.exp(-starts * inv)
    before = jnp.where(index < pos, jnp.exp(-((pos - 1 - index).astype(jnp.float32) * span) * inv), 0.0)
    after = jnp.where(index > pos, jnp.exp(-((index - pos - 1).astype(jnp.float32) * span) * inv), 0.0)
    keep = jnp.where(lane <= 1, step, 1.0)[0:1]
    carry = jnp.where(lane == 1, step * span, 0.0)[0:1]
    take = jnp.where((lane >= 2) & (lane <= 4), lag, 1.0)
    shift = jnp.where(lane == 4, lag * starts * inv, 0.0)
    edge = jnp.where(lane == 0, before, jnp.where(lane == 2, after, 0.0))
    return keep, carry, take, shift, edge


def level_coefs(count, size, inv, block_len, modes):
    slab = lax.broadcasted_iota(jnp.int32, (1, LANES), 1) // modes
    levels = []
    width = size
    while width < count * size:
        span = float(width * block_len)
        step = jnp.exp(-span * inv)
        levels.append((
            jnp.where(slab <= 1, step, 1.0),
            jnp.where(slab == 1, step * span, 0.0),
            jnp.where((slab >= 2) & (slab <= 4), step, 1.0),
            jnp.where(slab == 4, step * span * inv, 0.0),
        ))
        width *= 2
    return levels


def combine_pair(left, right, coefs, inv, modes):
    keep, carry, take, shift = coefs
    slab = lax.broadcasted_iota(jnp.int32, (1, LANES), 1) // modes
    s1 = row_sum(pltpu.roll(left, 3 * modes, 1) * right)
    s2 = row_sum(pltpu.roll(left, 4 * modes, 1) * right)
    s3 = row_sum(pltpu.roll(left, 2 * modes, 1) * right)
    cross = jnp.where(slab == 5, pltpu.roll(s1, 2 * modes, 1), 0.0) + jnp.where(
        slab == 6, pltpu.roll(s2, 2 * modes, 1) + pltpu.roll(s3 * inv, 3 * modes, 1), 0.0)
    return (keep * left + take * right + carry * pltpu.roll(left, modes, 1)
            + shift * pltpu.roll(right, modes, 1) + cross)


def fold_items(items, levels, edge_c, inv, modes):
    edge = edge_c[0:1] * items[0]
    for index in range(1, len(items)):
        edge = edge + edge_c[index:index + 1] * items[index]
    layer = list(items)
    for coefs in levels:
        layer = [combine_pair(layer[i], layer[i + 1], coefs, inv, modes) for i in range(0, len(layer), 2)]
    return layer[0], edge


def start_ring(buf, send_sems, recv_sems, count, pos, device_of):
    descs = []
    for dist in range(1, count):
        desc = pltpu.make_async_remote_copy(
            src_ref=buf.at[0],
            dst_ref=buf.at[count - dist],
            send_sem=send_sems.at[dist],
            recv_sem=recv_sems.at[count - dist],
            device_id=device_of((pos + dist) % count),
            device_id_type=pl.DeviceIdType.MESH,
        )
        desc.start()
        descs.append(desc)
    return descs


def finish_ring(descs, buf, count, pos):
    for desc in descs:
        desc.wait_recv()
    for desc in descs:
        desc.wait_send()
    return [buf[(slot - pos + count) % count] for slot in range(count)]


def dot_nn(left_op, right_op):
    return jnp.dot(left_op, right_op, precision=HIGH_PREC, preferred_element_type=jnp.float32)


def dot_nt(left_op, right_op):
    return lax.dot_general(left_op, right_op, (((1,), (1,)), ((), ())), precision=HIGH_PREC,
                           preferred_element_type=jnp.float32)


def dot_tn(left_op, right_op):
    return lax.dot_general(left_op, right_op, (((0,), (0,)), ((), ())), precision=HIGH_PREC,
                           preferred_element_type=jnp.float32)


def fused_kernel(counts, modes, x_ref, q_ref, k_ref, d_ref, mem_ref, res_ref, gain_ref,
                 mix_ref, small_ref,
                 buf_a, buf_b, buf_c, send_a, recv_a, send_b, recv_b, send_c, recv_c):
    count_a, count_b, count_c = counts
    channels, block_len = x_ref.shape
    seq_index = lax.axis_index("seq")
    ch_index = lax.axis_index("ch")
    pos_a = seq_index % count_a
    pos_b = seq_index // count_a

    def dev_a(other):
        return (pos_b * count_a + other, ch_index)

    def dev_b(other):
        return (other * count_a + pos_a, ch_index)

    def dev_c(other):
        return (seq_index, other)

    barrier = pltpu.get_barrier_semaphore()
    for count, pos, device_of in ((count_a, pos_a, dev_a), (count_b, pos_b, dev_b), (count_c, ch_index, dev_c)):
        for dist in range(1, count):
            pl.semaphore_signal(barrier, inc=1, device_id=device_of((pos + dist) % count),
                                device_id_type=pl.DeviceIdType.MESH)

    slab = lax.broadcasted_iota(jnp.int32, (1, LANES), 1) // modes
    mode_of = lax.broadcasted_iota(jnp.int32, (1, LANES), 1) % modes
    mem_v = jnp.zeros((1, LANES), jnp.float32)
    res_v = jnp.zeros((1, LANES), jnp.float32)
    for mode in range(modes):
        mem_v = jnp.where(mode_of == mode, mem_ref[mode], mem_v)
        res_v = jnp.where(mode_of == mode, res_ref[mode], res_v)
    inv = 1.0 / mem_v
    amp = res_v * jnp.sqrt(2.0 * inv)
    chan_of = lax.broadcasted_iota(jnp.int32, (channels, 1), 0)
    gain = jnp.zeros((channels, 1), jnp.float32)
    for chan in range(channels):
        gain = jnp.where(chan_of == chan, gain_ref[chan], gain)
    offs = lax.broadcasted_iota(jnp.int32, (block_len, LANES), 0).astype(jnp.float32)
    back = float(block_len - 1) - offs
    e_down = jnp.exp(-offs * inv)
    e_tail = jnp.exp(-back * inv)
    e_next = jnp.exp(-(offs + 1.0) * inv)
    e_up = jnp.exp(offs * inv)
    right_v = jnp.where(slab == 0, e_tail, jnp.where(slab == 1, e_tail * back, 0.0))
    right_g = jnp.where(slab == 2, e_down, jnp.where(slab == 3, e_next, jnp.where(
        slab == 4, e_next * ((offs + 1.0) * inv - 0.5), 0.0)))
    right_r = jnp.where(slab == 5, e_up, jnp.where(slab == 6, e_up * offs * inv, 0.0))

    x_float = x_ref[...].astype(jnp.float32)
    q_float = q_ref[...].astype(jnp.float32)
    k_float = k_ref[...].astype(jnp.float32)
    d_float = d_ref[...].astype(jnp.float32)
    values = x_float * k_float
    grad_mixed = d_float * q_float
    row_t = lax.broadcasted_iota(jnp.int32, (block_len, block_len), 0)
    col_s = lax.broadcasted_iota(jnp.int32, (block_len, block_len), 1)
    lower = row_t >= col_s
    pair = jnp.where(lower, dot_tn(grad_mixed, values), 0.0)
    near = dot_nn(pair, right_r)
    terms = jnp.where(slab == 5, e_down * near, jnp.where(
        slab == 6, e_down * ((offs * inv - 0.5) * pltpu.roll(near, modes, 1) - near), 0.0))
    local = row_sum(terms)
    skip = jnp.sum(grad_mixed * values, axis=1, keepdims=True)
    state = dot_nn(values, right_v) + dot_nn(grad_mixed, right_g) + jnp.where(slab == 7, skip, local)
    buf_a[0] = state
    edge_a_c = slab_coefs(count_a, 1, pos_a, inv, block_len, modes)[4]
    edge_b_c = slab_coefs(count_b, count_a, pos_b, inv, block_len, modes)[4]
    levels_a = level_coefs(count_a, 1, inv, block_len, modes)
    levels_b = level_coefs(count_b, count_a, inv, block_len, modes)
    near_w = jnp.exp(-(pos_a * block_len).astype(jnp.float32) * inv)
    far_w = jnp.exp(-((count_a - 1 - pos_a) * block_len).astype(jnp.float32) * inv)
    join = jnp.where(slab == 0, near_w, jnp.where(slab == 2, far_w, 0.0))
    pl.semaphore_wait(barrier, count_a + count_b + count_c - 3)

    descs = start_ring(buf_a, send_a, recv_a, count_a, pos_a, dev_a)
    toep = jnp.where(lower, dot_nt(jnp.where(slab == 0, e_down * amp, 0.0), jnp.where(slab == 0, e_up, 0.0)), 0.0)
    conv = dot_nt(values, toep)
    corr = dot_nn(grad_mixed, toep)
    into_f = jnp.where(slab == 0, e_next * amp, 0.0)
    into_b = jnp.where(slab == 2, jnp.exp(-(float(block_len) - offs) * inv) * amp, 0.0)
    items = finish_ring(descs, buf_a, count_a, pos_a)
    group, edge_a = fold_items(items, levels_a, edge_a_c, inv, modes)
    buf_b[0] = group
    descs = start_ring(buf_b, send_b, recv_b, count_b, pos_b, dev_b)
    items = finish_ring(descs, buf_b, count_b, pos_b)
    total, edge_b = fold_items(items, levels_b, edge_b_c, inv, modes)
    buf_c[0] = total
    descs = start_ring(buf_c, send_c, recv_c, count_c, ch_index, dev_c)
    edge = join * edge_b + edge_a
    conv = conv + dot_nt(edge, into_f)
    corr = corr + dot_nt(edge, into_b)
    mixed_out = conv + gain * values
    grad_values = gain * grad_mixed + corr
    mix_ref[0] = mixed_out
    mix_ref[1] = grad_values
    items = finish_ring(descs, buf_c, count_c, ch_index)
    sums = items[0]
    for item in items[1:]:
        sums = sums + item
    small_ref[0] = total
    small_ref[1] = sums


def output_kernel(scales, x_ref, q_ref, k_ref, d_ref, mix_ref, small_ref, mem_ref, res_ref,
                  out_ref, gx_ref, gq_ref, gk_ref, skip_ref, gres_ref, gmem_ref):
    mixed_out = mix_ref[0]
    grad_values = mix_ref[1]
    out_ref[...] = (q_ref[...].astype(jnp.float32) * mixed_out).astype(jnp.bfloat16)
    gx_ref[...] = (grad_values * k_ref[...].astype(jnp.float32)).astype(jnp.bfloat16)
    gq_ref[...] = (d_ref[...].astype(jnp.float32) * mixed_out).astype(jnp.bfloat16)
    gk_ref[...] = (grad_values * x_ref[...].astype(jnp.float32)).astype(jnp.bfloat16)
    modes = mem_ref.shape[0]
    channels = small_ref.shape[1]
    norm_scale, seq_scale = scales
    mode_of = lax.broadcasted_iota(jnp.int32, (1, LANES), 1) % modes
    mem_v = jnp.ones((1, LANES), jnp.float32)
    res_v = jnp.zeros((1, LANES), jnp.float32)
    for mode in range(modes):
        mem_v = jnp.where(mode_of == mode, mem_ref[mode], mem_v)
        res_v = jnp.where(mode_of == mode, res_ref[mode], res_v)
    gain = jnp.sqrt(2.0 / mem_v)
    sums = small_ref[1][0:1]
    grad_res = pltpu.roll(gain * sums * norm_scale, LANES - 5 * modes, 1)
    grad_mem = pltpu.roll(res_v * gain * sums * norm_scale, LANES - 6 * modes, 1)
    column = small_ref[0][:, 7 * modes:7 * modes + 1]
    lane = lax.broadcasted_iota(jnp.int32, (channels, LANES), 1)
    row = lax.broadcasted_iota(jnp.int32, (channels, LANES), 0)
    skip = jnp.sum(jnp.where(lane == row, column, 0.0), axis=0, keepdims=True) * seq_scale
    gres_ref[...] = grad_res[:, 0:modes]
    gmem_ref[...] = grad_mem[:, 0:modes]
    skip_ref[...] = skip[:, 0:channels]


def per_device(signal_x, gate_q, gate_k, skip_gain, residue, memory, cotangent):
    channels, block_len = signal_x.shape
    modes = memory.shape[0]
    seq_total = lax.axis_size("seq") * block_len
    all_channels = channels * lax.axis_size("ch")
    count_a = min(GROUP, lax.axis_size("seq"))
    count_b = lax.axis_size("seq") // count_a
    count_c = lax.axis_size("ch")
    msg = (channels, LANES)
    vmem = pl.BlockSpec(memory_space=pltpu.VMEM)
    half = jax.ShapeDtypeStruct(signal_x.shape, jnp.bfloat16)
    mix, small = pl.pallas_call(
        functools.partial(fused_kernel, (count_a, count_b, count_c), modes),
        out_shape=(jax.ShapeDtypeStruct((2,) + signal_x.shape, jnp.float32),
                   jax.ShapeDtypeStruct((2,) + msg, jnp.float32)),
        in_specs=[vmem] * 4 + [pl.BlockSpec(memory_space=pltpu.SMEM)] * 3,
        out_specs=(vmem,) * 2,
        scratch_shapes=[
            pltpu.VMEM((count_a,) + msg, jnp.float32),
            pltpu.VMEM((count_b,) + msg, jnp.float32),
            pltpu.VMEM((count_c,) + msg, jnp.float32),
            pltpu.SemaphoreType.DMA((count_a,)),
            pltpu.SemaphoreType.DMA((count_a,)),
            pltpu.SemaphoreType.DMA((count_b,)),
            pltpu.SemaphoreType.DMA((count_b,)),
            pltpu.SemaphoreType.DMA((count_c,)),
            pltpu.SemaphoreType.DMA((count_c,)),
        ],
        compiler_params=pltpu.CompilerParams(collective_id=0, has_side_effects=True),
    )(signal_x, gate_q, gate_k, cotangent, memory, residue, skip_gain)
    norm_scale = 1.0 / math.sqrt(all_channels * seq_total)
    smem = pl.BlockSpec(memory_space=pltpu.SMEM)
    output, grad_x, grad_q, grad_k, grad_skip, grad_residue, grad_memory = pl.pallas_call(
        functools.partial(output_kernel, (norm_scale, 1.0 / math.sqrt(seq_total))),
        out_shape=(half, half, half, half, jax.ShapeDtypeStruct((1, channels), jnp.float32),
                   jax.ShapeDtypeStruct((1, modes), jnp.float32), jax.ShapeDtypeStruct((1, modes), jnp.float32)),
        in_specs=[vmem] * 6 + [smem] * 2,
        out_specs=(vmem,) * 7,
    )(signal_x, gate_q, gate_k, cotangent, mix, small, memory, residue)
    grad_skip = grad_skip.reshape(channels)
    grad_residue = grad_residue.reshape(modes)
    grad_memory = grad_memory.reshape(modes)
    return (output, grad_x, grad_q, grad_k, grad_skip, grad_residue, grad_memory)


def solution(mesh):
    return jax.shard_map(
        per_device,
        mesh=mesh,
        in_specs=(
            P("ch", "seq"),
            P("ch", "seq"),
            P("ch", "seq"),
            P("ch"),
            P(),
            P(),
            P("ch", "seq"),
        ),
        out_specs=(
            P("ch", "seq"),
            P("ch", "seq"),
            P("ch", "seq"),
            P("ch", "seq"),
            P("ch"),
            P(),
            P(),
        ),
        check_vma=False,
    )
```

```python
import functools
import math

import jax
import jax.numpy as jnp
from jax import lax
from jax.experimental import pallas as pl
from jax.experimental.pallas import tpu as pltpu
from jax.sharding import PartitionSpec as P

HIGH_PREC = lax.Precision.HIGHEST


def mm(pattern, left_op, right_op):
    return jnp.einsum(pattern, left_op, right_op, precision=HIGH_PREC)


GROUP = 8
LANES = 128
SLABS = 8


def row_sum(value):
    return jnp.sum(value, axis=0, keepdims=True)


def slab_coefs(count, size, pos, inv, block_len, modes):
    lane = lax.broadcasted_iota(jnp.int32, (count, LANES), 1) // modes
    index = lax.broadcasted_iota(jnp.int32, (count, LANES), 0)
    span = float(size * block_len)
    step = jnp.exp(-span * inv)
    starts = index.astype(jnp.float32) * span
    lag = jnp.exp(-starts * inv)
    before = jnp.where(index < pos, jnp.exp(-((pos - 1 - index).astype(jnp.float32) * span) * inv), 0.0)
    after = jnp.where(index > pos, jnp.exp(-((index - pos - 1).astype(jnp.float32) * span) * inv), 0.0)
    keep = jnp.where(lane <= 1, step, 1.0)[0:1]
    carry = jnp.where(lane == 1, step * span, 0.0)[0:1]
    take = jnp.where((lane >= 2) & (lane <= 4), lag, 1.0)
    shift = jnp.where(lane == 4, lag * starts * inv, 0.0)
    edge = jnp.where(lane == 0, before, jnp.where(lane == 2, after, 0.0))
    return keep, carry, take, shift, edge


def level_coefs(count, size, inv, block_len, modes):
    slab = lax.broadcasted_iota(jnp.int32, (1, LANES), 1) // modes
    levels = []
    width = size
    while width < count * size:
        span = float(width * block_len)
        step = jnp.exp(-span * inv)
        levels.append((
            jnp.where(slab <= 1, step, 1.0),
            jnp.where(slab == 1, step * span, 0.0),
            jnp.where((slab >= 2) & (slab <= 4), step, 1.0),
            jnp.where(slab == 4, step * span * inv, 0.0),
        ))
        width *= 2
    return levels


def combine_pair(left, right, coefs, inv, modes):
    keep, carry, take, shift = coefs
    slab = lax.broadcasted_iota(jnp.int32, (1, LANES), 1) // modes
    s1 = row_sum(pltpu.roll(left, 3 * modes, 1) * right)
    s2 = row_sum(pltpu.roll(left, 4 * modes, 1) * right)
    s3 = row_sum(pltpu.roll(left, 2 * modes, 1) * right)
    cross = jnp.where(slab == 5, pltpu.roll(s1, 2 * modes, 1), 0.0) + jnp.where(
        slab == 6, pltpu.roll(s2, 2 * modes, 1) + pltpu.roll(s3 * inv, 3 * modes, 1), 0.0)
    return (keep * left + take * right + carry * pltpu.roll(left, modes, 1)
            + shift * pltpu.roll(right, modes, 1) + cross)


def fold_items(items, levels, edge_c, inv, modes):
    edge = edge_c[0:1] * items[0]
    for index in range(1, len(items)):
        edge = edge + edge_c[index:index + 1] * items[index]
    layer = list(items)
    for coefs in levels:
        layer = [combine_pair(layer[i], layer[i + 1], coefs, inv, modes) for i in range(0, len(layer), 2)]
    return layer[0], edge


def start_ring(buf, send_sems, recv_sems, count, pos, device_of):
    descs = []
    for dist in range(1, count):
        desc = pltpu.make_async_remote_copy(
            src_ref=buf.at[0],
            dst_ref=buf.at[count - dist],
            send_sem=send_sems.at[dist],
            recv_sem=recv_sems.at[count - dist],
            device_id=device_of((pos + dist) % count),
            device_id_type=pl.DeviceIdType.MESH,
        )
        desc.start()
        descs.append(desc)
    return descs


def finish_ring(descs, buf, count, pos):
    for desc in descs:
        desc.wait_recv()
    for desc in descs:
        desc.wait_send()
    return [buf[(slot - pos + count) % count] for slot in range(count)]


def dot_nn(left_op, right_op):
    return jnp.dot(left_op, right_op, precision=HIGH_PREC, preferred_element_type=jnp.float32)


def dot_nt(left_op, right_op):
    return lax.dot_general(left_op, right_op, (((1,), (1,)), ((), ())), precision=HIGH_PREC,
                           preferred_element_type=jnp.float32)


def dot_tn(left_op, right_op):
    return lax.dot_general(left_op, right_op, (((0,), (0,)), ((), ())), precision=HIGH_PREC,
                           preferred_element_type=jnp.float32)


def fused_kernel(counts, modes, x_ref, q_ref, k_ref, d_ref, mem_ref, res_ref, gain_ref,
                 mix_ref, small_ref,
                 buf_a, buf_b, buf_c, send_a, recv_a, send_b, recv_b, send_c, recv_c):
    count_a, count_b, count_c = counts
    channels, block_len = x_ref.shape
    seq_index = lax.axis_index("seq")
    ch_index = lax.axis_index("ch")
    pos_a = seq_index % count_a
    pos_b = seq_index // count_a

    def dev_a(other):
        return (pos_b * count_a + other, ch_index)

    def dev_b(other):
        return (other * count_a + pos_a, ch_index)

    def dev_c(other):
        return (seq_index, other)

    barrier = pltpu.get_barrier_semaphore()
    for count, pos, device_of in ((count_a, pos_a, dev_a), (count_b, pos_b, dev_b), (count_c, ch_index, dev_c)):
        for dist in range(1, count):
            pl.semaphore_signal(barrier, inc=1, device_id=device_of((pos + dist) % count),
                                device_id_type=pl.DeviceIdType.MESH)

    slab = lax.broadcasted_iota(jnp.int32, (1, LANES), 1) // modes
    mode_of = lax.broadcasted_iota(jnp.int32, (1, LANES), 1) % modes
    mem_v = jnp.zeros((1, LANES), jnp.float32)
    res_v = jnp.zeros((1, LANES), jnp.float32)
    for mode in range(modes):
        mem_v = jnp.where(mode_of == mode, mem_ref[mode], mem_v)
        res_v = jnp.where(mode_of == mode, res_ref[mode], res_v)
    inv = 1.0 / mem_v
    amp = res_v * jnp.sqrt(2.0 * inv)
    chan_of = lax.broadcasted_iota(jnp.int32, (channels, 1), 0)
    gain = jnp.zeros((channels, 1), jnp.float32)
    for chan in range(channels):
        gain = jnp.where(chan_of == chan, gain_ref[chan], gain)
    offs = lax.broadcasted_iota(jnp.int32, (block_len, LANES), 0).astype(jnp.float32)
    back = float(block_len - 1) - offs
    e_down = jnp.exp(-offs * inv)
    e_tail = jnp.exp(-back * inv)
    e_next = jnp.exp(-(offs + 1.0) * inv)
    e_up = jnp.exp(offs * inv)
    right_v = jnp.where(slab == 0, e_tail, jnp.where(slab == 1, e_tail * back, 0.0))
    right_g = jnp.where(slab == 2, e_down, jnp.where(slab == 3, e_next, jnp.where(
        slab == 4, e_next * ((offs + 1.0) * inv - 0.5), 0.0)))
    right_r = jnp.where(slab == 5, e_up, jnp.where(slab == 6, e_up * offs * inv, 0.0))

    x_float = x_ref[...].astype(jnp.float32)
    q_float = q_ref[...].astype(jnp.float32)
    k_float = k_ref[...].astype(jnp.float32)
    d_float = d_ref[...].astype(jnp.float32)
    values = x_float * k_float
    grad_mixed = d_float * q_float
    row_t = lax.broadcasted_iota(jnp.int32, (block_len, block_len), 0)
    col_s = lax.broadcasted_iota(jnp.int32, (block_len, block_len), 1)
    lower = row_t >= col_s
    pair = jnp.where(lower, dot_tn(grad_mixed, values), 0.0)
    near = dot_nn(pair, right_r)
    terms = jnp.where(slab == 5, e_down * near, jnp.where(
        slab == 6, e_down * ((offs * inv - 0.5) * pltpu.roll(near, modes, 1) - near), 0.0))
    local = row_sum(terms)
    skip = jnp.sum(grad_mixed * values, axis=1, keepdims=True)
    state = dot_nn(values, right_v) + dot_nn(grad_mixed, right_g) + jnp.where(slab == 7, skip, local)
    buf_a[0] = state
    pl.semaphore_wait(barrier, count_a + count_b + count_c - 3)

    descs = start_ring(buf_a, send_a, recv_a, count_a, pos_a, dev_a)
    edge_a_c = slab_coefs(count_a, 1, pos_a, inv, block_len, modes)[4]
    edge_b_c = slab_coefs(count_b, count_a, pos_b, inv, block_len, modes)[4]
    levels_a = level_coefs(count_a, 1, inv, block_len, modes)
    levels_b = level_coefs(count_b, count_a, inv, block_len, modes)
    near_w = jnp.exp(-(pos_a * block_len).astype(jnp.float32) * inv)
    far_w = jnp.exp(-((count_a - 1 - pos_a) * block_len).astype(jnp.float32) * inv)
    join = jnp.where(slab == 0, near_w, jnp.where(slab == 2, far_w, 0.0))
    toep = jnp.where(lower, dot_nt(jnp.where(slab == 0, e_down * amp, 0.0), jnp.where(slab == 0, e_up, 0.0)), 0.0)
    into_f = jnp.where(slab == 0, e_next * amp, 0.0)
    into_b = jnp.where(slab == 2, jnp.exp(-(float(block_len) - offs) * inv) * amp, 0.0)
    items = finish_ring(descs, buf_a, count_a, pos_a)
    group, edge_a = fold_items(items, levels_a, edge_a_c, inv, modes)
    buf_b[0] = group
    descs = start_ring(buf_b, send_b, recv_b, count_b, pos_b, dev_b)
    conv = dot_nt(values, toep)
    corr = dot_nn(grad_mixed, toep)
    items = finish_ring(descs, buf_b, count_b, pos_b)
    total, edge_b = fold_items(items, levels_b, edge_b_c, inv, modes)
    buf_c[0] = total
    descs = start_ring(buf_c, send_c, recv_c, count_c, ch_index, dev_c)
    edge = join * edge_b + edge_a
    conv = conv + dot_nt(edge, into_f)
    corr = corr + dot_nt(edge, into_b)
    mixed_out = conv + gain * values
    grad_values = gain * grad_mixed + corr
    mix_ref[0] = mixed_out
    mix_ref[1] = grad_values
    items = finish_ring(descs, buf_c, count_c, ch_index)
    sums = items[0]
    for item in items[1:]:
        sums = sums + item
    small_ref[0] = total
    small_ref[1] = sums


def output_kernel(scales, x_ref, q_ref, k_ref, d_ref, mix_ref, small_ref, mem_ref, res_ref,
                  out_ref, gx_ref, gq_ref, gk_ref, skip_ref, gres_ref, gmem_ref):
    mixed_out = mix_ref[0]
    grad_values = mix_ref[1]
    out_ref[...] = (q_ref[...].astype(jnp.float32) * mixed_out).astype(jnp.bfloat16)
    gx_ref[...] = (grad_values * k_ref[...].astype(jnp.float32)).astype(jnp.bfloat16)
    gq_ref[...] = (d_ref[...].astype(jnp.float32) * mixed_out).astype(jnp.bfloat16)
    gk_ref[...] = (grad_values * x_ref[...].astype(jnp.float32)).astype(jnp.bfloat16)
    modes = mem_ref.shape[0]
    channels = small_ref.shape[1]
    norm_scale, seq_scale = scales
    mode_of = lax.broadcasted_iota(jnp.int32, (1, LANES), 1) % modes
    mem_v = jnp.ones((1, LANES), jnp.float32)
    res_v = jnp.zeros((1, LANES), jnp.float32)
    for mode in range(modes):
        mem_v = jnp.where(mode_of == mode, mem_ref[mode], mem_v)
        res_v = jnp.where(mode_of == mode, res_ref[mode], res_v)
    gain = jnp.sqrt(2.0 / mem_v)
    sums = small_ref[1][0:1]
    grad_res = pltpu.roll(gain * sums * norm_scale, LANES - 5 * modes, 1)
    grad_mem = pltpu.roll(res_v * gain * sums * norm_scale, LANES - 6 * modes, 1)
    column = small_ref[0][:, 7 * modes:7 * modes + 1]
    lane = lax.broadcasted_iota(jnp.int32, (channels, LANES), 1)
    row = lax.broadcasted_iota(jnp.int32, (channels, LANES), 0)
    skip = jnp.sum(jnp.where(lane == row, column, 0.0), axis=0, keepdims=True) * seq_scale
    gres_ref[...] = grad_res[:, 0:modes]
    gmem_ref[...] = grad_mem[:, 0:modes]
    skip_ref[...] = skip[:, 0:channels]


def per_device(signal_x, gate_q, gate_k, skip_gain, residue, memory, cotangent):
    channels, block_len = signal_x.shape
    modes = memory.shape[0]
    seq_total = lax.axis_size("seq") * block_len
    all_channels = channels * lax.axis_size("ch")
    count_a = min(GROUP, lax.axis_size("seq"))
    count_b = lax.axis_size("seq") // count_a
    count_c = lax.axis_size("ch")
    msg = (channels, LANES)
    vmem = pl.BlockSpec(memory_space=pltpu.VMEM)
    half = jax.ShapeDtypeStruct(signal_x.shape, jnp.bfloat16)
    mix, small = pl.pallas_call(
        functools.partial(fused_kernel, (count_a, count_b, count_c), modes),
        out_shape=(jax.ShapeDtypeStruct((2,) + signal_x.shape, jnp.float32),
                   jax.ShapeDtypeStruct((2,) + msg, jnp.float32)),
        in_specs=[vmem] * 4 + [pl.BlockSpec(memory_space=pltpu.SMEM)] * 3,
        out_specs=(vmem,) * 2,
        scratch_shapes=[
            pltpu.VMEM((count_a,) + msg, jnp.float32),
            pltpu.VMEM((count_b,) + msg, jnp.float32),
            pltpu.VMEM((count_c,) + msg, jnp.float32),
            pltpu.SemaphoreType.DMA((count_a,)),
            pltpu.SemaphoreType.DMA((count_a,)),
            pltpu.SemaphoreType.DMA((count_b,)),
            pltpu.SemaphoreType.DMA((count_b,)),
            pltpu.SemaphoreType.DMA((count_c,)),
            pltpu.SemaphoreType.DMA((count_c,)),
        ],
        compiler_params=pltpu.CompilerParams(collective_id=0, has_side_effects=True),
    )(signal_x, gate_q, gate_k, cotangent, memory, residue, skip_gain)
    norm_scale = 1.0 / math.sqrt(all_channels * seq_total)
    smem = pl.BlockSpec(memory_space=pltpu.SMEM)
    output, grad_x, grad_q, grad_k, grad_skip, grad_residue, grad_memory = pl.pallas_call(
        functools.partial(output_kernel, (norm_scale, 1.0 / math.sqrt(seq_total))),
        out_shape=(half, half, half, half, jax.ShapeDtypeStruct((1, channels), jnp.float32),
                   jax.ShapeDtypeStruct((1, modes), jnp.float32), jax.ShapeDtypeStruct((1, modes), jnp.float32)),
        in_specs=[vmem] * 6 + [smem] * 2,
        out_specs=(vmem,) * 7,
    )(signal_x, gate_q, gate_k, cotangent, mix, small, memory, residue)
    grad_skip = grad_skip.reshape(channels)
    grad_residue = grad_residue.reshape(modes)
    grad_memory = grad_memory.reshape(modes)
    return (output, grad_x, grad_q, grad_k, grad_skip, grad_residue, grad_memory)


def solution(mesh):
    return jax.shard_map(
        per_device,
        mesh=mesh,
        in_specs=(
            P("ch", "seq"),
            P("ch", "seq"),
            P("ch", "seq"),
            P("ch"),
            P(),
            P(),
            P("ch", "seq"),
        ),
        out_specs=(
            P("ch", "seq"),
            P("ch", "seq"),
            P("ch", "seq"),
            P("ch", "seq"),
            P("ch"),
            P(),
            P(),
        ),
        check_vma=False,
    )
```

```python
import functools
import math

import jax
import jax.numpy as jnp
from jax import lax
from jax.experimental import pallas as pl
from jax.experimental.pallas import tpu as pltpu
from jax.sharding import PartitionSpec as P

HIGH_PREC = lax.Precision.HIGHEST


def mm(pattern, left_op, right_op):
    return jnp.einsum(pattern, left_op, right_op, precision=HIGH_PREC)


GROUP = 8
LANES = 128
SLABS = 8


def row_sum(value):
    return jnp.sum(value, axis=0, keepdims=True)


def slab_coefs(count, size, pos, inv, block_len, modes):
    lane = lax.broadcasted_iota(jnp.int32, (count, LANES), 1) // modes
    index = lax.broadcasted_iota(jnp.int32, (count, LANES), 0)
    span = float(size * block_len)
    step = jnp.exp(-span * inv)
    starts = index.astype(jnp.float32) * span
    lag = jnp.exp(-starts * inv)
    before = jnp.where(index < pos, jnp.exp(-((pos - 1 - index).astype(jnp.float32) * span) * inv), 0.0)
    after = jnp.where(index > pos, jnp.exp(-((index - pos - 1).astype(jnp.float32) * span) * inv), 0.0)
    keep = jnp.where(lane <= 1, step, 1.0)[0:1]
    carry = jnp.where(lane == 1, step * span, 0.0)[0:1]
    take = jnp.where((lane >= 2) & (lane <= 4), lag, 1.0)
    shift = jnp.where(lane == 4, lag * starts * inv, 0.0)
    edge = jnp.where(lane == 0, before, jnp.where(lane == 2, after, 0.0))
    return keep, carry, take, shift, edge


def level_coefs(count, size, inv, block_len, modes):
    slab = lax.broadcasted_iota(jnp.int32, (1, LANES), 1) // modes
    levels = []
    width = size
    while width < count * size:
        span = float(width * block_len)
        step = jnp.exp(-span * inv)
        levels.append((
            jnp.where(slab <= 1, step, 1.0),
            jnp.where(slab == 1, step * span, 0.0),
            jnp.where((slab >= 2) & (slab <= 4), step, 1.0),
            jnp.where(slab == 4, step * span * inv, 0.0),
        ))
        width *= 2
    return levels


def combine_pair(left, right, coefs, inv, modes):
    keep, carry, take, shift = coefs
    slab = lax.broadcasted_iota(jnp.int32, (1, LANES), 1) // modes
    s1 = row_sum(pltpu.roll(left, 3 * modes, 1) * right)
    s2 = row_sum(pltpu.roll(left, 4 * modes, 1) * right)
    s3 = row_sum(pltpu.roll(left, 2 * modes, 1) * right)
    cross = jnp.where(slab == 5, pltpu.roll(s1, 2 * modes, 1), 0.0) + jnp.where(
        slab == 6, pltpu.roll(s2, 2 * modes, 1) + pltpu.roll(s3 * inv, 3 * modes, 1), 0.0)
    return (keep * left + take * right + carry * pltpu.roll(left, modes, 1)
            + shift * pltpu.roll(right, modes, 1) + cross)


def fold_items(items, levels, edge_c, inv, modes):
    edge = edge_c[0:1] * items[0]
    for index in range(1, len(items)):
        edge = edge + edge_c[index:index + 1] * items[index]
    layer = list(items)
    for coefs in levels:
        layer = [combine_pair(layer[i], layer[i + 1], coefs, inv, modes) for i in range(0, len(layer), 2)]
    return layer[0], edge


def start_ring(buf, send_sems, recv_sems, count, pos, device_of):
    descs = []
    for dist in range(1, count):
        desc = pltpu.make_async_remote_copy(
            src_ref=buf.at[0],
            dst_ref=buf.at[count - dist],
            send_sem=send_sems.at[dist],
            recv_sem=recv_sems.at[count - dist],
            device_id=device_of((pos + dist) % count),
            device_id_type=pl.DeviceIdType.MESH,
        )
        desc.start()
        descs.append(desc)
    return descs


def finish_ring(descs, buf, count, pos):
    for desc in descs:
        desc.wait_recv()
    return [buf[(slot - pos + count) % count] for slot in range(count)]


def dot_nn(left_op, right_op):
    return jnp.dot(left_op, right_op, precision=HIGH_PREC, preferred_element_type=jnp.float32)


def dot_nt(left_op, right_op):
    return lax.dot_general(left_op, right_op, (((1,), (1,)), ((), ())), precision=HIGH_PREC,
                           preferred_element_type=jnp.float32)


def dot_tn(left_op, right_op):
    return lax.dot_general(left_op, right_op, (((0,), (0,)), ((), ())), precision=HIGH_PREC,
                           preferred_element_type=jnp.float32)


def fused_kernel(counts, modes, x_ref, q_ref, k_ref, d_ref, mem_ref, res_ref, gain_ref,
                 mix_ref, small_ref,
                 buf_a, buf_b, buf_c, send_a, recv_a, send_b, recv_b, send_c, recv_c):
    count_a, count_b, count_c = counts
    channels, block_len = x_ref.shape
    seq_index = lax.axis_index("seq")
    ch_index = lax.axis_index("ch")
    pos_a = seq_index % count_a
    pos_b = seq_index // count_a

    def dev_a(other):
        return (pos_b * count_a + other, ch_index)

    def dev_b(other):
        return (other * count_a + pos_a, ch_index)

    def dev_c(other):
        return (seq_index, other)

    barrier = pltpu.get_barrier_semaphore()
    for count, pos, device_of in ((count_a, pos_a, dev_a), (count_b, pos_b, dev_b), (count_c, ch_index, dev_c)):
        for dist in range(1, count):
            pl.semaphore_signal(barrier, inc=1, device_id=device_of((pos + dist) % count),
                                device_id_type=pl.DeviceIdType.MESH)

    slab = lax.broadcasted_iota(jnp.int32, (1, LANES), 1) // modes
    mode_of = lax.broadcasted_iota(jnp.int32, (1, LANES), 1) % modes
    mem_v = jnp.zeros((1, LANES), jnp.float32)
    res_v = jnp.zeros((1, LANES), jnp.float32)
    for mode in range(modes):
        mem_v = jnp.where(mode_of == mode, mem_ref[mode], mem_v)
        res_v = jnp.where(mode_of == mode, res_ref[mode], res_v)
    inv = 1.0 / mem_v
    amp = res_v * jnp.sqrt(2.0 * inv)
    chan_of = lax.broadcasted_iota(jnp.int32, (channels, 1), 0)
    gain = jnp.zeros((channels, 1), jnp.float32)
    for chan in range(channels):
        gain = jnp.where(chan_of == chan, gain_ref[chan], gain)
    offs = lax.broadcasted_iota(jnp.int32, (block_len, LANES), 0).astype(jnp.float32)
    back = float(block_len - 1) - offs
    e_down = jnp.exp(-offs * inv)
    e_tail = jnp.exp(-back * inv)
    e_next = jnp.exp(-(offs + 1.0) * inv)
    e_up = jnp.exp(offs * inv)
    right_v = jnp.where(slab == 0, e_tail, jnp.where(slab == 1, e_tail * back, 0.0))
    right_g = jnp.where(slab == 2, e_down, jnp.where(slab == 3, e_next, jnp.where(
        slab == 4, e_next * ((offs + 1.0) * inv - 0.5), 0.0)))
    right_r = jnp.where(slab == 5, e_up, jnp.where(slab == 6, e_up * offs * inv, 0.0))

    x_float = x_ref[...].astype(jnp.float32)
    q_float = q_ref[...].astype(jnp.float32)
    k_float = k_ref[...].astype(jnp.float32)
    d_float = d_ref[...].astype(jnp.float32)
    values = x_float * k_float
    grad_mixed = d_float * q_float
    row_t = lax.broadcasted_iota(jnp.int32, (block_len, block_len), 0)
    col_s = lax.broadcasted_iota(jnp.int32, (block_len, block_len), 1)
    lower = row_t >= col_s
    pair = jnp.where(lower, dot_tn(grad_mixed, values), 0.0)
    near = dot_nn(pair, right_r)
    terms = jnp.where(slab == 5, e_down * near, jnp.where(
        slab == 6, e_down * ((offs * inv - 0.5) * pltpu.roll(near, modes, 1) - near), 0.0))
    local = row_sum(terms)
    skip = jnp.sum(grad_mixed * values, axis=1, keepdims=True)
    state = dot_nn(values, right_v) + dot_nn(grad_mixed, right_g) + jnp.where(slab == 7, skip, local)
    buf_a[0] = state
    pl.semaphore_wait(barrier, count_a + count_b + count_c - 3)

    descs = start_ring(buf_a, send_a, recv_a, count_a, pos_a, dev_a)
    sent = list(descs)
    edge_a_c = slab_coefs(count_a, 1, pos_a, inv, block_len, modes)[4]
    edge_b_c = slab_coefs(count_b, count_a, pos_b, inv, block_len, modes)[4]
    levels_a = level_coefs(count_a, 1, inv, block_len, modes)
    levels_b = level_coefs(count_b, count_a, inv, block_len, modes)
    near_w = jnp.exp(-(pos_a * block_len).astype(jnp.float32) * inv)
    far_w = jnp.exp(-((count_a - 1 - pos_a) * block_len).astype(jnp.float32) * inv)
    join = jnp.where(slab == 0, near_w, jnp.where(slab == 2, far_w, 0.0))
    toep = jnp.where(lower, dot_nt(jnp.where(slab == 0, e_down * amp, 0.0), jnp.where(slab == 0, e_up, 0.0)), 0.0)
    into_f = jnp.where(slab == 0, e_next * amp, 0.0)
    into_b = jnp.where(slab == 2, jnp.exp(-(float(block_len) - offs) * inv) * amp, 0.0)
    items = finish_ring(descs, buf_a, count_a, pos_a)
    group, edge_a = fold_items(items, levels_a, edge_a_c, inv, modes)
    buf_b[0] = group
    descs = start_ring(buf_b, send_b, recv_b, count_b, pos_b, dev_b)
    sent += descs
    conv = dot_nt(values, toep)
    corr = dot_nn(grad_mixed, toep)
    items = finish_ring(descs, buf_b, count_b, pos_b)
    total, edge_b = fold_items(items, levels_b, edge_b_c, inv, modes)
    buf_c[0] = total
    descs = start_ring(buf_c, send_c, recv_c, count_c, ch_index, dev_c)
    sent += descs
    edge = join * edge_b + edge_a
    conv = conv + dot_nt(edge, into_f)
    corr = corr + dot_nt(edge, into_b)
    mixed_out = conv + gain * values
    grad_values = gain * grad_mixed + corr
    mix_ref[0] = mixed_out
    mix_ref[1] = grad_values
    items = finish_ring(descs, buf_c, count_c, ch_index)
    sums = items[0]
    for item in items[1:]:
        sums = sums + item
    small_ref[0] = total
    small_ref[1] = sums
    for desc in sent:
        desc.wait_send()


def output_kernel(scales, x_ref, q_ref, k_ref, d_ref, mix_ref, small_ref, mem_ref, res_ref,
                  out_ref, gx_ref, gq_ref, gk_ref, skip_ref, gres_ref, gmem_ref):
    mixed_out = mix_ref[0]
    grad_values = mix_ref[1]
    out_ref[...] = (q_ref[...].astype(jnp.float32) * mixed_out).astype(jnp.bfloat16)
    gx_ref[...] = (grad_values * k_ref[...].astype(jnp.float32)).astype(jnp.bfloat16)
    gq_ref[...] = (d_ref[...].astype(jnp.float32) * mixed_out).astype(jnp.bfloat16)
    gk_ref[...] = (grad_values * x_ref[...].astype(jnp.float32)).astype(jnp.bfloat16)
    modes = mem_ref.shape[0]
    channels = small_ref.shape[1]
    norm_scale, seq_scale = scales
    mode_of = lax.broadcasted_iota(jnp.int32, (1, LANES), 1) % modes
    mem_v = jnp.ones((1, LANES), jnp.float32)
    res_v = jnp.zeros((1, LANES), jnp.float32)
    for mode in range(modes):
        mem_v = jnp.where(mode_of == mode, mem_ref[mode], mem_v)
        res_v = jnp.where(mode_of == mode, res_ref[mode], res_v)
    gain = jnp.sqrt(2.0 / mem_v)
    sums = small_ref[1][0:1]
    grad_res = pltpu.roll(gain * sums * norm_scale, LANES - 5 * modes, 1)
    grad_mem = pltpu.roll(res_v * gain * sums * norm_scale, LANES - 6 * modes, 1)
    column = small_ref[0][:, 7 * modes:7 * modes + 1]
    lane = lax.broadcasted_iota(jnp.int32, (channels, LANES), 1)
    row = lax.broadcasted_iota(jnp.int32, (channels, LANES), 0)
    skip = jnp.sum(jnp.where(lane == row, column, 0.0), axis=0, keepdims=True) * seq_scale
    gres_ref[...] = grad_res[:, 0:modes]
    gmem_ref[...] = grad_mem[:, 0:modes]
    skip_ref[...] = skip[:, 0:channels]


def per_device(signal_x, gate_q, gate_k, skip_gain, residue, memory, cotangent):
    channels, block_len = signal_x.shape
    modes = memory.shape[0]
    seq_total = lax.axis_size("seq") * block_len
    all_channels = channels * lax.axis_size("ch")
    count_a = min(GROUP, lax.axis_size("seq"))
    count_b = lax.axis_size("seq") // count_a
    count_c = lax.axis_size("ch")
    msg = (channels, LANES)
    vmem = pl.BlockSpec(memory_space=pltpu.VMEM)
    half = jax.ShapeDtypeStruct(signal_x.shape, jnp.bfloat16)
    mix, small = pl.pallas_call(
        functools.partial(fused_kernel, (count_a, count_b, count_c), modes),
        out_shape=(jax.ShapeDtypeStruct((2,) + signal_x.shape, jnp.float32),
                   jax.ShapeDtypeStruct((2,) + msg, jnp.float32)),
        in_specs=[vmem] * 4 + [pl.BlockSpec(memory_space=pltpu.SMEM)] * 3,
        out_specs=(vmem,) * 2,
        scratch_shapes=[
            pltpu.VMEM((count_a,) + msg, jnp.float32),
            pltpu.VMEM((count_b,) + msg, jnp.float32),
            pltpu.VMEM((count_c,) + msg, jnp.float32),
            pltpu.SemaphoreType.DMA((count_a,)),
            pltpu.SemaphoreType.DMA((count_a,)),
            pltpu.SemaphoreType.DMA((count_b,)),
            pltpu.SemaphoreType.DMA((count_b,)),
            pltpu.SemaphoreType.DMA((count_c,)),
            pltpu.SemaphoreType.DMA((count_c,)),
        ],
        compiler_params=pltpu.CompilerParams(collective_id=0, has_side_effects=True),
    )(signal_x, gate_q, gate_k, cotangent, memory, residue, skip_gain)
    norm_scale = 1.0 / math.sqrt(all_channels * seq_total)
    smem = pl.BlockSpec(memory_space=pltpu.SMEM)
    output, grad_x, grad_q, grad_k, grad_skip, grad_residue, grad_memory = pl.pallas_call(
        functools.partial(output_kernel, (norm_scale, 1.0 / math.sqrt(seq_total))),
        out_shape=(half, half, half, half, jax.ShapeDtypeStruct((1, channels), jnp.float32),
                   jax.ShapeDtypeStruct((1, modes), jnp.float32), jax.ShapeDtypeStruct((1, modes), jnp.float32)),
        in_specs=[vmem] * 6 + [smem] * 2,
        out_specs=(vmem,) * 7,
    )(signal_x, gate_q, gate_k, cotangent, mix, small, memory, residue)
    grad_skip = grad_skip.reshape(channels)
    grad_residue = grad_residue.reshape(modes)
    grad_memory = grad_memory.reshape(modes)
    return (output, grad_x, grad_q, grad_k, grad_skip, grad_residue, grad_memory)


def solution(mesh):
    return jax.shard_map(
        per_device,
        mesh=mesh,
        in_specs=(
            P("ch", "seq"),
            P("ch", "seq"),
            P("ch", "seq"),
            P("ch"),
            P(),
            P(),
            P("ch", "seq"),
        ),
        out_specs=(
            P("ch", "seq"),
            P("ch", "seq"),
            P("ch", "seq"),
            P("ch", "seq"),
            P("ch"),
            P(),
            P(),
        ),
        check_vma=False,
    )
```

```python
import functools
import math

import jax
import jax.numpy as jnp
from jax import lax
from jax.experimental import pallas as pl
from jax.experimental.pallas import tpu as pltpu
from jax.sharding import PartitionSpec as P

HIGH_PREC = lax.Precision.HIGHEST


def mm(pattern, left_op, right_op):
    return jnp.einsum(pattern, left_op, right_op, precision=HIGH_PREC)


GROUP = 8
LANES = 128
SLABS = 8


def row_sum(value):
    return jnp.sum(value, axis=0, keepdims=True)


def slab_coefs(count, size, pos, inv, block_len, modes):
    lane = lax.broadcasted_iota(jnp.int32, (count, LANES), 1) // modes
    index = lax.broadcasted_iota(jnp.int32, (count, LANES), 0)
    span = float(size * block_len)
    step = jnp.exp(-span * inv)
    starts = index.astype(jnp.float32) * span
    lag = jnp.exp(-starts * inv)
    before = jnp.where(index < pos, jnp.exp(-((pos - 1 - index).astype(jnp.float32) * span) * inv), 0.0)
    after = jnp.where(index > pos, jnp.exp(-((index - pos - 1).astype(jnp.float32) * span) * inv), 0.0)
    keep = jnp.where(lane <= 1, step, 1.0)[0:1]
    carry = jnp.where(lane == 1, step * span, 0.0)[0:1]
    take = jnp.where((lane >= 2) & (lane <= 4), lag, 1.0)
    shift = jnp.where(lane == 4, lag * starts * inv, 0.0)
    edge = jnp.where(lane == 0, before, jnp.where(lane == 2, after, 0.0))
    return keep, carry, take, shift, edge


def level_coefs(count, size, inv, block_len, modes):
    slab = lax.broadcasted_iota(jnp.int32, (1, LANES), 1) // modes
    levels = []
    width = size
    while width < count * size:
        span = float(width * block_len)
        step = jnp.exp(-span * inv)
        levels.append((
            jnp.where(slab <= 1, step, 1.0),
            jnp.where(slab == 1, step * span, 0.0),
            jnp.where((slab >= 2) & (slab <= 4), step, 1.0),
            jnp.where(slab == 4, step * span * inv, 0.0),
        ))
        width *= 2
    return levels


def combine_pair(left, right, coefs, inv, modes):
    keep, carry, take, shift = coefs
    slab = lax.broadcasted_iota(jnp.int32, (1, LANES), 1) // modes
    s1 = row_sum(pltpu.roll(left, 3 * modes, 1) * right)
    s2 = row_sum(pltpu.roll(left, 4 * modes, 1) * right)
    s3 = row_sum(pltpu.roll(left, 2 * modes, 1) * right)
    cross = jnp.where(slab == 5, pltpu.roll(s1, 2 * modes, 1), 0.0) + jnp.where(
        slab == 6, pltpu.roll(s2, 2 * modes, 1) + pltpu.roll(s3 * inv, 3 * modes, 1), 0.0)
    return (keep * left + take * right + carry * pltpu.roll(left, modes, 1)
            + shift * pltpu.roll(right, modes, 1) + cross)


def fold_items(items, levels, edge_c, inv, modes):
    edge = edge_c[0:1] * items[0]
    for index in range(1, len(items)):
        edge = edge + edge_c[index:index + 1] * items[index]
    layer = list(items)
    for coefs in levels:
        layer = [combine_pair(layer[i], layer[i + 1], coefs, inv, modes) for i in range(0, len(layer), 2)]
    return layer[0], edge


def start_ring(buf, send_sems, recv_sems, count, pos, device_of):
    descs = []
    for dist in sorted(range(1, count), key=lambda d: -min(d, count - d)):
        desc = pltpu.make_async_remote_copy(
            src_ref=buf.at[0],
            dst_ref=buf.at[count - dist],
            send_sem=send_sems.at[dist],
            recv_sem=recv_sems.at[count - dist],
            device_id=device_of((pos + dist) % count),
            device_id_type=pl.DeviceIdType.MESH,
        )
        desc.start()
        descs.append(desc)
    return descs


def finish_ring(descs, buf, count, pos):
    for desc in descs:
        desc.wait_recv()
    return [buf[(slot - pos + count) % count] for slot in range(count)]


def dot_nn(left_op, right_op):
    return jnp.dot(left_op, right_op, precision=HIGH_PREC, preferred_element_type=jnp.float32)


def dot_nt(left_op, right_op):
    return lax.dot_general(left_op, right_op, (((1,), (1,)), ((), ())), precision=HIGH_PREC,
                           preferred_element_type=jnp.float32)


def dot_tn(left_op, right_op):
    return lax.dot_general(left_op, right_op, (((0,), (0,)), ((), ())), precision=HIGH_PREC,
                           preferred_element_type=jnp.float32)


def fused_kernel(counts, modes, x_ref, q_ref, k_ref, d_ref, mem_ref, res_ref, gain_ref,
                 mix_ref, small_ref,
                 buf_a, buf_b, buf_c, send_a, recv_a, send_b, recv_b, send_c, recv_c):
    count_a, count_b, count_c = counts
    channels, block_len = x_ref.shape
    seq_index = lax.axis_index("seq")
    ch_index = lax.axis_index("ch")
    pos_a = seq_index % count_a
    pos_b = seq_index // count_a

    def dev_a(other):
        return (pos_b * count_a + other, ch_index)

    def dev_b(other):
        return (other * count_a + pos_a, ch_index)

    def dev_c(other):
        return (seq_index, other)

    barrier = pltpu.get_barrier_semaphore()
    for count, pos, device_of in ((count_a, pos_a, dev_a), (count_b, pos_b, dev_b), (count_c, ch_index, dev_c)):
        for dist in range(1, count):
            pl.semaphore_signal(barrier, inc=1, device_id=device_of((pos + dist) % count),
                                device_id_type=pl.DeviceIdType.MESH)

    slab = lax.broadcasted_iota(jnp.int32, (1, LANES), 1) // modes
    mode_of = lax.broadcasted_iota(jnp.int32, (1, LANES), 1) % modes
    mem_v = jnp.zeros((1, LANES), jnp.float32)
    res_v = jnp.zeros((1, LANES), jnp.float32)
    for mode in range(modes):
        mem_v = jnp.where(mode_of == mode, mem_ref[mode], mem_v)
        res_v = jnp.where(mode_of == mode, res_ref[mode], res_v)
    inv = 1.0 / mem_v
    amp = res_v * jnp.sqrt(2.0 * inv)
    chan_of = lax.broadcasted_iota(jnp.int32, (channels, 1), 0)
    gain = jnp.zeros((channels, 1), jnp.float32)
    for chan in range(channels):
        gain = jnp.where(chan_of == chan, gain_ref[chan], gain)
    offs = lax.broadcasted_iota(jnp.int32, (block_len, LANES), 0).astype(jnp.float32)
    back = float(block_len - 1) - offs
    e_down = jnp.exp(-offs * inv)
    e_tail = jnp.exp(-back * inv)
    e_next = jnp.exp(-(offs + 1.0) * inv)
    e_up = jnp.exp(offs * inv)
    right_v = jnp.where(slab == 0, e_tail, jnp.where(slab == 1, e_tail * back, 0.0))
    right_g = jnp.where(slab == 2, e_down, jnp.where(slab == 3, e_next, jnp.where(
        slab == 4, e_next * ((offs + 1.0) * inv - 0.5), 0.0)))
    right_r = jnp.where(slab == 5, e_up, jnp.where(slab == 6, e_up * offs * inv, 0.0))

    x_float = x_ref[...].astype(jnp.float32)
    q_float = q_ref[...].astype(jnp.float32)
    k_float = k_ref[...].astype(jnp.float32)
    d_float = d_ref[...].astype(jnp.float32)
    values = x_float * k_float
    grad_mixed = d_float * q_float
    row_t = lax.broadcasted_iota(jnp.int32, (block_len, block_len), 0)
    col_s = lax.broadcasted_iota(jnp.int32, (block_len, block_len), 1)
    lower = row_t >= col_s
    pair = jnp.where(lower, dot_tn(grad_mixed, values), 0.0)
    near = dot_nn(pair, right_r)
    terms = jnp.where(slab == 5, e_down * near, jnp.where(
        slab == 6, e_down * ((offs * inv - 0.5) * pltpu.roll(near, modes, 1) - near), 0.0))
    local = row_sum(terms)
    skip = jnp.sum(grad_mixed * values, axis=1, keepdims=True)
    state = dot_nn(values, right_v) + dot_nn(grad_mixed, right_g) + jnp.where(slab == 7, skip, local)
    buf_a[0] = state
    pl.semaphore_wait(barrier, count_a + count_b + count_c - 3)

    descs = start_ring(buf_a, send_a, recv_a, count_a, pos_a, dev_a)
    sent = list(descs)
    edge_a_c = slab_coefs(count_a, 1, pos_a, inv, block_len, modes)[4]
    edge_b_c = slab_coefs(count_b, count_a, pos_b, inv, block_len, modes)[4]
    levels_a = level_coefs(count_a, 1, inv, block_len, modes)
    levels_b = level_coefs(count_b, count_a, inv, block_len, modes)
    near_w = jnp.exp(-(pos_a * block_len).astype(jnp.float32) * inv)
    far_w = jnp.exp(-((count_a - 1 - pos_a) * block_len).astype(jnp.float32) * inv)
    join = jnp.where(slab == 0, near_w, jnp.where(slab == 2, far_w, 0.0))
    toep = jnp.where(lower, dot_nt(jnp.where(slab == 0, e_down * amp, 0.0), jnp.where(slab == 0, e_up, 0.0)), 0.0)
    into_f = jnp.where(slab == 0, e_next * amp, 0.0)
    into_b = jnp.where(slab == 2, jnp.exp(-(float(block_len) - offs) * inv) * amp, 0.0)
    items = finish_ring(descs, buf_a, count_a, pos_a)
    group, edge_a = fold_items(items, levels_a, edge_a_c, inv, modes)
    buf_b[0] = group
    descs = start_ring(buf_b, send_b, recv_b, count_b, pos_b, dev_b)
    sent += descs
    conv = dot_nt(values, toep)
    corr = dot_nn(grad_mixed, toep)
    items = finish_ring(descs, buf_b, count_b, pos_b)
    total, edge_b = fold_items(items, levels_b, edge_b_c, inv, modes)
    buf_c[0] = total
    descs = start_ring(buf_c, send_c, recv_c, count_c, ch_index, dev_c)
    sent += descs
    edge = join * edge_b + edge_a
    conv = conv + dot_nt(edge, into_f)
    corr = corr + dot_nt(edge, into_b)
    mixed_out = conv + gain * values
    grad_values = gain * grad_mixed + corr
    mix_ref[0] = mixed_out
    mix_ref[1] = grad_values
    items = finish_ring(descs, buf_c, count_c, ch_index)
    sums = items[0]
    for item in items[1:]:
        sums = sums + item
    small_ref[0] = total
    small_ref[1] = sums
    for desc in sent:
        desc.wait_send()


def output_kernel(scales, x_ref, q_ref, k_ref, d_ref, mix_ref, small_ref, mem_ref, res_ref,
                  out_ref, gx_ref, gq_ref, gk_ref, skip_ref, gres_ref, gmem_ref):
    mixed_out = mix_ref[0]
    grad_values = mix_ref[1]
    out_ref[...] = (q_ref[...].astype(jnp.float32) * mixed_out).astype(jnp.bfloat16)
    gx_ref[...] = (grad_values * k_ref[...].astype(jnp.float32)).astype(jnp.bfloat16)
    gq_ref[...] = (d_ref[...].astype(jnp.float32) * mixed_out).astype(jnp.bfloat16)
    gk_ref[...] = (grad_values * x_ref[...].astype(jnp.float32)).astype(jnp.bfloat16)
    modes = mem_ref.shape[0]
    channels = small_ref.shape[1]
    norm_scale, seq_scale = scales
    mode_of = lax.broadcasted_iota(jnp.int32, (1, LANES), 1) % modes
    mem_v = jnp.ones((1, LANES), jnp.float32)
    res_v = jnp.zeros((1, LANES), jnp.float32)
    for mode in range(modes):
        mem_v = jnp.where(mode_of == mode, mem_ref[mode], mem_v)
        res_v = jnp.where(mode_of == mode, res_ref[mode], res_v)
    gain = jnp.sqrt(2.0 / mem_v)
    sums = small_ref[1][0:1]
    grad_res = pltpu.roll(gain * sums * norm_scale, LANES - 5 * modes, 1)
    grad_mem = pltpu.roll(res_v * gain * sums * norm_scale, LANES - 6 * modes, 1)
    column = small_ref[0][:, 7 * modes:7 * modes + 1]
    lane = lax.broadcasted_iota(jnp.int32, (channels, LANES), 1)
    row = lax.broadcasted_iota(jnp.int32, (channels, LANES), 0)
    skip = jnp.sum(jnp.where(lane == row, column, 0.0), axis=0, keepdims=True) * seq_scale
    gres_ref[...] = grad_res[:, 0:modes]
    gmem_ref[...] = grad_mem[:, 0:modes]
    skip_ref[...] = skip[:, 0:channels]


def per_device(signal_x, gate_q, gate_k, skip_gain, residue, memory, cotangent):
    channels, block_len = signal_x.shape
    modes = memory.shape[0]
    seq_total = lax.axis_size("seq") * block_len
    all_channels = channels * lax.axis_size("ch")
    count_a = min(GROUP, lax.axis_size("seq"))
    count_b = lax.axis_size("seq") // count_a
    count_c = lax.axis_size("ch")
    msg = (channels, LANES)
    vmem = pl.BlockSpec(memory_space=pltpu.VMEM)
    half = jax.ShapeDtypeStruct(signal_x.shape, jnp.bfloat16)
    mix, small = pl.pallas_call(
        functools.partial(fused_kernel, (count_a, count_b, count_c), modes),
        out_shape=(jax.ShapeDtypeStruct((2,) + signal_x.shape, jnp.float32),
                   jax.ShapeDtypeStruct((2,) + msg, jnp.float32)),
        in_specs=[vmem] * 4 + [pl.BlockSpec(memory_space=pltpu.SMEM)] * 3,
        out_specs=(vmem,) * 2,
        scratch_shapes=[
            pltpu.VMEM((count_a,) + msg, jnp.float32),
            pltpu.VMEM((count_b,) + msg, jnp.float32),
            pltpu.VMEM((count_c,) + msg, jnp.float32),
            pltpu.SemaphoreType.DMA((count_a,)),
            pltpu.SemaphoreType.DMA((count_a,)),
            pltpu.SemaphoreType.DMA((count_b,)),
            pltpu.SemaphoreType.DMA((count_b,)),
            pltpu.SemaphoreType.DMA((count_c,)),
            pltpu.SemaphoreType.DMA((count_c,)),
        ],
        compiler_params=pltpu.CompilerParams(collective_id=0, has_side_effects=True),
    )(signal_x, gate_q, gate_k, cotangent, memory, residue, skip_gain)
    norm_scale = 1.0 / math.sqrt(all_channels * seq_total)
    smem = pl.BlockSpec(memory_space=pltpu.SMEM)
    output, grad_x, grad_q, grad_k, grad_skip, grad_residue, grad_memory = pl.pallas_call(
        functools.partial(output_kernel, (norm_scale, 1.0 / math.sqrt(seq_total))),
        out_shape=(half, half, half, half, jax.ShapeDtypeStruct((1, channels), jnp.float32),
                   jax.ShapeDtypeStruct((1, modes), jnp.float32), jax.ShapeDtypeStruct((1, modes), jnp.float32)),
        in_specs=[vmem] * 6 + [smem] * 2,
        out_specs=(vmem,) * 7,
    )(signal_x, gate_q, gate_k, cotangent, mix, small, memory, residue)
    grad_skip = grad_skip.reshape(channels)
    grad_residue = grad_residue.reshape(modes)
    grad_memory = grad_memory.reshape(modes)
    return (output, grad_x, grad_q, grad_k, grad_skip, grad_residue, grad_memory)


def solution(mesh):
    return jax.shard_map(
        per_device,
        mesh=mesh,
        in_specs=(
            P("ch", "seq"),
            P("ch", "seq"),
            P("ch", "seq"),
            P("ch"),
            P(),
            P(),
            P("ch", "seq"),
        ),
        out_specs=(
            P("ch", "seq"),
            P("ch", "seq"),
            P("ch", "seq"),
            P("ch", "seq"),
            P("ch"),
            P(),
            P(),
        ),
        check_vma=False,
    )
```

```python
import functools
import math

import jax
import jax.numpy as jnp
from jax import lax
from jax.experimental import pallas as pl
from jax.experimental.pallas import tpu as pltpu
from jax.sharding import PartitionSpec as P

HIGH_PREC = lax.Precision.HIGHEST


def mm(pattern, left_op, right_op):
    return jnp.einsum(pattern, left_op, right_op, precision=HIGH_PREC)


GROUP = 8
LANES = 128
SLABS = 8


def row_sum(value):
    return jnp.sum(value, axis=0, keepdims=True)


def slab_coefs(count, size, pos, inv, block_len, modes):
    lane = lax.broadcasted_iota(jnp.int32, (count, LANES), 1) // modes
    index = lax.broadcasted_iota(jnp.int32, (count, LANES), 0)
    span = float(size * block_len)
    step = jnp.exp(-span * inv)
    starts = index.astype(jnp.float32) * span
    lag = jnp.exp(-starts * inv)
    before = jnp.where(index < pos, jnp.exp(-((pos - 1 - index).astype(jnp.float32) * span) * inv), 0.0)
    after = jnp.where(index > pos, jnp.exp(-((index - pos - 1).astype(jnp.float32) * span) * inv), 0.0)
    keep = jnp.where(lane <= 1, step, 1.0)[0:1]
    carry = jnp.where(lane == 1, step * span, 0.0)[0:1]
    take = jnp.where((lane >= 2) & (lane <= 4), lag, 1.0)
    shift = jnp.where(lane == 4, lag * starts * inv, 0.0)
    edge = jnp.where(lane == 0, before, jnp.where(lane == 2, after, 0.0))
    return keep, carry, take, shift, edge


def level_coefs(count, size, inv, block_len, modes):
    slab = lax.broadcasted_iota(jnp.int32, (1, LANES), 1) // modes
    levels = []
    width = size
    while width < count * size:
        span = float(width * block_len)
        step = jnp.exp(-span * inv)
        levels.append((
            jnp.where(slab <= 1, step, 1.0),
            jnp.where(slab == 1, step * span, 0.0),
            jnp.where((slab >= 2) & (slab <= 4), step, 1.0),
            jnp.where(slab == 4, step * span * inv, 0.0),
        ))
        width *= 2
    return levels


def combine_pair(left, right, coefs, inv, modes):
    keep, carry, take, shift = coefs
    slab = lax.broadcasted_iota(jnp.int32, (1, LANES), 1) // modes
    s1 = row_sum(pltpu.roll(left, 3 * modes, 1) * right)
    s2 = row_sum(pltpu.roll(left, 4 * modes, 1) * right)
    s3 = row_sum(pltpu.roll(left, 2 * modes, 1) * right)
    cross = jnp.where(slab == 5, pltpu.roll(s1, 2 * modes, 1), 0.0) + jnp.where(
        slab == 6, pltpu.roll(s2, 2 * modes, 1) + pltpu.roll(s3 * inv, 3 * modes, 1), 0.0)
    return (keep * left + take * right + carry * pltpu.roll(left, modes, 1)
            + shift * pltpu.roll(right, modes, 1) + cross)


def fold_items(items, levels, edge_c, inv, modes):
    edge = edge_c[0:1] * items[0]
    for index in range(1, len(items)):
        edge = edge + edge_c[index:index + 1] * items[index]
    layer = list(items)
    for coefs in levels:
        layer = [combine_pair(layer[i], layer[i + 1], coefs, inv, modes) for i in range(0, len(layer), 2)]
    return layer[0], edge


def start_ring(buf, send_sems, recv_sems, count, pos, device_of):
    descs = []
    for dist in sorted(range(1, count), key=lambda d: -min(d, count - d)):
        desc = pltpu.make_async_remote_copy(
            src_ref=buf.at[0],
            dst_ref=buf.at[count - dist],
            send_sem=send_sems.at[dist],
            recv_sem=recv_sems.at[count - dist],
            device_id=device_of((pos + dist) % count),
            device_id_type=pl.DeviceIdType.MESH,
        )
        desc.start()
        descs.append(desc)
    return descs


def finish_ring(descs, buf, count, pos):
    for desc in descs:
        desc.wait_recv()
    return [buf[(slot - pos + count) % count] for slot in range(count)]


def dot_nn(left_op, right_op):
    return jnp.dot(left_op, right_op, precision=HIGH_PREC, preferred_element_type=jnp.float32)


def dot_nt(left_op, right_op):
    return lax.dot_general(left_op, right_op, (((1,), (1,)), ((), ())), precision=HIGH_PREC,
                           preferred_element_type=jnp.float32)


def dot_tn(left_op, right_op):
    return lax.dot_general(left_op, right_op, (((0,), (0,)), ((), ())), precision=HIGH_PREC,
                           preferred_element_type=jnp.float32)


def fused_kernel(counts, modes, x_ref, q_ref, k_ref, d_ref, mem_ref, res_ref, gain_ref,
                 mix_ref, small_ref,
                 buf_a, buf_b, buf_c, send_a, recv_a, send_b, recv_b, send_c, recv_c):
    count_a, count_b, count_c = counts
    channels, block_len = x_ref.shape
    seq_index = lax.axis_index("seq")
    ch_index = lax.axis_index("ch")
    pos_a = seq_index % count_a
    pos_b = seq_index // count_a

    def dev_a(other):
        return (pos_b * count_a + other, ch_index)

    def dev_b(other):
        return (other * count_a + pos_a, ch_index)

    def dev_c(other):
        return (seq_index, other)

    barrier = pltpu.get_barrier_semaphore()
    for count, pos, device_of in ((count_b, pos_b, dev_b), (count_a, pos_a, dev_a), (count_c, ch_index, dev_c)):
        for dist in sorted(range(1, count), key=lambda d: -min(d, count - d)):
            pl.semaphore_signal(barrier, inc=1, device_id=device_of((pos + dist) % count),
                                device_id_type=pl.DeviceIdType.MESH)

    slab = lax.broadcasted_iota(jnp.int32, (1, LANES), 1) // modes
    mode_of = lax.broadcasted_iota(jnp.int32, (1, LANES), 1) % modes
    mem_v = jnp.zeros((1, LANES), jnp.float32)
    res_v = jnp.zeros((1, LANES), jnp.float32)
    for mode in range(modes):
        mem_v = jnp.where(mode_of == mode, mem_ref[mode], mem_v)
        res_v = jnp.where(mode_of == mode, res_ref[mode], res_v)
    inv = 1.0 / mem_v
    amp = res_v * jnp.sqrt(2.0 * inv)
    chan_of = lax.broadcasted_iota(jnp.int32, (channels, 1), 0)
    gain = jnp.zeros((channels, 1), jnp.float32)
    for chan in range(channels):
        gain = jnp.where(chan_of == chan, gain_ref[chan], gain)
    offs = lax.broadcasted_iota(jnp.int32, (block_len, LANES), 0).astype(jnp.float32)
    back = float(block_len - 1) - offs
    e_down = jnp.exp(-offs * inv)
    e_tail = jnp.exp(-back * inv)
    e_next = jnp.exp(-(offs + 1.0) * inv)
    e_up = jnp.exp(offs * inv)
    right_v = jnp.where(slab == 0, e_tail, jnp.where(slab == 1, e_tail * back, 0.0))
    right_g = jnp.where(slab == 2, e_down, jnp.where(slab == 3, e_next, jnp.where(
        slab == 4, e_next * ((offs + 1.0) * inv - 0.5), 0.0)))
    right_r = jnp.where(slab == 5, e_up, jnp.where(slab == 6, e_up * offs * inv, 0.0))

    x_float = x_ref[...].astype(jnp.float32)
    q_float = q_ref[...].astype(jnp.float32)
    k_float = k_ref[...].astype(jnp.float32)
    d_float = d_ref[...].astype(jnp.float32)
    values = x_float * k_float
    grad_mixed = d_float * q_float
    row_t = lax.broadcasted_iota(jnp.int32, (block_len, block_len), 0)
    col_s = lax.broadcasted_iota(jnp.int32, (block_len, block_len), 1)
    lower = row_t >= col_s
    pair = jnp.where(lower, dot_tn(grad_mixed, values), 0.0)
    near = dot_nn(pair, right_r)
    terms = jnp.where(slab == 5, e_down * near, jnp.where(
        slab == 6, e_down * ((offs * inv - 0.5) * pltpu.roll(near, modes, 1) - near), 0.0))
    local = row_sum(terms)
    skip = jnp.sum(grad_mixed * values, axis=1, keepdims=True)
    state = dot_nn(values, right_v) + dot_nn(grad_mixed, right_g) + jnp.where(slab == 7, skip, local)
    buf_a[0] = state
    pl.semaphore_wait(barrier, count_a + count_b + count_c - 3)

    descs = start_ring(buf_a, send_a, recv_a, count_a, pos_a, dev_a)
    sent = list(descs)
    edge_a_c = slab_coefs(count_a, 1, pos_a, inv, block_len, modes)[4]
    edge_b_c = slab_coefs(count_b, count_a, pos_b, inv, block_len, modes)[4]
    levels_a = level_coefs(count_a, 1, inv, block_len, modes)
    levels_b = level_coefs(count_b, count_a, inv, block_len, modes)
    near_w = jnp.exp(-(pos_a * block_len).astype(jnp.float32) * inv)
    far_w = jnp.exp(-((count_a - 1 - pos_a) * block_len).astype(jnp.float32) * inv)
    join = jnp.where(slab == 0, near_w, jnp.where(slab == 2, far_w, 0.0))
    toep = jnp.where(lower, dot_nt(jnp.where(slab == 0, e_down * amp, 0.0), jnp.where(slab == 0, e_up, 0.0)), 0.0)
    into_f = jnp.where(slab == 0, e_next * amp, 0.0)
    into_b = jnp.where(slab == 2, jnp.exp(-(float(block_len) - offs) * inv) * amp, 0.0)
    items = finish_ring(descs, buf_a, count_a, pos_a)
    group, edge_a = fold_items(items, levels_a, edge_a_c, inv, modes)
    buf_b[0] = group
    descs = start_ring(buf_b, send_b, recv_b, count_b, pos_b, dev_b)
    sent += descs
    conv = dot_nt(values, toep)
    corr = dot_nn(grad_mixed, toep)
    items = finish_ring(descs, buf_b, count_b, pos_b)
    total, edge_b = fold_items(items, levels_b, edge_b_c, inv, modes)
    buf_c[0] = total
    descs = start_ring(buf_c, send_c, recv_c, count_c, ch_index, dev_c)
    sent += descs
    edge = join * edge_b + edge_a
    conv = conv + dot_nt(edge, into_f)
    corr = corr + dot_nt(edge, into_b)
    mixed_out = conv + gain * values
    grad_values = gain * grad_mixed + corr
    mix_ref[0] = mixed_out
    mix_ref[1] = grad_values
    items = finish_ring(descs, buf_c, count_c, ch_index)
    sums = items[0]
    for item in items[1:]:
        sums = sums + item
    small_ref[0] = total
    small_ref[1] = sums
    for desc in sent:
        desc.wait_send()


def output_kernel(scales, x_ref, q_ref, k_ref, d_ref, mix_ref, small_ref, mem_ref, res_ref,
                  out_ref, gx_ref, gq_ref, gk_ref, skip_ref, gres_ref, gmem_ref):
    mixed_out = mix_ref[0]
    grad_values = mix_ref[1]
    out_ref[...] = (q_ref[...].astype(jnp.float32) * mixed_out).astype(jnp.bfloat16)
    gx_ref[...] = (grad_values * k_ref[...].astype(jnp.float32)).astype(jnp.bfloat16)
    gq_ref[...] = (d_ref[...].astype(jnp.float32) * mixed_out).astype(jnp.bfloat16)
    gk_ref[...] = (grad_values * x_ref[...].astype(jnp.float32)).astype(jnp.bfloat16)
    modes = mem_ref.shape[0]
    channels = small_ref.shape[1]
    norm_scale, seq_scale = scales
    mode_of = lax.broadcasted_iota(jnp.int32, (1, LANES), 1) % modes
    mem_v = jnp.ones((1, LANES), jnp.float32)
    res_v = jnp.zeros((1, LANES), jnp.float32)
    for mode in range(modes):
        mem_v = jnp.where(mode_of == mode, mem_ref[mode], mem_v)
        res_v = jnp.where(mode_of == mode, res_ref[mode], res_v)
    gain = jnp.sqrt(2.0 / mem_v)
    sums = small_ref[1][0:1]
    grad_res = pltpu.roll(gain * sums * norm_scale, LANES - 5 * modes, 1)
    grad_mem = pltpu.roll(res_v * gain * sums * norm_scale, LANES - 6 * modes, 1)
    column = small_ref[0][:, 7 * modes:7 * modes + 1]
    lane = lax.broadcasted_iota(jnp.int32, (channels, LANES), 1)
    row = lax.broadcasted_iota(jnp.int32, (channels, LANES), 0)
    skip = jnp.sum(jnp.where(lane == row, column, 0.0), axis=0, keepdims=True) * seq_scale
    gres_ref[...] = grad_res[:, 0:modes]
    gmem_ref[...] = grad_mem[:, 0:modes]
    skip_ref[...] = skip[:, 0:channels]


def per_device(signal_x, gate_q, gate_k, skip_gain, residue, memory, cotangent):
    channels, block_len = signal_x.shape
    modes = memory.shape[0]
    seq_total = lax.axis_size("seq") * block_len
    all_channels = channels * lax.axis_size("ch")
    count_a = min(GROUP, lax.axis_size("seq"))
    count_b = lax.axis_size("seq") // count_a
    count_c = lax.axis_size("ch")
    msg = (channels, LANES)
    vmem = pl.BlockSpec(memory_space=pltpu.VMEM)
    half = jax.ShapeDtypeStruct(signal_x.shape, jnp.bfloat16)
    mix, small = pl.pallas_call(
        functools.partial(fused_kernel, (count_a, count_b, count_c), modes),
        out_shape=(jax.ShapeDtypeStruct((2,) + signal_x.shape, jnp.float32),
                   jax.ShapeDtypeStruct((2,) + msg, jnp.float32)),
        in_specs=[vmem] * 4 + [pl.BlockSpec(memory_space=pltpu.SMEM)] * 3,
        out_specs=(vmem,) * 2,
        scratch_shapes=[
            pltpu.VMEM((count_a,) + msg, jnp.float32),
            pltpu.VMEM((count_b,) + msg, jnp.float32),
            pltpu.VMEM((count_c,) + msg, jnp.float32),
            pltpu.SemaphoreType.DMA((count_a,)),
            pltpu.SemaphoreType.DMA((count_a,)),
            pltpu.SemaphoreType.DMA((count_b,)),
            pltpu.SemaphoreType.DMA((count_b,)),
            pltpu.SemaphoreType.DMA((count_c,)),
            pltpu.SemaphoreType.DMA((count_c,)),
        ],
        compiler_params=pltpu.CompilerParams(collective_id=0, has_side_effects=True),
    )(signal_x, gate_q, gate_k, cotangent, memory, residue, skip_gain)
    norm_scale = 1.0 / math.sqrt(all_channels * seq_total)
    smem = pl.BlockSpec(memory_space=pltpu.SMEM)
    output, grad_x, grad_q, grad_k, grad_skip, grad_residue, grad_memory = pl.pallas_call(
        functools.partial(output_kernel, (norm_scale, 1.0 / math.sqrt(seq_total))),
        out_shape=(half, half, half, half, jax.ShapeDtypeStruct((1, channels), jnp.float32),
                   jax.ShapeDtypeStruct((1, modes), jnp.float32), jax.ShapeDtypeStruct((1, modes), jnp.float32)),
        in_specs=[vmem] * 6 + [smem] * 2,
        out_specs=(vmem,) * 7,
    )(signal_x, gate_q, gate_k, cotangent, mix, small, memory, residue)
    grad_skip = grad_skip.reshape(channels)
    grad_residue = grad_residue.reshape(modes)
    grad_memory = grad_memory.reshape(modes)
    return (output, grad_x, grad_q, grad_k, grad_skip, grad_residue, grad_memory)


def solution(mesh):
    return jax.shard_map(
        per_device,
        mesh=mesh,
        in_specs=(
            P("ch", "seq"),
            P("ch", "seq"),
            P("ch", "seq"),
            P("ch"),
            P(),
            P(),
            P("ch", "seq"),
        ),
        out_specs=(
            P("ch", "seq"),
            P("ch", "seq"),
            P("ch", "seq"),
            P("ch", "seq"),
            P("ch"),
            P(),
            P(),
        ),
        check_vma=False,
    )
```

```python
import functools
import math

import jax
import jax.numpy as jnp
from jax import lax
from jax.experimental import pallas as pl
from jax.experimental.pallas import tpu as pltpu
from jax.sharding import PartitionSpec as P

HIGH_PREC = lax.Precision.HIGHEST


def mm(pattern, left_op, right_op):
    return jnp.einsum(pattern, left_op, right_op, precision=HIGH_PREC)


GROUP = 8
LANES = 128
SLABS = 8


def row_sum(value):
    return jnp.sum(value, axis=0, keepdims=True)


def slab_coefs(count, size, pos, inv, block_len, modes):
    lane = lax.broadcasted_iota(jnp.int32, (count, LANES), 1) // modes
    index = lax.broadcasted_iota(jnp.int32, (count, LANES), 0)
    span = float(size * block_len)
    step = jnp.exp(-span * inv)
    starts = index.astype(jnp.float32) * span
    lag = jnp.exp(-starts * inv)
    before = jnp.where(index < pos, jnp.exp(-((pos - 1 - index).astype(jnp.float32) * span) * inv), 0.0)
    after = jnp.where(index > pos, jnp.exp(-((index - pos - 1).astype(jnp.float32) * span) * inv), 0.0)
    keep = jnp.where(lane <= 1, step, 1.0)[0:1]
    carry = jnp.where(lane == 1, step * span, 0.0)[0:1]
    take = jnp.where((lane >= 2) & (lane <= 4), lag, 1.0)
    shift = jnp.where(lane == 4, lag * starts * inv, 0.0)
    edge = jnp.where(lane == 0, before, jnp.where(lane == 2, after, 0.0))
    return keep, carry, take, shift, edge


def level_coefs(count, size, inv, block_len, modes):
    slab = lax.broadcasted_iota(jnp.int32, (1, LANES), 1) // modes
    levels = []
    width = size
    while width < count * size:
        span = float(width * block_len)
        step = jnp.exp(-span * inv)
        levels.append((
            jnp.where(slab <= 1, step, 1.0),
            jnp.where(slab == 1, step * span, 0.0),
            jnp.where((slab >= 2) & (slab <= 4), step, 1.0),
            jnp.where(slab == 4, step * span * inv, 0.0),
        ))
        width *= 2
    return levels


def combine_pair(left, right, coefs, inv, modes):
    keep, carry, take, shift = coefs
    slab = lax.broadcasted_iota(jnp.int32, (1, LANES), 1) // modes
    s1 = row_sum(pltpu.roll(left, 3 * modes, 1) * right)
    s2 = row_sum(pltpu.roll(left, 4 * modes, 1) * right)
    s3 = row_sum(pltpu.roll(left, 2 * modes, 1) * right)
    cross = jnp.where(slab == 5, pltpu.roll(s1, 2 * modes, 1), 0.0) + jnp.where(
        slab == 6, pltpu.roll(s2, 2 * modes, 1) + pltpu.roll(s3 * inv, 3 * modes, 1), 0.0)
    return (keep * left + take * right + carry * pltpu.roll(left, modes, 1)
            + shift * pltpu.roll(right, modes, 1) + cross)


def fold_items(items, levels, edge_c, inv, modes):
    edge = edge_c[0:1] * items[0]
    for index in range(1, len(items)):
        edge = edge + edge_c[index:index + 1] * items[index]
    layer = list(items)
    for coefs in levels:
        layer = [combine_pair(layer[i], layer[i + 1], coefs, inv, modes) for i in range(0, len(layer), 2)]
    return layer[0], edge


def start_ring(buf, send_sems, recv_sems, count, pos, device_of):
    descs = []
    for dist in sorted(range(1, count), key=lambda d: -min(d, count - d)):
        desc = pltpu.make_async_remote_copy(
            src_ref=buf.at[0],
            dst_ref=buf.at[count - dist],
            send_sem=send_sems.at[dist],
            recv_sem=recv_sems.at[count - dist],
            device_id=device_of((pos + dist) % count),
            device_id_type=pl.DeviceIdType.MESH,
        )
        desc.start()
        descs.append(desc)
    return descs


def finish_ring(descs, buf, count, pos):
    for desc in descs:
        desc.wait_recv()
    return [buf[(slot - pos + count) % count] for slot in range(count)]


def dot_nn(left_op, right_op):
    return jnp.dot(left_op, right_op, precision=HIGH_PREC, preferred_element_type=jnp.float32)


def dot_nt(left_op, right_op):
    return lax.dot_general(left_op, right_op, (((1,), (1,)), ((), ())), precision=HIGH_PREC,
                           preferred_element_type=jnp.float32)


def dot_tn(left_op, right_op):
    return lax.dot_general(left_op, right_op, (((0,), (0,)), ((), ())), precision=HIGH_PREC,
                           preferred_element_type=jnp.float32)


def fused_kernel(counts, modes, x_ref, q_ref, k_ref, d_ref, mem_ref, res_ref, gain_ref,
                 mix_ref, small_ref,
                 buf_a, buf_b, buf_d, buf_c, send_a, recv_a, send_b, recv_b, send_d, recv_d, send_c, recv_c):
    count_a, count_b, count_c = counts
    channels, block_len = x_ref.shape
    seq_index = lax.axis_index("seq")
    ch_index = lax.axis_index("ch")
    pos_a = seq_index % count_a
    pos_b = seq_index // count_a

    def dev_a(other):
        return (pos_b * count_a + other, ch_index)

    count_d = count_b // 2
    pos_x = pos_b % 2
    pos_y = pos_b // 2

    def dev_b(other):
        return ((pos_y * 2 + other) * count_a + pos_a, ch_index)

    def dev_d(other):
        return ((other * 2 + pos_x) * count_a + pos_a, ch_index)

    def dev_c(other):
        return (seq_index, other)

    barrier = pltpu.get_barrier_semaphore()
    for count, pos, device_of in ((count_a, pos_a, dev_a), (2, pos_x, dev_b), (count_d, pos_y, dev_d),
                                  (count_c, ch_index, dev_c)):
        for dist in range(1, count):
            pl.semaphore_signal(barrier, inc=1, device_id=device_of((pos + dist) % count),
                                device_id_type=pl.DeviceIdType.MESH)

    slab = lax.broadcasted_iota(jnp.int32, (1, LANES), 1) // modes
    mode_of = lax.broadcasted_iota(jnp.int32, (1, LANES), 1) % modes
    mem_v = jnp.zeros((1, LANES), jnp.float32)
    res_v = jnp.zeros((1, LANES), jnp.float32)
    for mode in range(modes):
        mem_v = jnp.where(mode_of == mode, mem_ref[mode], mem_v)
        res_v = jnp.where(mode_of == mode, res_ref[mode], res_v)
    inv = 1.0 / mem_v
    amp = res_v * jnp.sqrt(2.0 * inv)
    chan_of = lax.broadcasted_iota(jnp.int32, (channels, 1), 0)
    gain = jnp.zeros((channels, 1), jnp.float32)
    for chan in range(channels):
        gain = jnp.where(chan_of == chan, gain_ref[chan], gain)
    offs = lax.broadcasted_iota(jnp.int32, (block_len, LANES), 0).astype(jnp.float32)
    back = float(block_len - 1) - offs
    e_down = jnp.exp(-offs * inv)
    e_tail = jnp.exp(-back * inv)
    e_next = jnp.exp(-(offs + 1.0) * inv)
    e_up = jnp.exp(offs * inv)
    right_v = jnp.where(slab == 0, e_tail, jnp.where(slab == 1, e_tail * back, 0.0))
    right_g = jnp.where(slab == 2, e_down, jnp.where(slab == 3, e_next, jnp.where(
        slab == 4, e_next * ((offs + 1.0) * inv - 0.5), 0.0)))
    right_r = jnp.where(slab == 5, e_up, jnp.where(slab == 6, e_up * offs * inv, 0.0))

    x_float = x_ref[...].astype(jnp.float32)
    q_float = q_ref[...].astype(jnp.float32)
    k_float = k_ref[...].astype(jnp.float32)
    d_float = d_ref[...].astype(jnp.float32)
    values = x_float * k_float
    grad_mixed = d_float * q_float
    row_t = lax.broadcasted_iota(jnp.int32, (block_len, block_len), 0)
    col_s = lax.broadcasted_iota(jnp.int32, (block_len, block_len), 1)
    lower = row_t >= col_s
    pair = jnp.where(lower, dot_tn(grad_mixed, values), 0.0)
    near = dot_nn(pair, right_r)
    terms = jnp.where(slab == 5, e_down * near, jnp.where(
        slab == 6, e_down * ((offs * inv - 0.5) * pltpu.roll(near, modes, 1) - near), 0.0))
    local = row_sum(terms)
    skip = jnp.sum(grad_mixed * values, axis=1, keepdims=True)
    state = dot_nn(values, right_v) + dot_nn(grad_mixed, right_g) + jnp.where(slab == 7, skip, local)
    buf_a[0] = state
    pl.semaphore_wait(barrier, count_a + 2 + count_d + count_c - 4)

    descs = start_ring(buf_a, send_a, recv_a, count_a, pos_a, dev_a)
    sent = list(descs)
    edge_a_c = slab_coefs(count_a, 1, pos_a, inv, block_len, modes)[4]
    edge_b_c = slab_coefs(2, count_a, pos_x, inv, block_len, modes)[4]
    edge_d_c = slab_coefs(count_d, 2 * count_a, pos_y, inv, block_len, modes)[4]
    levels_a = level_coefs(count_a, 1, inv, block_len, modes)
    levels_b = level_coefs(2, count_a, inv, block_len, modes)
    levels_d = level_coefs(count_d, 2 * count_a, inv, block_len, modes)
    near_x = jnp.exp(-(pos_x * count_a * block_len).astype(jnp.float32) * inv)
    far_x = jnp.exp(-((1 - pos_x) * count_a * block_len).astype(jnp.float32) * inv)
    join_x = jnp.where(slab == 0, near_x, jnp.where(slab == 2, far_x, 0.0))
    near_w = jnp.exp(-(pos_a * block_len).astype(jnp.float32) * inv)
    far_w = jnp.exp(-((count_a - 1 - pos_a) * block_len).astype(jnp.float32) * inv)
    join = jnp.where(slab == 0, near_w, jnp.where(slab == 2, far_w, 0.0))
    toep = jnp.where(lower, dot_nt(jnp.where(slab == 0, e_down * amp, 0.0), jnp.where(slab == 0, e_up, 0.0)), 0.0)
    into_f = jnp.where(slab == 0, e_next * amp, 0.0)
    into_b = jnp.where(slab == 2, jnp.exp(-(float(block_len) - offs) * inv) * amp, 0.0)
    items = finish_ring(descs, buf_a, count_a, pos_a)
    group, edge_a = fold_items(items, levels_a, edge_a_c, inv, modes)
    buf_b[0] = group
    descs = start_ring(buf_b, send_b, recv_b, 2, pos_x, dev_b)
    sent += descs
    conv = dot_nt(values, toep)
    items = finish_ring(descs, buf_b, 2, pos_x)
    pair_sum, edge_x = fold_items(items, levels_b, edge_b_c, inv, modes)
    buf_d[0] = pair_sum
    descs = start_ring(buf_d, send_d, recv_d, count_d, pos_y, dev_d)
    sent += descs
    corr = dot_nn(grad_mixed, toep)
    items = finish_ring(descs, buf_d, count_d, pos_y)
    total, edge_y = fold_items(items, levels_d, edge_d_c, inv, modes)
    edge_b = join_x * edge_y + edge_x
    buf_c[0] = total
    descs = start_ring(buf_c, send_c, recv_c, count_c, ch_index, dev_c)
    sent += descs
    edge = join * edge_b + edge_a
    conv = conv + dot_nt(edge, into_f)
    corr = corr + dot_nt(edge, into_b)
    mixed_out = conv + gain * values
    grad_values = gain * grad_mixed + corr
    mix_ref[0] = mixed_out
    mix_ref[1] = grad_values
    items = finish_ring(descs, buf_c, count_c, ch_index)
    sums = items[0]
    for item in items[1:]:
        sums = sums + item
    small_ref[0] = total
    small_ref[1] = sums
    for desc in sent:
        desc.wait_send()


def output_kernel(scales, x_ref, q_ref, k_ref, d_ref, mix_ref, small_ref, mem_ref, res_ref,
                  out_ref, gx_ref, gq_ref, gk_ref, skip_ref, gres_ref, gmem_ref):
    mixed_out = mix_ref[0]
    grad_values = mix_ref[1]
    out_ref[...] = (q_ref[...].astype(jnp.float32) * mixed_out).astype(jnp.bfloat16)
    gx_ref[...] = (grad_values * k_ref[...].astype(jnp.float32)).astype(jnp.bfloat16)
    gq_ref[...] = (d_ref[...].astype(jnp.float32) * mixed_out).astype(jnp.bfloat16)
    gk_ref[...] = (grad_values * x_ref[...].astype(jnp.float32)).astype(jnp.bfloat16)
    modes = mem_ref.shape[0]
    channels = small_ref.shape[1]
    norm_scale, seq_scale = scales
    mode_of = lax.broadcasted_iota(jnp.int32, (1, LANES), 1) % modes
    mem_v = jnp.ones((1, LANES), jnp.float32)
    res_v = jnp.zeros((1, LANES), jnp.float32)
    for mode in range(modes):
        mem_v = jnp.where(mode_of == mode, mem_ref[mode], mem_v)
        res_v = jnp.where(mode_of == mode, res_ref[mode], res_v)
    gain = jnp.sqrt(2.0 / mem_v)
    sums = small_ref[1][0:1]
    grad_res = pltpu.roll(gain * sums * norm_scale, LANES - 5 * modes, 1)
    grad_mem = pltpu.roll(res_v * gain * sums * norm_scale, LANES - 6 * modes, 1)
    column = small_ref[0][:, 7 * modes:7 * modes + 1]
    lane = lax.broadcasted_iota(jnp.int32, (channels, LANES), 1)
    row = lax.broadcasted_iota(jnp.int32, (channels, LANES), 0)
    skip = jnp.sum(jnp.where(lane == row, column, 0.0), axis=0, keepdims=True) * seq_scale
    gres_ref[...] = grad_res[:, 0:modes]
    gmem_ref[...] = grad_mem[:, 0:modes]
    skip_ref[...] = skip[:, 0:channels]


def per_device(signal_x, gate_q, gate_k, skip_gain, residue, memory, cotangent):
    channels, block_len = signal_x.shape
    modes = memory.shape[0]
    seq_total = lax.axis_size("seq") * block_len
    all_channels = channels * lax.axis_size("ch")
    count_a = min(GROUP, lax.axis_size("seq"))
    count_b = lax.axis_size("seq") // count_a
    count_c = lax.axis_size("ch")
    msg = (channels, LANES)
    vmem = pl.BlockSpec(memory_space=pltpu.VMEM)
    half = jax.ShapeDtypeStruct(signal_x.shape, jnp.bfloat16)
    mix, small = pl.pallas_call(
        functools.partial(fused_kernel, (count_a, count_b, count_c), modes),
        out_shape=(jax.ShapeDtypeStruct((2,) + signal_x.shape, jnp.float32),
                   jax.ShapeDtypeStruct((2,) + msg, jnp.float32)),
        in_specs=[vmem] * 4 + [pl.BlockSpec(memory_space=pltpu.SMEM)] * 3,
        out_specs=(vmem,) * 2,
        scratch_shapes=[
            pltpu.VMEM((count_a,) + msg, jnp.float32),
            pltpu.VMEM((2,) + msg, jnp.float32),
            pltpu.VMEM((count_b // 2,) + msg, jnp.float32),
            pltpu.VMEM((count_c,) + msg, jnp.float32),
            pltpu.SemaphoreType.DMA((count_a,)),
            pltpu.SemaphoreType.DMA((count_a,)),
            pltpu.SemaphoreType.DMA((2,)),
            pltpu.SemaphoreType.DMA((2,)),
            pltpu.SemaphoreType.DMA((count_b // 2,)),
            pltpu.SemaphoreType.DMA((count_b // 2,)),
            pltpu.SemaphoreType.DMA((count_c,)),
            pltpu.SemaphoreType.DMA((count_c,)),
        ],
        compiler_params=pltpu.CompilerParams(collective_id=0, has_side_effects=True),
    )(signal_x, gate_q, gate_k, cotangent, memory, residue, skip_gain)
    norm_scale = 1.0 / math.sqrt(all_channels * seq_total)
    smem = pl.BlockSpec(memory_space=pltpu.SMEM)
    output, grad_x, grad_q, grad_k, grad_skip, grad_residue, grad_memory = pl.pallas_call(
        functools.partial(output_kernel, (norm_scale, 1.0 / math.sqrt(seq_total))),
        out_shape=(half, half, half, half, jax.ShapeDtypeStruct((1, channels), jnp.float32),
                   jax.ShapeDtypeStruct((1, modes), jnp.float32), jax.ShapeDtypeStruct((1, modes), jnp.float32)),
        in_specs=[vmem] * 6 + [smem] * 2,
        out_specs=(vmem,) * 7,
    )(signal_x, gate_q, gate_k, cotangent, mix, small, memory, residue)
    grad_skip = grad_skip.reshape(channels)
    grad_residue = grad_residue.reshape(modes)
    grad_memory = grad_memory.reshape(modes)
    return (output, grad_x, grad_q, grad_k, grad_skip, grad_residue, grad_memory)


def solution(mesh):
    return jax.shard_map(
        per_device,
        mesh=mesh,
        in_specs=(
            P("ch", "seq"),
            P("ch", "seq"),
            P("ch", "seq"),
            P("ch"),
            P(),
            P(),
            P("ch", "seq"),
        ),
        out_specs=(
            P("ch", "seq"),
            P("ch", "seq"),
            P("ch", "seq"),
            P("ch", "seq"),
            P("ch"),
            P(),
            P(),
        ),
        check_vma=False,
    )
```

```python
import functools
import math

import jax
import jax.numpy as jnp
from jax import lax
from jax.experimental import pallas as pl
from jax.experimental.pallas import tpu as pltpu
from jax.sharding import PartitionSpec as P

HIGH_PREC = lax.Precision.HIGHEST


def mm(pattern, left_op, right_op):
    return jnp.einsum(pattern, left_op, right_op, precision=HIGH_PREC)


GROUP = 16
LANES = 128
SLABS = 8


def row_sum(value):
    return jnp.sum(value, axis=0, keepdims=True)


def slab_coefs(count, size, pos, inv, block_len, modes):
    lane = lax.broadcasted_iota(jnp.int32, (count, LANES), 1) // modes
    index = lax.broadcasted_iota(jnp.int32, (count, LANES), 0)
    span = float(size * block_len)
    step = jnp.exp(-span * inv)
    starts = index.astype(jnp.float32) * span
    lag = jnp.exp(-starts * inv)
    before = jnp.where(index < pos, jnp.exp(-((pos - 1 - index).astype(jnp.float32) * span) * inv), 0.0)
    after = jnp.where(index > pos, jnp.exp(-((index - pos - 1).astype(jnp.float32) * span) * inv), 0.0)
    keep = jnp.where(lane <= 1, step, 1.0)[0:1]
    carry = jnp.where(lane == 1, step * span, 0.0)[0:1]
    take = jnp.where((lane >= 2) & (lane <= 4), lag, 1.0)
    shift = jnp.where(lane == 4, lag * starts * inv, 0.0)
    edge = jnp.where(lane == 0, before, jnp.where(lane == 2, after, 0.0))
    return keep, carry, take, shift, edge


def level_coefs(count, size, inv, block_len, modes):
    slab = lax.broadcasted_iota(jnp.int32, (1, LANES), 1) // modes
    levels = []
    width = size
    while width < count * size:
        span = float(width * block_len)
        step = jnp.exp(-span * inv)
        levels.append((
            jnp.where(slab <= 1, step, 1.0),
            jnp.where(slab == 1, step * span, 0.0),
            jnp.where((slab >= 2) & (slab <= 4), step, 1.0),
            jnp.where(slab == 4, step * span * inv, 0.0),
        ))
        width *= 2
    return levels


def combine_pair(left, right, coefs, inv, modes):
    keep, carry, take, shift = coefs
    slab = lax.broadcasted_iota(jnp.int32, (1, LANES), 1) // modes
    s1 = row_sum(pltpu.roll(left, 3 * modes, 1) * right)
    s2 = row_sum(pltpu.roll(left, 4 * modes, 1) * right)
    s3 = row_sum(pltpu.roll(left, 2 * modes, 1) * right)
    cross = jnp.where(slab == 5, pltpu.roll(s1, 2 * modes, 1), 0.0) + jnp.where(
        slab == 6, pltpu.roll(s2, 2 * modes, 1) + pltpu.roll(s3 * inv, 3 * modes, 1), 0.0)
    return (keep * left + take * right + carry * pltpu.roll(left, modes, 1)
            + shift * pltpu.roll(right, modes, 1) + cross)


def fold_items(items, levels, edge_c, inv, modes):
    edge = edge_c[0:1] * items[0]
    for index in range(1, len(items)):
        edge = edge + edge_c[index:index + 1] * items[index]
    layer = list(items)
    for coefs in levels:
        layer = [combine_pair(layer[i], layer[i + 1], coefs, inv, modes) for i in range(0, len(layer), 2)]
    return layer[0], edge


def start_ring(buf, send_sems, recv_sems, count, pos, device_of):
    descs = []
    for dist in sorted(range(1, count), key=lambda d: -min(d, count - d)):
        desc = pltpu.make_async_remote_copy(
            src_ref=buf.at[0],
            dst_ref=buf.at[count - dist],
            send_sem=send_sems.at[dist],
            recv_sem=recv_sems.at[count - dist],
            device_id=device_of((pos + dist) % count),
            device_id_type=pl.DeviceIdType.MESH,
        )
        desc.start()
        descs.append(desc)
    return descs


def finish_ring(descs, buf, count, pos):
    for desc in descs:
        desc.wait_recv()
    return [buf[(slot - pos + count) % count] for slot in range(count)]


def dot_nn(left_op, right_op):
    return jnp.dot(left_op, right_op, precision=HIGH_PREC, preferred_element_type=jnp.float32)


def dot_nt(left_op, right_op):
    return lax.dot_general(left_op, right_op, (((1,), (1,)), ((), ())), precision=HIGH_PREC,
                           preferred_element_type=jnp.float32)


def dot_tn(left_op, right_op):
    return lax.dot_general(left_op, right_op, (((0,), (0,)), ((), ())), precision=HIGH_PREC,
                           preferred_element_type=jnp.float32)


def fused_kernel(counts, modes, x_ref, q_ref, k_ref, d_ref, mem_ref, res_ref, gain_ref,
                 mix_ref, small_ref,
                 buf_a, buf_b, buf_c, send_a, recv_a, send_b, recv_b, send_c, recv_c):
    count_a, count_b, count_c = counts
    channels, block_len = x_ref.shape
    seq_index = lax.axis_index("seq")
    ch_index = lax.axis_index("ch")
    pos_a = seq_index % count_a
    pos_b = seq_index // count_a

    def dev_a(other):
        return (pos_b * count_a + other, ch_index)

    def dev_b(other):
        return (other * count_a + pos_a, ch_index)

    def dev_c(other):
        return (seq_index, other)

    barrier = pltpu.get_barrier_semaphore()
    for count, pos, device_of in ((count_a, pos_a, dev_a), (count_b, pos_b, dev_b), (count_c, ch_index, dev_c)):
        for dist in range(1, count):
            pl.semaphore_signal(barrier, inc=1, device_id=device_of((pos + dist) % count),
                                device_id_type=pl.DeviceIdType.MESH)

    slab = lax.broadcasted_iota(jnp.int32, (1, LANES), 1) // modes
    mode_of = lax.broadcasted_iota(jnp.int32, (1, LANES), 1) % modes
    mem_v = jnp.zeros((1, LANES), jnp.float32)
    res_v = jnp.zeros((1, LANES), jnp.float32)
    for mode in range(modes):
        mem_v = jnp.where(mode_of == mode, mem_ref[mode], mem_v)
        res_v = jnp.where(mode_of == mode, res_ref[mode], res_v)
    inv = 1.0 / mem_v
    amp = res_v * jnp.sqrt(2.0 * inv)
    chan_of = lax.broadcasted_iota(jnp.int32, (channels, 1), 0)
    gain = jnp.zeros((channels, 1), jnp.float32)
    for chan in range(channels):
        gain = jnp.where(chan_of == chan, gain_ref[chan], gain)
    offs = lax.broadcasted_iota(jnp.int32, (block_len, LANES), 0).astype(jnp.float32)
    back = float(block_len - 1) - offs
    e_down = jnp.exp(-offs * inv)
    e_tail = jnp.exp(-back * inv)
    e_next = jnp.exp(-(offs + 1.0) * inv)
    e_up = jnp.exp(offs * inv)
    right_v = jnp.where(slab == 0, e_tail, jnp.where(slab == 1, e_tail * back, 0.0))
    right_g = jnp.where(slab == 2, e_down, jnp.where(slab == 3, e_next, jnp.where(
        slab == 4, e_next * ((offs + 1.0) * inv - 0.5), 0.0)))
    right_r = jnp.where(slab == 5, e_up, jnp.where(slab == 6, e_up * offs * inv, 0.0))

    x_float = x_ref[...].astype(jnp.float32)
    q_float = q_ref[...].astype(jnp.float32)
    k_float = k_ref[...].astype(jnp.float32)
    d_float = d_ref[...].astype(jnp.float32)
    values = x_float * k_float
    grad_mixed = d_float * q_float
    row_t = lax.broadcasted_iota(jnp.int32, (block_len, block_len), 0)
    col_s = lax.broadcasted_iota(jnp.int32, (block_len, block_len), 1)
    lower = row_t >= col_s
    pair = jnp.where(lower, dot_tn(grad_mixed, values), 0.0)
    near = dot_nn(pair, right_r)
    terms = jnp.where(slab == 5, e_down * near, jnp.where(
        slab == 6, e_down * ((offs * inv - 0.5) * pltpu.roll(near, modes, 1) - near), 0.0))
    local = row_sum(terms)
    skip = jnp.sum(grad_mixed * values, axis=1, keepdims=True)
    state = dot_nn(values, right_v) + dot_nn(grad_mixed, right_g) + jnp.where(slab == 7, skip, local)
    buf_a[0] = state
    pl.semaphore_wait(barrier, count_a + count_b + count_c - 3)

    descs = start_ring(buf_a, send_a, recv_a, count_a, pos_a, dev_a)
    sent = list(descs)
    edge_a_c = slab_coefs(count_a, 1, pos_a, inv, block_len, modes)[4]
    edge_b_c = slab_coefs(count_b, count_a, pos_b, inv, block_len, modes)[4]
    levels_a = level_coefs(count_a, 1, inv, block_len, modes)
    levels_b = level_coefs(count_b, count_a, inv, block_len, modes)
    near_w = jnp.exp(-(pos_a * block_len).astype(jnp.float32) * inv)
    far_w = jnp.exp(-((count_a - 1 - pos_a) * block_len).astype(jnp.float32) * inv)
    join = jnp.where(slab == 0, near_w, jnp.where(slab == 2, far_w, 0.0))
    toep = jnp.where(lower, dot_nt(jnp.where(slab == 0, e_down * amp, 0.0), jnp.where(slab == 0, e_up, 0.0)), 0.0)
    into_f = jnp.where(slab == 0, e_next * amp, 0.0)
    into_b = jnp.where(slab == 2, jnp.exp(-(float(block_len) - offs) * inv) * amp, 0.0)
    items = finish_ring(descs, buf_a, count_a, pos_a)
    group, edge_a = fold_items(items, levels_a, edge_a_c, inv, modes)
    buf_b[0] = group
    descs = start_ring(buf_b, send_b, recv_b, count_b, pos_b, dev_b)
    sent += descs
    conv = dot_nt(values, toep)
    corr = dot_nn(grad_mixed, toep)
    items = finish_ring(descs, buf_b, count_b, pos_b)
    total, edge_b = fold_items(items, levels_b, edge_b_c, inv, modes)
    buf_c[0] = total
    descs = start_ring(buf_c, send_c, recv_c, count_c, ch_index, dev_c)
    sent += descs
    edge = join * edge_b + edge_a
    conv = conv + dot_nt(edge, into_f)
    corr = corr + dot_nt(edge, into_b)
    mixed_out = conv + gain * values
    grad_values = gain * grad_mixed + corr
    mix_ref[0] = mixed_out
    mix_ref[1] = grad_values
    items = finish_ring(descs, buf_c, count_c, ch_index)
    sums = items[0]
    for item in items[1:]:
        sums = sums + item
    small_ref[0] = total
    small_ref[1] = sums
    for desc in sent:
        desc.wait_send()


def output_kernel(scales, x_ref, q_ref, k_ref, d_ref, mix_ref, small_ref, mem_ref, res_ref,
                  out_ref, gx_ref, gq_ref, gk_ref, skip_ref, gres_ref, gmem_ref):
    mixed_out = mix_ref[0]
    grad_values = mix_ref[1]
    out_ref[...] = (q_ref[...].astype(jnp.float32) * mixed_out).astype(jnp.bfloat16)
    gx_ref[...] = (grad_values * k_ref[...].astype(jnp.float32)).astype(jnp.bfloat16)
    gq_ref[...] = (d_ref[...].astype(jnp.float32) * mixed_out).astype(jnp.bfloat16)
    gk_ref[...] = (grad_values * x_ref[...].astype(jnp.float32)).astype(jnp.bfloat16)
    modes = mem_ref.shape[0]
    channels = small_ref.shape[1]
    norm_scale, seq_scale = scales
    mode_of = lax.broadcasted_iota(jnp.int32, (1, LANES), 1) % modes
    mem_v = jnp.ones((1, LANES), jnp.float32)
    res_v = jnp.zeros((1, LANES), jnp.float32)
    for mode in range(modes):
        mem_v = jnp.where(mode_of == mode, mem_ref[mode], mem_v)
        res_v = jnp.where(mode_of == mode, res_ref[mode], res_v)
    gain = jnp.sqrt(2.0 / mem_v)
    sums = small_ref[1][0:1]
    grad_res = pltpu.roll(gain * sums * norm_scale, LANES - 5 * modes, 1)
    grad_mem = pltpu.roll(res_v * gain * sums * norm_scale, LANES - 6 * modes, 1)
    column = small_ref[0][:, 7 * modes:7 * modes + 1]
    lane = lax.broadcasted_iota(jnp.int32, (channels, LANES), 1)
    row = lax.broadcasted_iota(jnp.int32, (channels, LANES), 0)
    skip = jnp.sum(jnp.where(lane == row, column, 0.0), axis=0, keepdims=True) * seq_scale
    gres_ref[...] = grad_res[:, 0:modes]
    gmem_ref[...] = grad_mem[:, 0:modes]
    skip_ref[...] = skip[:, 0:channels]


def per_device(signal_x, gate_q, gate_k, skip_gain, residue, memory, cotangent):
    channels, block_len = signal_x.shape
    modes = memory.shape[0]
    seq_total = lax.axis_size("seq") * block_len
    all_channels = channels * lax.axis_size("ch")
    count_a = min(GROUP, lax.axis_size("seq"))
    count_b = lax.axis_size("seq") // count_a
    count_c = lax.axis_size("ch")
    msg = (channels, LANES)
    vmem = pl.BlockSpec(memory_space=pltpu.VMEM)
    half = jax.ShapeDtypeStruct(signal_x.shape, jnp.bfloat16)
    mix, small = pl.pallas_call(
        functools.partial(fused_kernel, (count_a, count_b, count_c), modes),
        out_shape=(jax.ShapeDtypeStruct((2,) + signal_x.shape, jnp.float32),
                   jax.ShapeDtypeStruct((2,) + msg, jnp.float32)),
        in_specs=[vmem] * 4 + [pl.BlockSpec(memory_space=pltpu.SMEM)] * 3,
        out_specs=(vmem,) * 2,
        scratch_shapes=[
            pltpu.VMEM((count_a,) + msg, jnp.float32),
            pltpu.VMEM((count_b,) + msg, jnp.float32),
            pltpu.VMEM((count_c,) + msg, jnp.float32),
            pltpu.SemaphoreType.DMA((count_a,)),
            pltpu.SemaphoreType.DMA((count_a,)),
            pltpu.SemaphoreType.DMA((count_b,)),
            pltpu.SemaphoreType.DMA((count_b,)),
            pltpu.SemaphoreType.DMA((count_c,)),
            pltpu.SemaphoreType.DMA((count_c,)),
        ],
        compiler_params=pltpu.CompilerParams(collective_id=0, has_side_effects=True),
    )(signal_x, gate_q, gate_k, cotangent, memory, residue, skip_gain)
    norm_scale = 1.0 / math.sqrt(all_channels * seq_total)
    smem = pl.BlockSpec(memory_space=pltpu.SMEM)
    output, grad_x, grad_q, grad_k, grad_skip, grad_residue, grad_memory = pl.pallas_call(
        functools.partial(output_kernel, (norm_scale, 1.0 / math.sqrt(seq_total))),
        out_shape=(half, half, half, half, jax.ShapeDtypeStruct((1, channels), jnp.float32),
                   jax.ShapeDtypeStruct((1, modes), jnp.float32), jax.ShapeDtypeStruct((1, modes), jnp.float32)),
        in_specs=[vmem] * 6 + [smem] * 2,
        out_specs=(vmem,) * 7,
    )(signal_x, gate_q, gate_k, cotangent, mix, small, memory, residue)
    grad_skip = grad_skip.reshape(channels)
    grad_residue = grad_residue.reshape(modes)
    grad_memory = grad_memory.reshape(modes)
    return (output, grad_x, grad_q, grad_k, grad_skip, grad_residue, grad_memory)


def solution(mesh):
    return jax.shard_map(
        per_device,
        mesh=mesh,
        in_specs=(
            P("ch", "seq"),
            P("ch", "seq"),
            P("ch", "seq"),
            P("ch"),
            P(),
            P(),
            P("ch", "seq"),
        ),
        out_specs=(
            P("ch", "seq"),
            P("ch", "seq"),
            P("ch", "seq"),
            P("ch", "seq"),
            P("ch"),
            P(),
            P(),
        ),
        check_vma=False,
    )
```
